32 devices in a mesh: dp: 8 (over z, y), fsdp: 4 (over x, core).
Axes of the slice: x: 2, y: 2, z: 4, core: 2. Of those that a mesh axis runs over, the one named last changes fastest.
Arguments:
- tokens: bfloat16 [32, 1024, 1024], P(('dp', 'fsdp')), may hold values from -6 to 6
- key_len: int32 [32], P(('dp', 'fsdp')), may hold values from 256 to 1024, as said below
- section: int32 [32], P(('dp', 'fsdp')), may hold values from 1 to 7
- params: float32 [12611584], P(('dp', 'fsdp'))
- first_moment: float32 [12611584], P(('dp', 'fsdp')), may hold values from -6 to 6
- second_moment: float32 [12611584], P(('dp', 'fsdp')), may hold values from 327 to 32768
- cotangent: bfloat16 [32, 1024, 1024], P(('dp', 'fsdp')), may hold values from -6 to 6
Outputs:
- block_out: bfloat16 [32, 1024, 1024], P(('dp', 'fsdp'))
- input_grad: bfloat16 [32, 1024, 1024], P(('dp', 'fsdp'))
- param_grad: float32 [12611584], P(('dp', 'fsdp'))
- new_params: float32 [12611584], P(('dp', 'fsdp'))
- new_first: float32 [12611584], P(('dp', 'fsdp'))
- new_second: float32 [12611584], P(('dp', 'fsdp'))
- section_grad: float32 [7, 4096], replicated
The draws below stay inside these ranges and needn't reach their ends.
Inputs may be any that keep to these rules, and one draw needn't show every extreme that they name: Each item's keys are its first key_len frames; some item has exactly 1024.
All inputs are finite; a program needn't handle non-finite values.
Results may differ from the reference program's by a relative error of at most 0.014.
The reference program's roundings to bfloat16 on the way count: a program that leaves them out, or rounds other values in their place, can miss the bound.
Values may be sent and summed in bfloat16 or wider, within the bound.
No kernel may reach another device: no remote copies, remote signals or barrier semaphores. Data moves between devices by JAX's collectives and lax.ppermute only.
A program may use at most 384 MiB of HBM per device.

```python
import math
import jax
import jax.numpy as jnp
from jax import lax

D = 1024
HEADS = 16
FF = 4096
SECTIONS = 7
LEN = 1024
HEAD_DIM = 64
ITEMS = 32
PARAMS = 12611584


def draw_key_len(key, part):
    base = jax.random.fold_in(key, 17)
    key_one, key_two = jax.random.split(base)
    drawn = jax.random.randint(key_one, (ITEMS,), LEN // 4, LEN + 1)
    chosen = jax.random.randint(key_two, (), 0, ITEMS)
    return jnp.where(jnp.arange(ITEMS) == chosen, LEN, drawn).astype(jnp.int32)


def draw_params(key, part):
    subkeys = jax.random.split(jax.random.fold_in(key, 29), 5)
    column = jnp.where(jnp.arange(3 * D) < 2 * D, 1.5, 1.0)
    w_qkv = jax.random.normal(subkeys[0], (D, 3 * D), jnp.float32) * column[None, :] / math.sqrt(D)
    w_out = jax.random.normal(subkeys[1], (D, D), jnp.float32) * (math.sqrt(LEN) / 4.0) / math.sqrt(D)
    w_up = jax.random.normal(subkeys[2], (D, FF), jnp.float32) / math.sqrt(D)
    w_down = jax.random.normal(subkeys[3], (FF, D), jnp.float32) * 2.0 / math.sqrt(FF)
    is_gain = jnp.arange(4 * D) // D % 2 == 0
    table = jnp.where(is_gain[None, :], 1.0, 0.0) + 0.3 * jax.random.normal(subkeys[4], (SECTIONS, 4 * D), jnp.float32)
    return jnp.concatenate([w_qkv.ravel(), w_out.ravel(), w_up.ravel(), w_down.ravel(), table.ravel()]).astype(jnp.float32)


def place_ends(values, stream_key, smallest, largest):
    longest = values.shape.index(max(values.shape))
    spots = []
    for shift in (0, 1):
        where = [jax.random.randint(jax.random.fold_in(stream_key, axis), (), 0, length) for axis, length in enumerate(values.shape)]
        where[longest] = (where[longest] + shift) % values.shape[longest]
        spots.append(tuple(where))
    return values.at[spots[0]].set(smallest).at[spots[1]].set(largest)


def block_scale(stream_key, extent, cuts, least, high):
    loudness, own = 1.0, jax.random.fold_in(stream_key, 6)
    for position, blocks in cuts:
        steps = jnp.exp(jax.random.uniform(jax.random.fold_in(own, position), (blocks,), jnp.float32, least / len(cuts), high / len(cuts)))
        loudness = loudness * jnp.repeat(steps, extent[position] // blocks).reshape([-1 if axis == position else 1 for axis in range(len(extent))])
    return loudness


def normal_values(own_key, extent, scale, limit, pieces=(), held_as=jnp.bfloat16):
    values = scale * jax.random.normal(own_key, extent, jnp.float32)
    if pieces:
        values = values * block_scale(own_key, extent, pieces, -0.22, 0.18)
    return jnp.clip(values, -limit, limit).astype(held_as)


def setup_inputs(seed: int = 0) -> dict:
    keys = jax.random.split(jax.random.key(seed), 8)
    return {
        "tokens": normal_values(keys[0], (ITEMS, LEN, D), 1.0, 6.0, ((0, 32),)),
        "key_len": draw_key_len(jax.random.fold_in(keys[7], 71), 0),
        "section": place_ends(jax.random.randint(keys[2], (ITEMS,), 1, SECTIONS + 1), jax.random.fold_in(keys[2], 1), 1, SECTIONS).astype(jnp.int32),
        "params": draw_params(jax.random.fold_in(keys[7], 71), 0),
        "first_moment": normal_values(keys[4], (PARAMS,), 1.0, 6.0, ((0, 32),), jnp.float32),
        "second_moment": jnp.clip(jnp.exp(math.log(32768.0) - 4.6072475 * jax.random.uniform(keys[5], (PARAMS,), jnp.float32) ** block_scale(keys[5], (PARAMS,), ((0, 32),), -0.2, 0.2)), 327.0, 32768.0),
        "cotangent": normal_values(keys[6], (ITEMS, LEN, D), 1.0, 6.0, ((0, 32),)),
    }


@jax.custom_vjp
def low(v):
    return lax.optimization_barrier(v.astype(jnp.bfloat16)).astype(jnp.float32)

@jax.custom_vjp
def low_back(v):
    return v

def low_keep(v):
    return (low(v), None)

def low_pass(kept, grad):
    return (grad,)

def back_keep(v):
    return (v, None)

def back_low(kept, grad):
    return (low(grad),)
low.defvjp(low_keep, low_pass)
low_back.defvjp(back_keep, back_low)
beta_one = 0.9
beta_two = 0.95
adam_eps = 1e-08
learn_rate = 0.05
bias_one = 1.0 - 0.9 ** 10
bias_two = 1.0 - 0.95 ** 10

def adanorm(field, gain_rows, shift_rows):
    average = lax.optimization_barrier(jnp.mean(field, -1, keepdims=True))
    centred = field - average
    spread = lax.optimization_barrier(jnp.mean(centred * centred, -1, keepdims=True))
    return centred * lax.rsqrt(spread + 1e-05) * gain_rows + shift_rows

def split_params(flat):
    first = 3 * D * D
    second = first + D * D
    third = second + D * FF
    fourth = third + FF * D
    return (flat[:first].reshape(D, 3 * D), flat[first:second].reshape(D, D), flat[second:third].reshape(D, FF), flat[third:fourth].reshape(FF, D), flat[fourth:].reshape(SECTIONS, 4 * D))

def project(field, matrix):
    return jnp.einsum('ild,de->ile', field, matrix, precision=lax.Precision.HIGHEST)

def reference(tokens, key_len, section, params, first_moment, second_moment, cotangent):
    score_scale = HEAD_DIM ** (-0.5)

    def attend_item(queries, keys_all, values, valid_count):
        scores = jnp.einsum('qhd,khd->hqk', queries, keys_all, precision=lax.Precision.HIGHEST) * score_scale
        key_valid = jnp.arange(LEN) < valid_count
        scores = jnp.where(key_valid[None, None, :], scores, -1e+30)
        scores = low_back(scores)
        softmax_w = jax.nn.softmax(scores, axis=-1)
        return jnp.einsum('hqk,khd->qhd', low(softmax_w), values, precision=lax.Precision.HIGHEST)
    checked = jax.checkpoint(attend_item)

    def forward(param_values, inputs):
        w_qkv, w_out, w_up, w_down, table = split_params(low(param_values))
        modulation = table[section - 1]
        gain_one = modulation[:, None, 0:D]
        shift_one = modulation[:, None, D:2 * D]
        gain_two = modulation[:, None, 2 * D:3 * D]
        shift_two = modulation[:, None, 3 * D:4 * D]
        low_one = low(adanorm(inputs, gain_one, shift_one))
        qkv = low_back(low(project(low_one, w_qkv)))
        qkv = qkv.reshape(ITEMS, LEN, 3, HEADS, HEAD_DIM)
        mixture = lax.map(lambda operands: checked(*operands), (qkv[:, :, 0], qkv[:, :, 1], qkv[:, :, 2], key_len))
        mixture = low_back(low(mixture.reshape(ITEMS, LEN, D)))
        attended = low_back(project(mixture, w_out))
        middle = inputs + attended
        low_two = low(adanorm(middle, gain_two, shift_two))
        projected = low_back(project(low_two, w_up))
        activated = low(jax.nn.gelu(projected))
        branch = low_back(project(activated, w_down))
        return middle + branch
    result, pullback = jax.vjp(forward, params, tokens.astype(jnp.float32))
    param_grad, token_grad = pullback(cotangent.astype(jnp.float32))
    new_first = beta_one * first_moment + (1.0 - beta_one) * param_grad
    new_second = beta_two * second_moment + (1.0 - beta_two) * param_grad * param_grad
    new_params = params - learn_rate * (new_first / bias_one) / (jnp.sqrt(new_second / bias_two) + adam_eps)
    table_start = 4 * D * D + 2 * D * FF
    section_grad = param_grad[table_start:].reshape(SECTIONS, 4 * D)
    return (result.astype(jnp.bfloat16), token_grad.astype(jnp.bfloat16), param_grad, new_params, new_first, new_second, section_grad)
```

```python
import jax
import jax.numpy as jnp
from jax import lax
from jax.experimental import pallas as pl
from jax.experimental.pallas import tpu as pltpu
from jax.sharding import PartitionSpec as P

D = 1024
HEADS = 16
FF = 4096
SECTIONS = 7


beta_one = 0.9
beta_two = 0.95
adam_eps = 1e-08
learn_rate = 0.05
bias_one = 1.0 - 0.9**10
bias_two = 1.0 - 0.95**10


def adanorm(field, gain_rows, shift_rows):
    average = jnp.mean(field, -1, keepdims=True)
    centred = field - average
    spread = jnp.mean(centred * centred, -1, keepdims=True)
    return centred * lax.rsqrt(spread + 1e-05) * gain_rows + shift_rows


def unpack(flat):
    first = 3 * D * D
    second = first + D * D
    third = second + D * FF
    fourth = third + FF * D
    return (
        flat[:first].reshape(D, 3 * D),
        flat[first:second].reshape(D, D),
        flat[second:third].reshape(D, FF),
        flat[third:fourth].reshape(FF, D),
        flat[fourth:].reshape(SECTIONS, 4 * D),
    )


def dot_trans(left, right):
    return lax.dot_general(
        left, right, (((1,), (1,)), ((), ())), preferred_element_type=jnp.float32
    )


def dot_inner(left, right):
    return lax.dot_general(
        left, right, (((0,), (0,)), ((), ())), preferred_element_type=jnp.float32
    )


def masked_scores(query_block, keys_all, key_valid, score_scale):
    scores = (
        jnp.einsum("qhd,khd->hqk", query_block, keys_all, preferred_element_type=jnp.float32)
        * score_scale
    )
    return jnp.where(key_valid, scores, -1e30)


def attend_forward(operands):
    queries, keys_all, values, valid_count = operands
    frames = queries.shape[0]
    block_rows = min(512, frames)
    score_scale = queries.shape[2] ** (-0.5)
    key_valid = (jnp.arange(frames) < valid_count)[None, None, :]
    outputs = []
    totals = []
    for offset in range(0, frames, block_rows):
        scores = masked_scores(
            queries[offset : offset + block_rows], keys_all, key_valid, score_scale
        )
        row_max = jnp.max(scores, -1, keepdims=True)
        log_total = row_max + jnp.log(jnp.sum(jnp.exp(scores - row_max), -1, keepdims=True))
        softmax_w = jnp.exp(scores - log_total).astype(jnp.bfloat16)
        outputs.append(
            jnp.einsum(
                "hqk,khd->qhd", softmax_w, values, preferred_element_type=jnp.float32
            ).astype(jnp.bfloat16)
        )
        totals.append(log_total[..., 0])
    return (jnp.concatenate(outputs, 0), jnp.concatenate(totals, 1))


def attend_backward(operands):
    queries, keys_all, values, valid_count, log_totals, grad_mix = operands
    frames = queries.shape[0]
    block_rows = min(512, frames)
    score_scale = queries.shape[2] ** (-0.5)
    key_valid = (jnp.arange(frames) < valid_count)[None, None, :]
    grad_keys = jnp.zeros(keys_all.shape, jnp.float32)
    grad_values = jnp.zeros(values.shape, jnp.float32)
    grad_queries = []
    for offset in range(0, frames, block_rows):
        query_block = queries[offset : offset + block_rows]
        grad_block = grad_mix[offset : offset + block_rows]
        scores = masked_scores(query_block, keys_all, key_valid, score_scale)
        softmax_w = jnp.exp(scores - log_totals[:, offset : offset + block_rows, None])
        grad_probs = jnp.einsum(
            "qhd,khd->hqk", grad_block, values, preferred_element_type=jnp.float32
        )
        grad_values = grad_values + jnp.einsum(
            "hqk,qhd->khd",
            softmax_w.astype(jnp.bfloat16),
            grad_block,
            preferred_element_type=jnp.float32,
        )
        grad_scores = (
            softmax_w * (grad_probs - jnp.sum(softmax_w * grad_probs, -1, keepdims=True))
        ).astype(jnp.bfloat16)
        grad_queries.append(
            jnp.einsum("hqk,khd->qhd", grad_scores, keys_all, preferred_element_type=jnp.float32)
            * score_scale
        )
        grad_keys = (
            grad_keys
            + jnp.einsum(
                "hqk,qhd->khd", grad_scores, query_block, preferred_element_type=jnp.float32
            )
            * score_scale
        )
    return jnp.stack([jnp.concatenate(grad_queries, 0), grad_keys, grad_values], 1).astype(
        jnp.bfloat16
    )


def per_device(tokens, key_len, section, params, first_moment, second_moment, cotangent):
    item_count, frames, features = tokens.shape
    row_count = item_count * frames
    head_size = features // HEADS
    low_params = params.astype(jnp.bfloat16)
    gathered = lax.all_gather(low_params, ("dp", "fsdp"), axis=0, tiled=True)
    w_qkv, w_out, w_up, w_down, table = unpack(gathered)
    picker = (section[:, None] - 1 == jnp.arange(SECTIONS)[None, :]).astype(jnp.float32)
    modulation = jnp.dot(picker, table.astype(jnp.float32), precision=lax.Precision.HIGHEST)
    gain_one = modulation[:, None, 0:features]
    shift_one = modulation[:, None, features : 2 * features]
    gain_two = modulation[:, None, 2 * features : 3 * features]
    shift_two = modulation[:, None, 3 * features : 4 * features]
    inputs = tokens.astype(jnp.float32)
    normed_one, norm_one_back = jax.vjp(adanorm, inputs, gain_one, shift_one)
    low_one = normed_one.astype(jnp.bfloat16).reshape(row_count, features)
    qkv = jnp.dot(low_one, w_qkv, preferred_element_type=jnp.float32).astype(jnp.bfloat16)
    qkv = qkv.reshape(item_count, frames, 3, HEADS, head_size)
    queries = qkv[:, :, 0]
    keys_all = qkv[:, :, 1]
    values = qkv[:, :, 2]
    mixture, log_totals = lax.map(attend_forward, (queries, keys_all, values, key_len))
    mixture = mixture.reshape(row_count, features)
    attended = jnp.dot(mixture, w_out, preferred_element_type=jnp.float32)
    middle = inputs + attended.reshape(item_count, frames, features)
    normed_two, norm_two_back = jax.vjp(adanorm, middle, gain_two, shift_two)
    low_two = normed_two.astype(jnp.bfloat16).reshape(row_count, features)
    projected = jnp.dot(low_two, w_up, preferred_element_type=jnp.float32)
    activated, gelu_back = jax.vjp(jax.nn.gelu, projected)
    low_act = activated.astype(jnp.bfloat16)
    branch = jnp.dot(low_act, w_down, preferred_element_type=jnp.float32)
    block_out = (middle + branch.reshape(item_count, frames, features)).astype(jnp.bfloat16)
    regathered = lax.all_gather(low_params, ("dp", "fsdp"), axis=0, tiled=True)
    w_qkv, w_out, w_up, w_down, table = unpack(regathered)
    grad_y = cotangent.astype(jnp.float32)
    low_gy = cotangent.reshape(row_count, features)
    grad_down = dot_inner(low_act, low_gy)
    grad_act = dot_trans(low_gy, w_down)
    (grad_proj,) = gelu_back(grad_act)
    low_gp = grad_proj.astype(jnp.bfloat16)
    grad_up = dot_inner(low_two, low_gp)
    grad_norm_two = dot_trans(low_gp, w_up).reshape(item_count, frames, features)
    grad_mid_part, grad_gain_two, grad_shift_two = norm_two_back(grad_norm_two)
    grad_mid = grad_y + grad_mid_part
    low_gm = grad_mid.astype(jnp.bfloat16).reshape(row_count, features)
    grad_out_w = dot_inner(mixture, low_gm)
    grad_mix = (
        dot_trans(low_gm, w_out).astype(jnp.bfloat16).reshape(item_count, frames, HEADS, head_size)
    )
    grad_qkv = lax.map(attend_backward, (queries, keys_all, values, key_len, log_totals, grad_mix))
    grad_qkv = grad_qkv.reshape(row_count, 3 * features)
    grad_qkv_w = dot_inner(low_one, grad_qkv)
    grad_norm_one = dot_trans(grad_qkv, w_qkv).reshape(item_count, frames, features)
    grad_in_part, grad_gain_one, grad_shift_one = norm_one_back(grad_norm_one)
    input_grad = (grad_mid + grad_in_part).astype(jnp.bfloat16)
    per_item = jnp.concatenate(
        [grad_gain_one[:, 0], grad_shift_one[:, 0], grad_gain_two[:, 0], grad_shift_two[:, 0]], 1
    )
    grad_table = jnp.einsum("is,ic->sc", picker, per_item, precision=lax.Precision.HIGHEST)
    table_flat = grad_table.ravel()
    table_size = table_flat.shape[0]
    flat_grads = jnp.concatenate(
        [
            grad_qkv_w.ravel(),
            grad_out_w.ravel(),
            grad_up.ravel(),
            grad_down.ravel(),
            jnp.zeros((table_size,), jnp.float32),
        ]
    )
    table_start = flat_grads.shape[0] - table_size
    shard_size = params.shape[0]
    weight_part = lax.psum_scatter(
        lax.slice_in_dim(flat_grads, 0, lax.axis_size(("dp", "fsdp")) * shard_size, axis=0),
        ("dp", "fsdp"),
        scatter_dimension=0,
        tiled=True,
    )
    section_total = lax.psum(table_flat, ("dp", "fsdp"))
    padded = jnp.concatenate(
        [
            jnp.zeros((shard_size,), jnp.float32),
            section_total,
            jnp.zeros((shard_size,), jnp.float32),
        ]
    )
    slice_start = jnp.clip(
        lax.axis_index(("dp", "fsdp")) * shard_size - table_start + shard_size,
        0,
        table_size + shard_size,
    ).astype(jnp.int32)
    param_grad = weight_part + lax.dynamic_slice_in_dim(padded, slice_start, shard_size)
    section_grad = section_total.reshape(SECTIONS, 4 * features)
    new_first = beta_one * first_moment + (1.0 - beta_one) * param_grad
    new_second = beta_two * second_moment + (1.0 - beta_two) * param_grad * param_grad
    new_params = params - learn_rate * (new_first / bias_one) / (
        jnp.sqrt(new_second / bias_two) + adam_eps
    )
    return (block_out, input_grad, param_grad, new_params, new_first, new_second, section_grad)


LANES = 128
TILE = 16
EPS = 1e-05
VMEM_LIMIT = 62 * 1024 * 1024
GELU_C = 0.7978845608028654
GELU_A = 0.044715
BF = jnp.bfloat16
F32 = jnp.float32


def params_of(*semantics):
    return pltpu.CompilerParams(
        dimension_semantics=semantics or None, vmem_limit_bytes=VMEM_LIMIT
    )


def cost(flops, moved, transcendentals=0):
    return pl.CostEstimate(
        flops=int(flops), bytes_accessed=int(moved), transcendentals=int(transcendentals)
    )


def dot_nn(left, right):
    return lax.dot_general(left, right, (((1,), (0,)), ((), ())), preferred_element_type=F32)


def dot_nt(left, right):
    return lax.dot_general(left, right, (((1,), (1,)), ((), ())), preferred_element_type=F32)


def dot_tn(left, right):
    return lax.dot_general(left, right, (((0,), (0,)), ((), ())), preferred_element_type=F32)


def from_tiles(ref, first, count):
    rows = ref.shape[0] * TILE
    parts = [ref[:, first + c].reshape(rows, LANES) for c in range(count)]
    return parts[0] if count == 1 else jnp.concatenate(parts, 1)


def to_tiles(ref, first, value):
    rows, columns = value.shape
    for c in range(columns // LANES):
        part = value[:, c * LANES : (c + 1) * LANES].astype(BF)
        ref[:, first + c] = part.reshape(rows // TILE, TILE, LANES)


def row_chunks(kind):
    return {0: 3 * D // LANES, 1: D // LANES, 2: FF // LANES}[kind]


def each_tile(kinds, body):
    def span(kind, start, rows):
        step = row_chunks(kind)
        block = TILE * step

        def one(index, carry):
            base = start + index * block
            for c in range(step):
                body(base // TILE + c, base + c, step)
            return carry

        lax.fori_loop(0, rows // block, one, 0)

    @pl.when(kinds[0] == 0)
    def _():
        span(0, 0, 3072)

    for part in range(3):
        for kind in (1, 2):

            @pl.when(kinds[part] == kind)
            def _():
                span(kind, part * 1024, 1024)


def pack_kernel(kinds, flat_ref, tiles_ref):
    def body(tile, row, step):
        tiles_ref[tile] = flat_ref[pl.ds(row, TILE, stride=step), :].astype(BF)

    each_tile(kinds, body)


def unpack_kernel(kinds, tiles_ref, flat_ref):
    def body(tile, row, step):
        flat_ref[pl.ds(row, TILE, stride=step), :] = tiles_ref[tile].astype(F32)

    each_tile(kinds, body)


def shard_kinds(index):
    start = index * 3072 + jnp.arange(3, dtype=jnp.int32) * 1024
    qkv_end = 3 * D * D // LANES
    out_end = qkv_end + D * D // LANES
    up_end = out_end + D * FF // LANES
    return jnp.where(
        start < qkv_end, 0, jnp.where((start < out_end) | (start >= up_end), 1, 2)
    ).astype(jnp.int32)


def pack_shard(kinds, flat):
    return pl.pallas_call(
        pack_kernel,
        out_shape=jax.ShapeDtypeStruct((192, TILE, LANES), BF),
        in_specs=[pl.BlockSpec(memory_space=pltpu.SMEM), pl.BlockSpec(memory_space=pltpu.VMEM)],
        out_specs=pl.BlockSpec(memory_space=pltpu.VMEM),
        compiler_params=params_of(),
        cost_estimate=cost(0, 3 << 20),
        name="pack_shard",
    )(kinds, flat)


def unpack_shard(kinds, tiles):
    return pl.pallas_call(
        unpack_kernel,
        out_shape=jax.ShapeDtypeStruct((3072, LANES), F32),
        in_specs=[pl.BlockSpec(memory_space=pltpu.SMEM), pl.BlockSpec(memory_space=pltpu.VMEM)],
        out_specs=pl.BlockSpec(memory_space=pltpu.VMEM),
        compiler_params=params_of(),
        cost_estimate=cost(0, 3 << 20),
        name="unpack_shard",
    )(kinds, tiles)


def centre(field):
    average = jnp.mean(field, -1, keepdims=True)
    centred = field - average
    spread = jnp.mean(centred * centred, -1, keepdims=True)
    inverse = lax.rsqrt(spread + EPS)
    return centred * inverse, inverse


def norm_back(zhat, inverse, grad, gain):
    scaled = grad * gain
    mean_one = jnp.mean(scaled, -1, keepdims=True)
    mean_two = jnp.mean(scaled * zhat, -1, keepdims=True)
    return inverse * (scaled - mean_one - zhat * mean_two)


def qkv_kernel(x_ref, mod_ref, w_ref, low_ref, qkv_ref):
    @pl.when(pl.program_id(0) == 0)
    def _():
        zhat, _ = centre(x_ref[...].astype(F32))
        low_ref[...] = (zhat * mod_ref[0:1, :] + mod_ref[1:2, :]).astype(BF)

    weights = from_tiles(w_ref, 0, w_ref.shape[1])
    qkv_ref[...] = dot_nn(low_ref[...], weights).astype(BF)


def project_qkv(x, mod, tiles):
    chunks = 4
    width = chunks * LANES
    return pl.pallas_call(
        qkv_kernel,
        grid=(3 * D // width,),
        out_shape=(
            jax.ShapeDtypeStruct((1024, D), BF),
            jax.ShapeDtypeStruct((1024, 3 * D), BF),
        ),
        in_specs=[
            pl.BlockSpec((1024, D), lambda j: (0, 0)),
            pl.BlockSpec((4, D), lambda j: (0, 0)),
            pl.BlockSpec((64, chunks, TILE, LANES), lambda j: (0, j, 0, 0)),
        ],
        out_specs=(
            pl.BlockSpec((1024, D), lambda j: (0, 0)),
            pl.BlockSpec((1024, width), lambda j: (0, j)),
        ),
        compiler_params=params_of("arbitrary"),
        cost_estimate=cost(6.4e9, 18e6),
        name="project_qkv",
    )(x, mod, tiles.reshape(-1, 24, TILE, LANES))


def head_lanes(head):
    lane = lax.broadcasted_iota(jnp.int32, (1, LANES), 1)
    return (lane >= 64) if head else (lane < 64)


def attend_kernel(len_ref, q_ref, k_ref, v_ref, out_ref):
    rows = 256
    frames = k_ref.shape[0]
    valid = lax.broadcasted_iota(jnp.int32, (1, frames), 1) < len_ref[0]
    keys = k_ref[...]
    zero = jnp.zeros((), BF)
    values = [jnp.where(head_lanes(h), v_ref[...], zero) for h in range(2)]
    for offset in range(0, frames, rows):
        queries = q_ref[offset : offset + rows, :] * jnp.asarray(0.125, BF)
        total = None
        for h in range(2):
            scores = dot_nt(jnp.where(head_lanes(h), queries, zero), keys)
            scores = jnp.where(valid, scores, -1e30)
            weights = jnp.exp(scores - jnp.max(scores, -1, keepdims=True))
            weights = weights * (1.0 / jnp.sum(weights, -1, keepdims=True))
            mixed = dot_nn(weights.astype(BF), values[h])
            total = mixed if total is None else total + mixed
        out_ref[offset : offset + rows, :] = total.astype(BF)


def attend(key_len, qkv):
    pairs = HEADS // 2
    return pl.pallas_call(
        attend_kernel,
        grid=(pairs,),
        out_shape=jax.ShapeDtypeStruct((1024, D), BF),
        in_specs=[
            pl.BlockSpec(memory_space=pltpu.SMEM),
            pl.BlockSpec((1024, LANES), lambda j: (0, j)),
            pl.BlockSpec((1024, LANES), lambda j: (0, pairs + j)),
            pl.BlockSpec((1024, LANES), lambda j: (0, 2 * pairs + j)),
        ],
        out_specs=pl.BlockSpec((1024, LANES), lambda j: (0, j)),
        compiler_params=params_of("arbitrary"),
        cost_estimate=cost(17e9, 8e6, 16e6),
        name="attend",
    )(key_len, qkv, qkv, qkv)


def attend_back_kernel(len_ref, q_ref, k_ref, v_ref, do_ref, dq_ref, dk_ref, dv_ref, dk_acc, dv_acc):
    rows = 256
    frames = k_ref.shape[0]
    valid = lax.broadcasted_iota(jnp.int32, (frames, 1), 0) < len_ref[0]
    keys = k_ref[...]
    values = v_ref[...]
    zero = jnp.zeros((), BF)
    masked_keys = [jnp.where(head_lanes(h), keys, zero) for h in range(2)]
    for offset in range(0, frames, rows):
        queries = q_ref[offset : offset + rows, :] * jnp.asarray(0.125, BF)
        grads = do_ref[offset : offset + rows, :]
        total = None
        for h in range(2):
            masked_q = jnp.where(head_lanes(h), queries, zero)
            masked_g = jnp.where(head_lanes(h), grads, zero)
            scores = dot_nt(keys, masked_q)
            scores = jnp.where(valid, scores, -1e30)
            weights = jnp.exp(scores - jnp.max(scores, 0, keepdims=True))
            weights = weights * (1.0 / jnp.sum(weights, 0, keepdims=True))
            grad_w = dot_nt(values, masked_g)
            product = weights * grad_w
            back = product - weights * jnp.sum(product, 0, keepdims=True)
            back = back.astype(BF)
            part_v = dot_nn(weights.astype(BF), masked_g)
            part_k = dot_nn(back, masked_q)
            if offset == 0 and h == 0:
                dv_acc[...] = part_v
                dk_acc[...] = part_k
            else:
                dv_acc[...] += part_v
                dk_acc[...] += part_k
            part_q = dot_tn(back, masked_keys[h])
            total = part_q if total is None else total + part_q
        dq_ref[offset : offset + rows, :] = (total * 0.125).astype(BF)
    dk_ref[...] = dk_acc[...].astype(BF)
    dv_ref[...] = dv_acc[...].astype(BF)


def attend_back(key_len, qkv, grad_mix):
    pairs = HEADS // 2
    block = lambda shift: pl.BlockSpec((1024, LANES), lambda j: (0, shift + j))
    return pl.pallas_call(
        attend_back_kernel,
        grid=(pairs,),
        out_shape=(jax.ShapeDtypeStruct((1024, D), BF),) * 3,
        in_specs=[
            pl.BlockSpec(memory_space=pltpu.SMEM),
            block(0),
            block(pairs),
            block(2 * pairs),
            block(0),
        ],
        out_specs=(block(0),) * 3,
        scratch_shapes=[pltpu.VMEM((1024, LANES), F32)] * 2,
        compiler_params=params_of("arbitrary"),
        cost_estimate=cost(43e9, 14e6, 16e6),
        name="attend_back",
    )(key_len, qkv, qkv, qkv, grad_mix)


def middle_kernel(x_ref, mod_ref, mix_ref, w_ref, mid_ref, low_ref):
    weights = from_tiles(w_ref, 0, w_ref.shape[1])
    middle = x_ref[...].astype(F32) + dot_nn(mix_ref[...], weights)
    mid_ref[...] = middle
    zhat, _ = centre(middle)
    low_ref[...] = (zhat * mod_ref[2:3, :] + mod_ref[3:4, :]).astype(BF)


def middle_rows(x, mod, mixture, tiles):
    rows = 256
    return pl.pallas_call(
        middle_kernel,
        grid=(1024 // rows,),
        out_shape=(jax.ShapeDtypeStruct((1024, D), F32), jax.ShapeDtypeStruct((1024, D), BF)),
        in_specs=[
            pl.BlockSpec((rows, D), lambda i: (i, 0)),
            pl.BlockSpec((4, D), lambda i: (0, 0)),
            pl.BlockSpec((rows, D), lambda i: (i, 0)),
            pl.BlockSpec((64, 8, TILE, LANES), lambda i: (3, 0, 0, 0)),
        ],
        out_specs=(
            pl.BlockSpec((rows, D), lambda i: (i, 0)),
            pl.BlockSpec((rows, D), lambda i: (i, 0)),
        ),
        compiler_params=params_of("arbitrary"),
        cost_estimate=cost(2.2e9, 12e6),
        name="middle_rows",
    )(x, mod, mixture, tiles.reshape(-1, 8, TILE, LANES))


def ffn_kernel(
    mid_ref, mod_ref, low_ref, dy_ref, up_ref, down_ref,
    out_ref, dmid_ref, low_dmid_ref, dmod_ref, dup_ref, ddown_ref,
    y_acc, dh_acc, low_t, act_s, du_s,
):
    step = pl.program_id(0)
    frames = mid_ref.shape[0]
    rows = 256

    @pl.when(step == 0)
    def _():
        y_acc[...] = jnp.zeros_like(y_acc)
        dh_acc[...] = jnp.zeros_like(dh_acc)
        low_t[...] = low_ref[...].T

    up = from_tiles(up_ref, 0, up_ref.shape[1])
    down = from_tiles(down_ref, 0, down_ref.shape[1])
    for offset in range(0, frames, rows):
        here = slice(offset, offset + rows)
        hidden = dot_nn(low_ref[here, :], up)
        grad_act = dot_nt(dy_ref[here, :], down)
        square = hidden * hidden
        inner = GELU_C * (hidden + GELU_A * (square * hidden))
        bend = jnp.tanh(inner)
        half = 0.5 * (1.0 + bend)
        act = (hidden * half).astype(BF)
        slope = half + 0.5 * hidden * (1.0 - bend * bend) * (
            GELU_C * (1.0 + 3.0 * GELU_A * square)
        )
        grad_hidden = (grad_act * slope).astype(BF)
        act_s[here, :] = act
        du_s[here, :] = grad_hidden
        y_acc[here, :] += dot_nn(act, down)
        dh_acc[here, :] += dot_nt(grad_hidden, up)
    to_tiles(ddown_ref, 0, dot_tn(act_s[...], dy_ref[...]))
    to_tiles(dup_ref, 0, dot_nn(low_t[...], du_s[...]))

    @pl.when(step == pl.num_programs(0) - 1)
    def _():
        grad_gain = jnp.zeros((1, D), F32)
        grad_shift = jnp.zeros((1, D), F32)
        for offset in range(0, frames, rows):
            here = slice(offset, offset + rows)
            middle = mid_ref[here, :]
            out_ref[here, :] = (middle + y_acc[here, :]).astype(BF)
            zhat, inverse = centre(middle)
            grad = dh_acc[here, :]
            grad_gain += jnp.sum(grad * zhat, 0, keepdims=True)
            grad_shift += jnp.sum(grad, 0, keepdims=True)
            grad_mid = dy_ref[here, :].astype(F32) + norm_back(zhat, inverse, grad, mod_ref[2:3, :])
            dmid_ref[here, :] = grad_mid
            low_dmid_ref[here, :] = grad_mid.astype(BF)
        dmod_ref[0:1, :] = grad_gain
        dmod_ref[1:2, :] = grad_shift


def ffn_both(middle, mod, low_two, dy, tiles):
    chunks = 4
    width = chunks * LANES
    steps = FF // width
    whole = lambda *shape: pl.BlockSpec(shape, lambda j: (0,) * len(shape))
    once = lambda *shape: pl.BlockSpec(
        shape, lambda j: (0,) * len(shape), pipeline_mode=pl.Buffered(1)
    )
    return pl.pallas_call(
        ffn_kernel,
        grid=(steps,),
        out_shape=(
            jax.ShapeDtypeStruct((1024, D), BF),
            jax.ShapeDtypeStruct((1024, D), F32),
            jax.ShapeDtypeStruct((1024, D), BF),
            jax.ShapeDtypeStruct((2, D), F32),
            jax.ShapeDtypeStruct((64, 32, TILE, LANES), BF),
            jax.ShapeDtypeStruct((256, 8, TILE, LANES), BF),
        ),
        in_specs=[
            once(1024, D),
            whole(4, D),
            once(1024, D),
            once(1024, D),
            pl.BlockSpec((64, chunks, TILE, LANES), lambda j: (1, j, 0, 0)),
            pl.BlockSpec((width // TILE, 8, TILE, LANES), lambda j: (512 * TILE // width + j, 0, 0, 0)),
        ],
        out_specs=(
            once(1024, D),
            once(1024, D),
            once(1024, D),
            whole(2, D),
            pl.BlockSpec((64, chunks, TILE, LANES), lambda j: (0, j, 0, 0)),
            pl.BlockSpec((width // TILE, 8, TILE, LANES), lambda j: (j, 0, 0, 0)),
        ),
        scratch_shapes=[
            pltpu.VMEM((1024, D), F32),
            pltpu.VMEM((1024, D), F32),
            pltpu.VMEM((D, 1024), BF),
            pltpu.VMEM((1024, width), BF),
            pltpu.VMEM((1024, width), BF),
        ],
        compiler_params=params_of("arbitrary"),
        cost_estimate=cost(52e9, 60e6, 4e6),
        name="ffn_both",
    )(
        middle, mod, low_two, dy,
        tiles.reshape(-1, 32, TILE, LANES), tiles.reshape(-1, 8, TILE, LANES),
    )


def out_back_kernel(mix_ref, dmid_ref, w_ref, dmix_ref, dw_ref):
    weights = from_tiles(w_ref, 0, w_ref.shape[1])
    dmix_ref[...] = dot_nt(dmid_ref[...], weights).astype(BF)
    to_tiles(dw_ref, 0, dot_tn(mix_ref[...], dmid_ref[...]))


def out_back(mixture, low_dmid, tiles):
    width = 256
    return pl.pallas_call(
        out_back_kernel,
        grid=(D // width,),
        out_shape=(
            jax.ShapeDtypeStruct((1024, D), BF),
            jax.ShapeDtypeStruct((64, 8, TILE, LANES), BF),
        ),
        in_specs=[
            pl.BlockSpec((1024, width), lambda j: (0, j)),
            pl.BlockSpec((1024, D), lambda j: (0, 0)),
            pl.BlockSpec((width // TILE, 8, TILE, LANES), lambda j: (192 * TILE // width + j, 0, 0, 0)),
        ],
        out_specs=(
            pl.BlockSpec((1024, width), lambda j: (0, j)),
            pl.BlockSpec((width // TILE, 8, TILE, LANES), lambda j: (j, 0, 0, 0)),
        ),
        compiler_params=params_of("arbitrary"),
        cost_estimate=cost(4.3e9, 10e6),
        name="out_back",
    )(mixture, low_dmid, tiles.reshape(-1, 8, TILE, LANES))


def qkv_weight_kernel(low_ref, dq_ref, dk_ref, dv_ref, dw_ref):
    for third, grad_ref in enumerate((dq_ref, dk_ref, dv_ref)):
        to_tiles(dw_ref, third * 8, dot_tn(low_ref[...], grad_ref[...]))


def qkv_weight_grad(low_one, dq, dk, dv):
    width = 256
    whole = pl.BlockSpec((1024, D), lambda j: (0, 0))
    return pl.pallas_call(
        qkv_weight_kernel,
        grid=(D // width,),
        out_shape=jax.ShapeDtypeStruct((64, 24, TILE, LANES), BF),
        in_specs=[pl.BlockSpec((1024, width), lambda j: (0, j)), whole, whole, whole],
        out_specs=pl.BlockSpec((width // TILE, 24, TILE, LANES), lambda j: (j, 0, 0, 0)),
        compiler_params=params_of("arbitrary"),
        cost_estimate=cost(6.4e9, 15e6),
        name="qkv_weight_grad",
    )(low_one, dq, dk, dv)


def input_kernel(x_ref, mod_ref, dmid_ref, dq_ref, dk_ref, dv_ref, w_ref, grad_ref, dmod_ref):
    grad = None
    for third, part_ref in enumerate((dq_ref, dk_ref, dv_ref)):
        part = dot_nt(part_ref[...], from_tiles(w_ref, third * 8, 8))
        grad = part if grad is None else grad + part
    zhat, inverse = centre(x_ref[...].astype(F32))

    @pl.when(pl.program_id(0) == 0)
    def _():
        dmod_ref[...] = jnp.zeros_like(dmod_ref)

    dmod_ref[0:1, :] += jnp.sum(grad * zhat, 0, keepdims=True)
    dmod_ref[1:2, :] += jnp.sum(grad, 0, keepdims=True)
    grad_ref[...] = (dmid_ref[...] + norm_back(zhat, inverse, grad, mod_ref[0:1, :])).astype(BF)


def input_back(x, mod, dmid, dq, dk, dv, tiles):
    rows = 256
    block = pl.BlockSpec((rows, D), lambda i: (i, 0))
    return pl.pallas_call(
        input_kernel,
        grid=(1024 // rows,),
        out_shape=(jax.ShapeDtypeStruct((1024, D), BF), jax.ShapeDtypeStruct((2, D), F32)),
        in_specs=[
            block,
            pl.BlockSpec((4, D), lambda i: (0, 0)),
            block,
            block,
            block,
            block,
            pl.BlockSpec((64, 24, TILE, LANES), lambda i: (0, 0, 0, 0)),
        ],
        out_specs=(block, pl.BlockSpec((2, D), lambda i: (0, 0))),
        compiler_params=params_of("arbitrary"),
        cost_estimate=cost(6.4e9, 22e6),
        name="input_back",
    )(x, mod, dmid, dq, dk, dv, tiles.reshape(-1, 24, TILE, LANES))


def flat_index():
    return lax.axis_index(("dp", "fsdp"))


def exchange(value, mask, count):
    return lax.ppermute(value, ("dp", "fsdp"), [(i, i ^ mask) for i in range(count)])


def sum_everywhere(value, count):
    mask = 1
    while mask < count:
        value = value + exchange(value, mask, count)
        mask *= 2
    return value


def fast_device(tokens, key_len, section, params, first_moment, second_moment, cotangent):
    count = lax.axis_size(("dp", "fsdp"))
    index = flat_index()
    shard = params.shape[0]
    table_size = SECTIONS * 4 * D
    aligned = (count * shard - table_size) // count
    slip = table_size // count
    kinds = shard_kinds(index)
    x = tokens[0]
    dy = cotangent[0]

    before = lax.ppermute(
        params[shard - table_size :], ("dp", "fsdp"), [(i, i + 1) for i in range(count - 1)]
    )
    own = lax.dynamic_slice(
        jnp.concatenate([before, params]), (table_size - index * slip,), (aligned,)
    )
    packed = pack_shard(kinds, own.reshape(aligned // LANES, LANES))
    tiles = gather_tiles(packed, index, count)

    last = index == count - 1
    table = jnp.where(last, params[shard - table_size :], 0.0).astype(BF)
    table = sum_everywhere(table.reshape(SECTIONS, 4 * D), count)
    picker = (section[0] - 1 == jnp.arange(SECTIONS)).astype(F32)[:, None]
    mod = jnp.sum(picker * table.astype(F32), 0).reshape(4, D)

    low_one, qkv = project_qkv(x, mod, tiles)
    mixture = attend(key_len, qkv)
    middle, low_two = middle_rows(x, mod, mixture, tiles)
    block_out, dmid, low_dmid, dmod_two, grad_up, grad_down = ffn_both(
        middle, mod, low_two, dy, tiles
    )
    grad_mix, grad_out = out_back(mixture, low_dmid, tiles)
    dq, dk, dv = attend_back(key_len, qkv, grad_mix)
    grad_qkv = qkv_weight_grad(low_one, dq, dk, dv)
    input_grad, dmod_one = input_back(x, mod, dmid, dq, dk, dv, tiles)

    per_item = jnp.concatenate([dmod_one, dmod_two], 0).reshape(1, 4 * D)
    section_grad = sum_everywhere(picker * per_item, count)

    reduced = reduce_tiles(grad_qkv, grad_out, grad_up, grad_down, index, count)
    summed = unpack_shard(kinds, reduced).reshape(aligned)
    after = lax.ppermute(
        summed[:table_size], ("dp", "fsdp"), [(i, i - 1) for i in range(1, count)]
    )
    after = jnp.where(last, section_grad.reshape(table_size), after)
    param_grad = lax.dynamic_slice(jnp.concatenate([summed, after]), (index * slip,), (shard,))
    new_first = beta_one * first_moment + (1.0 - beta_one) * param_grad
    new_second = beta_two * second_moment + (1.0 - beta_two) * param_grad * param_grad
    new_params = params - learn_rate * (new_first / bias_one) / (
        jnp.sqrt(new_second / bias_two) + adam_eps
    )
    return (
        block_out[None],
        input_grad[None],
        param_grad,
        new_params,
        new_first,
        new_second,
        section_grad,
    )


def gather_tiles(packed, index, count):
    return lax.all_gather(packed, ("dp", "fsdp"), axis=0, tiled=True)


def reduce_tiles(grad_qkv, grad_out, grad_up, grad_down, index, count):
    parts = [g.reshape(-1, TILE, LANES) for g in (grad_qkv, grad_out, grad_up, grad_down)]
    return lax.psum_scatter(
        jnp.concatenate(parts, 0), ("dp", "fsdp"), scatter_dimension=0, tiled=True
    )


def solution(mesh):
    in_specs = (
        P(("dp", "fsdp"), None, None),
        P(("dp", "fsdp")),
        P(("dp", "fsdp")),
        P(("dp", "fsdp")),
        P(("dp", "fsdp")),
        P(("dp", "fsdp")),
        P(("dp", "fsdp"), None, None),
    )
    out_specs = (
        P(("dp", "fsdp"), None, None),
        P(("dp", "fsdp"), None, None),
        P(("dp", "fsdp")),
        P(("dp", "fsdp")),
        P(("dp", "fsdp")),
        P(("dp", "fsdp")),
        P(),
    )
    fast = dict(mesh.shape) == {"dp": 8, "fsdp": 4}
    return jax.shard_map(
        fast_device if fast else per_device, mesh=mesh, in_specs=in_specs, out_specs=out_specs, check_vma=False
    )
```

```python
import jax
import jax.numpy as jnp
from jax import lax
from jax.experimental import pallas as pl
from jax.experimental.pallas import tpu as pltpu
from jax.sharding import PartitionSpec as P

D = 1024
HEADS = 16
FF = 4096
SECTIONS = 7


beta_one = 0.9
beta_two = 0.95
adam_eps = 1e-08
learn_rate = 0.05
bias_one = 1.0 - 0.9**10
bias_two = 1.0 - 0.95**10


def adanorm(field, gain_rows, shift_rows):
    average = jnp.mean(field, -1, keepdims=True)
    centred = field - average
    spread = jnp.mean(centred * centred, -1, keepdims=True)
    return centred * lax.rsqrt(spread + 1e-05) * gain_rows + shift_rows


def unpack(flat):
    first = 3 * D * D
    second = first + D * D
    third = second + D * FF
    fourth = third + FF * D
    return (
        flat[:first].reshape(D, 3 * D),
        flat[first:second].reshape(D, D),
        flat[second:third].reshape(D, FF),
        flat[third:fourth].reshape(FF, D),
        flat[fourth:].reshape(SECTIONS, 4 * D),
    )


def dot_trans(left, right):
    return lax.dot_general(
        left, right, (((1,), (1,)), ((), ())), preferred_element_type=jnp.float32
    )


def dot_inner(left, right):
    return lax.dot_general(
        left, right, (((0,), (0,)), ((), ())), preferred_element_type=jnp.float32
    )


def masked_scores(query_block, keys_all, key_valid, score_scale):
    scores = (
        jnp.einsum("qhd,khd->hqk", query_block, keys_all, preferred_element_type=jnp.float32)
        * score_scale
    )
    return jnp.where(key_valid, scores, -1e30)


def attend_forward(operands):
    queries, keys_all, values, valid_count = operands
    frames = queries.shape[0]
    block_rows = min(512, frames)
    score_scale = queries.shape[2] ** (-0.5)
    key_valid = (jnp.arange(frames) < valid_count)[None, None, :]
    outputs = []
    totals = []
    for offset in range(0, frames, block_rows):
        scores = masked_scores(
            queries[offset : offset + block_rows], keys_all, key_valid, score_scale
        )
        row_max = jnp.max(scores, -1, keepdims=True)
        log_total = row_max + jnp.log(jnp.sum(jnp.exp(scores - row_max), -1, keepdims=True))
        softmax_w = jnp.exp(scores - log_total).astype(jnp.bfloat16)
        outputs.append(
            jnp.einsum(
                "hqk,khd->qhd", softmax_w, values, preferred_element_type=jnp.float32
            ).astype(jnp.bfloat16)
        )
        totals.append(log_total[..., 0])
    return (jnp.concatenate(outputs, 0), jnp.concatenate(totals, 1))


def attend_backward(operands):
    queries, keys_all, values, valid_count, log_totals, grad_mix = operands
    frames = queries.shape[0]
    block_rows = min(512, frames)
    score_scale = queries.shape[2] ** (-0.5)
    key_valid = (jnp.arange(frames) < valid_count)[None, None, :]
    grad_keys = jnp.zeros(keys_all.shape, jnp.float32)
    grad_values = jnp.zeros(values.shape, jnp.float32)
    grad_queries = []
    for offset in range(0, frames, block_rows):
        query_block = queries[offset : offset + block_rows]
        grad_block = grad_mix[offset : offset + block_rows]
        scores = masked_scores(query_block, keys_all, key_valid, score_scale)
        softmax_w = jnp.exp(scores - log_totals[:, offset : offset + block_rows, None])
        grad_probs = jnp.einsum(
            "qhd,khd->hqk", grad_block, values, preferred_element_type=jnp.float32
        )
        grad_values = grad_values + jnp.einsum(
            "hqk,qhd->khd",
            softmax_w.astype(jnp.bfloat16),
            grad_block,
            preferred_element_type=jnp.float32,
        )
        grad_scores = (
            softmax_w * (grad_probs - jnp.sum(softmax_w * grad_probs, -1, keepdims=True))
        ).astype(jnp.bfloat16)
        grad_queries.append(
            jnp.einsum("hqk,khd->qhd", grad_scores, keys_all, preferred_element_type=jnp.float32)
            * score_scale
        )
        grad_keys = (
            grad_keys
            + jnp.einsum(
                "hqk,qhd->khd", grad_scores, query_block, preferred_element_type=jnp.float32
            )
            * score_scale
        )
    return jnp.stack([jnp.concatenate(grad_queries, 0), grad_keys, grad_values], 1).astype(
        jnp.bfloat16
    )


def per_device(tokens, key_len, section, params, first_moment, second_moment, cotangent):
    item_count, frames, features = tokens.shape
    row_count = item_count * frames
    head_size = features // HEADS
    low_params = params.astype(jnp.bfloat16)
    gathered = lax.all_gather(low_params, ("dp", "fsdp"), axis=0, tiled=True)
    w_qkv, w_out, w_up, w_down, table = unpack(gathered)
    picker = (section[:, None] - 1 == jnp.arange(SECTIONS)[None, :]).astype(jnp.float32)
    modulation = jnp.dot(picker, table.astype(jnp.float32), precision=lax.Precision.HIGHEST)
    gain_one = modulation[:, None, 0:features]
    shift_one = modulation[:, None, features : 2 * features]
    gain_two = modulation[:, None, 2 * features : 3 * features]
    shift_two = modulation[:, None, 3 * features : 4 * features]
    inputs = tokens.astype(jnp.float32)
    normed_one, norm_one_back = jax.vjp(adanorm, inputs, gain_one, shift_one)
    low_one = normed_one.astype(jnp.bfloat16).reshape(row_count, features)
    qkv = jnp.dot(low_one, w_qkv, preferred_element_type=jnp.float32).astype(jnp.bfloat16)
    qkv = qkv.reshape(item_count, frames, 3, HEADS, head_size)
    queries = qkv[:, :, 0]
    keys_all = qkv[:, :, 1]
    values = qkv[:, :, 2]
    mixture, log_totals = lax.map(attend_forward, (queries, keys_all, values, key_len))
    mixture = mixture.reshape(row_count, features)
    attended = jnp.dot(mixture, w_out, preferred_element_type=jnp.float32)
    middle = inputs + attended.reshape(item_count, frames, features)
    normed_two, norm_two_back = jax.vjp(adanorm, middle, gain_two, shift_two)
    low_two = normed_two.astype(jnp.bfloat16).reshape(row_count, features)
    projected = jnp.dot(low_two, w_up, preferred_element_type=jnp.float32)
    activated, gelu_back = jax.vjp(jax.nn.gelu, projected)
    low_act = activated.astype(jnp.bfloat16)
    branch = jnp.dot(low_act, w_down, preferred_element_type=jnp.float32)
    block_out = (middle + branch.reshape(item_count, frames, features)).astype(jnp.bfloat16)
    regathered = lax.all_gather(low_params, ("dp", "fsdp"), axis=0, tiled=True)
    w_qkv, w_out, w_up, w_down, table = unpack(regathered)
    grad_y = cotangent.astype(jnp.float32)
    low_gy = cotangent.reshape(row_count, features)
    grad_down = dot_inner(low_act, low_gy)
    grad_act = dot_trans(low_gy, w_down)
    (grad_proj,) = gelu_back(grad_act)
    low_gp = grad_proj.astype(jnp.bfloat16)
    grad_up = dot_inner(low_two, low_gp)
    grad_norm_two = dot_trans(low_gp, w_up).reshape(item_count, frames, features)
    grad_mid_part, grad_gain_two, grad_shift_two = norm_two_back(grad_norm_two)
    grad_mid = grad_y + grad_mid_part
    low_gm = grad_mid.astype(jnp.bfloat16).reshape(row_count, features)
    grad_out_w = dot_inner(mixture, low_gm)
    grad_mix = (
        dot_trans(low_gm, w_out).astype(jnp.bfloat16).reshape(item_count, frames, HEADS, head_size)
    )
    grad_qkv = lax.map(attend_backward, (queries, keys_all, values, key_len, log_totals, grad_mix))
    grad_qkv = grad_qkv.reshape(row_count, 3 * features)
    grad_qkv_w = dot_inner(low_one, grad_qkv)
    grad_norm_one = dot_trans(grad_qkv, w_qkv).reshape(item_count, frames, features)
    grad_in_part, grad_gain_one, grad_shift_one = norm_one_back(grad_norm_one)
    input_grad = (grad_mid + grad_in_part).astype(jnp.bfloat16)
    per_item = jnp.concatenate(
        [grad_gain_one[:, 0], grad_shift_one[:, 0], grad_gain_two[:, 0], grad_shift_two[:, 0]], 1
    )
    grad_table = jnp.einsum("is,ic->sc", picker, per_item, precision=lax.Precision.HIGHEST)
    table_flat = grad_table.ravel()
    table_size = table_flat.shape[0]
    flat_grads = jnp.concatenate(
        [
            grad_qkv_w.ravel(),
            grad_out_w.ravel(),
            grad_up.ravel(),
            grad_down.ravel(),
            jnp.zeros((table_size,), jnp.float32),
        ]
    )
    table_start = flat_grads.shape[0] - table_size
    shard_size = params.shape[0]
    weight_part = lax.psum_scatter(
        lax.slice_in_dim(flat_grads, 0, lax.axis_size(("dp", "fsdp")) * shard_size, axis=0),
        ("dp", "fsdp"),
        scatter_dimension=0,
        tiled=True,
    )
    section_total = lax.psum(table_flat, ("dp", "fsdp"))
    padded = jnp.concatenate(
        [
            jnp.zeros((shard_size,), jnp.float32),
            section_total,
            jnp.zeros((shard_size,), jnp.float32),
        ]
    )
    slice_start = jnp.clip(
        lax.axis_index(("dp", "fsdp")) * shard_size - table_start + shard_size,
        0,
        table_size + shard_size,
    ).astype(jnp.int32)
    param_grad = weight_part + lax.dynamic_slice_in_dim(padded, slice_start, shard_size)
    section_grad = section_total.reshape(SECTIONS, 4 * features)
    new_first = beta_one * first_moment + (1.0 - beta_one) * param_grad
    new_second = beta_two * second_moment + (1.0 - beta_two) * param_grad * param_grad
    new_params = params - learn_rate * (new_first / bias_one) / (
        jnp.sqrt(new_second / bias_two) + adam_eps
    )
    return (block_out, input_grad, param_grad, new_params, new_first, new_second, section_grad)


LANES = 128
TILE = 16
EPS = 1e-05
VMEM_LIMIT = 62 * 1024 * 1024
GELU_C = 0.7978845608028654
GELU_A = 0.044715
BF = jnp.bfloat16
F32 = jnp.float32


def params_of(*semantics):
    return pltpu.CompilerParams(
        dimension_semantics=semantics or None, vmem_limit_bytes=VMEM_LIMIT
    )


def cost(flops, moved, transcendentals=0):
    return pl.CostEstimate(
        flops=int(flops), bytes_accessed=int(moved), transcendentals=int(transcendentals)
    )


ANYWHERE = pl.BlockSpec(memory_space=pl.ANY)


def without(kernel, first, count):
    def called(*refs):
        kernel(*refs[:first], *refs[first + count :])

    return called


def dot_nn(left, right):
    return lax.dot_general(left, right, (((1,), (0,)), ((), ())), preferred_element_type=F32)


def dot_nt(left, right):
    return lax.dot_general(left, right, (((1,), (1,)), ((), ())), preferred_element_type=F32)


def dot_tn(left, right):
    return lax.dot_general(left, right, (((0,), (0,)), ((), ())), preferred_element_type=F32)


def from_tiles(ref, first, count):
    rows = ref.shape[0] * TILE
    parts = [ref[:, first + c].reshape(rows, LANES) for c in range(count)]
    return parts[0] if count == 1 else jnp.concatenate(parts, 1)


def to_tiles(ref, first, value):
    rows, columns = value.shape
    for c in range(columns // LANES):
        part = value[:, c * LANES : (c + 1) * LANES].astype(BF)
        ref[:, first + c] = part.reshape(rows // TILE, TILE, LANES)


def row_chunks(kind):
    return {0: 3 * D // LANES, 1: D // LANES, 2: FF // LANES}[kind]


def each_tile(kinds, body):
    def span(kind, start, rows):
        step = row_chunks(kind)
        block = TILE * step

        def one(index, carry):
            base = start + index * block
            for c in range(step):
                body(base // TILE + c, base + c, step)
            return carry

        lax.fori_loop(0, rows // block, one, 0)

    @pl.when(kinds[0] == 0)
    def _():
        span(0, 0, 3072)

    for part in range(3):
        for kind in (1, 2):

            @pl.when(kinds[part] == kind)
            def _():
                span(kind, part * 1024, 1024)


def pack_kernel(kinds, flat_ref, tiles_ref):
    def body(tile, row, step):
        tiles_ref[tile] = flat_ref[pl.ds(row, TILE, stride=step), :].astype(BF)

    each_tile(kinds, body)


def unpack_kernel(kinds, tiles_ref, flat_ref):
    def body(tile, row, step):
        flat_ref[pl.ds(row, TILE, stride=step), :] = tiles_ref[tile].astype(F32)

    each_tile(kinds, body)


def shard_kinds(index):
    start = index * 3072 + jnp.arange(3, dtype=jnp.int32) * 1024
    qkv_end = 3 * D * D // LANES
    out_end = qkv_end + D * D // LANES
    up_end = out_end + D * FF // LANES
    return jnp.where(
        start < qkv_end, 0, jnp.where((start < out_end) | (start >= up_end), 1, 2)
    ).astype(jnp.int32)


def pack_shard(kinds, flat):
    return pl.pallas_call(
        pack_kernel,
        out_shape=jax.ShapeDtypeStruct((192, TILE, LANES), BF),
        in_specs=[pl.BlockSpec(memory_space=pltpu.SMEM), pl.BlockSpec(memory_space=pltpu.VMEM)],
        out_specs=pl.BlockSpec(memory_space=pltpu.VMEM),
        compiler_params=params_of(),
        cost_estimate=cost(0, 3 << 20),
        name="pack_shard",
    )(kinds, flat)


def unpack_shard(kinds, tiles):
    return pl.pallas_call(
        unpack_kernel,
        out_shape=jax.ShapeDtypeStruct((3072, LANES), F32),
        in_specs=[pl.BlockSpec(memory_space=pltpu.SMEM), pl.BlockSpec(memory_space=pltpu.VMEM)],
        out_specs=pl.BlockSpec(memory_space=pltpu.VMEM),
        compiler_params=params_of(),
        cost_estimate=cost(0, 3 << 20),
        name="unpack_shard",
    )(kinds, tiles)


def centre(field):
    average = jnp.mean(field, -1, keepdims=True)
    centred = field - average
    spread = jnp.mean(centred * centred, -1, keepdims=True)
    inverse = lax.rsqrt(spread + EPS)
    return centred * inverse, inverse


def norm_back(zhat, inverse, grad, gain):
    scaled = grad * gain
    mean_one = jnp.mean(scaled, -1, keepdims=True)
    mean_two = jnp.mean(scaled * zhat, -1, keepdims=True)
    return inverse * (scaled - mean_one - zhat * mean_two)


def qkv_kernel(x_ref, mod_ref, w_ref, low_ref, qkv_ref):
    @pl.when(pl.program_id(0) == 0)
    def _():
        zhat, _ = centre(x_ref[...].astype(F32))
        low_ref[...] = (zhat * mod_ref[0:1, :] + mod_ref[1:2, :]).astype(BF)

    weights = from_tiles(w_ref, 0, w_ref.shape[1])
    qkv_ref[...] = dot_nn(low_ref[...], weights).astype(BF)


def project_qkv(x, mod, tiles):
    chunks = 4
    width = chunks * LANES
    return pl.pallas_call(
        qkv_kernel,
        grid=(3 * D // width,),
        out_shape=(
            jax.ShapeDtypeStruct((1024, D), BF),
            jax.ShapeDtypeStruct((1024, 3 * D), BF),
        ),
        in_specs=[
            pl.BlockSpec((1024, D), lambda j: (0, 0)),
            pl.BlockSpec((4, D), lambda j: (0, 0)),
            pl.BlockSpec((64, chunks, TILE, LANES), lambda j: (0, j, 0, 0)),
        ],
        out_specs=(
            pl.BlockSpec((1024, D), lambda j: (0, 0)),
            pl.BlockSpec((1024, width), lambda j: (0, j)),
        ),
        compiler_params=params_of("arbitrary"),
        cost_estimate=cost(6.4e9, 18e6),
        name="project_qkv",
    )(x, mod, tiles.reshape(-1, 24, TILE, LANES))


def head_lanes(head):
    lane = lax.broadcasted_iota(jnp.int32, (1, LANES), 1)
    return (lane >= 64) if head else (lane < 64)


def attend_kernel(len_ref, q_ref, k_ref, v_ref, out_ref):
    rows = 256
    frames = k_ref.shape[0]
    valid = lax.broadcasted_iota(jnp.int32, (1, frames), 1) < len_ref[0]
    keys = k_ref[...]
    zero = jnp.zeros((), BF)
    values = [jnp.where(head_lanes(h), v_ref[...], zero) for h in range(2)]
    for offset in range(0, frames, rows):
        queries = q_ref[offset : offset + rows, :] * jnp.asarray(0.125, BF)
        total = None
        for h in range(2):
            scores = dot_nt(jnp.where(head_lanes(h), queries, zero), keys)
            scores = jnp.where(valid, scores, -1e30)
            weights = jnp.exp(scores - jnp.max(scores, -1, keepdims=True))
            weights = weights * (1.0 / jnp.sum(weights, -1, keepdims=True))
            mixed = dot_nn(weights.astype(BF), values[h])
            total = mixed if total is None else total + mixed
        out_ref[offset : offset + rows, :] = total.astype(BF)


def attend(key_len, qkv):
    pairs = HEADS // 2
    return pl.pallas_call(
        attend_kernel,
        grid=(pairs,),
        out_shape=jax.ShapeDtypeStruct((1024, D), BF),
        in_specs=[
            pl.BlockSpec(memory_space=pltpu.SMEM),
            pl.BlockSpec((1024, LANES), lambda j: (0, j)),
            pl.BlockSpec((1024, LANES), lambda j: (0, pairs + j)),
            pl.BlockSpec((1024, LANES), lambda j: (0, 2 * pairs + j)),
        ],
        out_specs=pl.BlockSpec((1024, LANES), lambda j: (0, j)),
        compiler_params=params_of("arbitrary"),
        cost_estimate=cost(17e9, 8e6, 16e6),
        name="attend",
    )(key_len, qkv, qkv, qkv)


def attend_back_kernel(len_ref, q_ref, k_ref, v_ref, do_ref, dq_ref, dk_ref, dv_ref, dk_acc, dv_acc):
    rows = 256
    frames = k_ref.shape[0]
    valid = lax.broadcasted_iota(jnp.int32, (frames, 1), 0) < len_ref[0]
    keys = k_ref[...]
    values = v_ref[...]
    zero = jnp.zeros((), BF)
    masked_keys = [jnp.where(head_lanes(h), keys, zero) for h in range(2)]
    for offset in range(0, frames, rows):
        queries = q_ref[offset : offset + rows, :] * jnp.asarray(0.125, BF)
        grads = do_ref[offset : offset + rows, :]
        total = None
        for h in range(2):
            masked_q = jnp.where(head_lanes(h), queries, zero)
            masked_g = jnp.where(head_lanes(h), grads, zero)
            scores = dot_nt(keys, masked_q)
            scores = jnp.where(valid, scores, -1e30)
            weights = jnp.exp(scores - jnp.max(scores, 0, keepdims=True))
            weights = weights * (1.0 / jnp.sum(weights, 0, keepdims=True))
            grad_w = dot_nt(values, masked_g)
            product = weights * grad_w
            back = product - weights * jnp.sum(product, 0, keepdims=True)
            back = back.astype(BF)
            part_v = dot_nn(weights.astype(BF), masked_g)
            part_k = dot_nn(back, masked_q)
            if offset == 0 and h == 0:
                dv_acc[...] = part_v
                dk_acc[...] = part_k
            else:
                dv_acc[...] += part_v
                dk_acc[...] += part_k
            part_q = dot_tn(back, masked_keys[h])
            total = part_q if total is None else total + part_q
        dq_ref[offset : offset + rows, :] = (total * 0.125).astype(BF)
    dk_ref[...] = dk_acc[...].astype(BF)
    dv_ref[...] = dv_acc[...].astype(BF)


def attend_back(key_len, qkv, grad_mix, first, count, earlier, waits=()):
    pairs = HEADS // 2
    block = lambda shift: pl.BlockSpec((1024, LANES), lambda j: (0, shift + first + j))
    kept = () if earlier is None else tuple(earlier)
    return pl.pallas_call(
        without(attend_back_kernel, 5, len(kept) + len(waits)),
        grid=(count,),
        out_shape=(jax.ShapeDtypeStruct((1024, D), BF),) * 3,
        in_specs=[
            pl.BlockSpec(memory_space=pltpu.SMEM),
            block(0),
            block(pairs),
            block(2 * pairs),
            block(0),
        ]
        + [ANYWHERE] * (len(kept) + len(waits)),
        out_specs=(block(0),) * 3,
        input_output_aliases={5 + i: i for i in range(len(kept))},
        scratch_shapes=[pltpu.VMEM((1024, LANES), F32)] * 2,
        compiler_params=params_of("arbitrary"),
        cost_estimate=cost(11e9 * count, 2e6 * count, 4e6 * count),
        name="attend_back",
    )(key_len, qkv, qkv, qkv, grad_mix, *kept, *waits)


def middle_kernel(x_ref, mod_ref, mix_ref, w_ref, mid_ref, low_ref):
    weights = from_tiles(w_ref, 0, w_ref.shape[1])
    middle = x_ref[...].astype(F32) + dot_nn(mix_ref[...], weights)
    mid_ref[...] = middle
    zhat, _ = centre(middle)
    low_ref[...] = (zhat * mod_ref[2:3, :] + mod_ref[3:4, :]).astype(BF)


def middle_rows(x, mod, mixture, tiles):
    rows = 256
    return pl.pallas_call(
        middle_kernel,
        grid=(1024 // rows,),
        out_shape=(jax.ShapeDtypeStruct((1024, D), F32), jax.ShapeDtypeStruct((1024, D), BF)),
        in_specs=[
            pl.BlockSpec((rows, D), lambda i: (i, 0)),
            pl.BlockSpec((4, D), lambda i: (0, 0)),
            pl.BlockSpec((rows, D), lambda i: (i, 0)),
            pl.BlockSpec((64, 8, TILE, LANES), lambda i: (3, 0, 0, 0)),
        ],
        out_specs=(
            pl.BlockSpec((rows, D), lambda i: (i, 0)),
            pl.BlockSpec((rows, D), lambda i: (i, 0)),
        ),
        compiler_params=params_of("arbitrary"),
        cost_estimate=cost(2.2e9, 12e6),
        name="middle_rows",
    )(x, mod, mixture, tiles.reshape(-1, 8, TILE, LANES))


def ffn_kernel(
    mid_ref, mod_ref, low_ref, dy_ref, up_ref, down_ref,
    out_ref, dmid_ref, low_dmid_ref, dmod_ref, grads_ref,
    y_acc, dh_acc, low_t, act_s, du_s, dup_s, ddown_s, sems,
):
    step = pl.program_id(0)
    frames = mid_ref.shape[0]
    rows = 256

    @pl.when(step == 0)
    def _():
        y_acc[...] = jnp.zeros_like(y_acc)
        dh_acc[...] = jnp.zeros_like(dh_acc)
        low_t[...] = low_ref[...].T

    up = from_tiles(up_ref, 0, up_ref.shape[1])
    down = from_tiles(down_ref, 0, down_ref.shape[1])
    for offset in range(0, frames, rows):
        here = slice(offset, offset + rows)
        hidden = dot_nn(low_ref[here, :], up)
        grad_act = dot_nt(dy_ref[here, :], down)
        square = hidden * hidden
        inner = GELU_C * (hidden + GELU_A * (square * hidden))
        bend = jnp.tanh(inner)
        half = 0.5 * (1.0 + bend)
        act = (hidden * half).astype(BF)
        slope = half + 0.5 * hidden * (1.0 - bend * bend) * (
            GELU_C * (1.0 + 3.0 * GELU_A * square)
        )
        grad_hidden = (grad_act * slope).astype(BF)
        act_s[here, :] = act
        du_s[here, :] = grad_hidden
        y_acc[here, :] += dot_nn(act, down)
        dh_acc[here, :] += dot_nt(grad_hidden, up)
    slot = step % 2

    def copies(which, index):
        return (
            pltpu.make_async_copy(
                ddown_s.at[which], grads_ref.at[pl.ds(80 + index * 8, 8)], sems.at[which, 0]
            ),
            pltpu.make_async_copy(
                dup_s.at[which],
                grads_ref.at[pl.ds(16, 64), pl.ds(index * 4, 4)],
                sems.at[which, 1],
            ),
        )

    @pl.when(step >= 2)
    def _():
        for copy in copies(slot, step - 2):
            copy.wait()

    grad_down = dot_tn(act_s[...], dy_ref[...])
    for c in range(D // LANES):
        part = grad_down[:, c * LANES : (c + 1) * LANES].astype(BF).reshape(8, 4, TILE, LANES)
        for r in range(4):
            ddown_s[slot, :, r * 8 + c] = part[:, r]
    grad_up = dot_nn(low_t[...], du_s[...])
    for c in range(4):
        part = grad_up[:, c * LANES : (c + 1) * LANES].astype(BF)
        dup_s[slot, :, c] = part.reshape(64, TILE, LANES)
    for copy in copies(slot, step):
        copy.start()

    @pl.when(step == pl.num_programs(0) - 1)
    def _():
        for index in (step - 1, step):
            for copy in copies(index % 2, index):
                copy.wait()

    @pl.when(step == pl.num_programs(0) - 1)
    def _():
        grad_gain = jnp.zeros((1, D), F32)
        grad_shift = jnp.zeros((1, D), F32)
        for offset in range(0, frames, rows):
            here = slice(offset, offset + rows)
            middle = mid_ref[here, :]
            out_ref[here, :] = (middle + y_acc[here, :]).astype(BF)
            zhat, inverse = centre(middle)
            grad = dh_acc[here, :]
            grad_gain += jnp.sum(grad * zhat, 0, keepdims=True)
            grad_shift += jnp.sum(grad, 0, keepdims=True)
            grad_mid = dy_ref[here, :].astype(F32) + norm_back(zhat, inverse, grad, mod_ref[2:3, :])
            dmid_ref[here, :] = grad_mid
            low_dmid_ref[here, :] = grad_mid.astype(BF)
        dmod_ref[0:1, :] = grad_gain
        dmod_ref[1:2, :] = grad_shift


def ffn_both(middle, mod, low_two, dy, tiles):
    chunks = 4
    width = chunks * LANES
    steps = FF // width
    whole = lambda *shape: pl.BlockSpec(shape, lambda j: (0,) * len(shape))
    once = lambda *shape: pl.BlockSpec(
        shape, lambda j: (0,) * len(shape), pipeline_mode=pl.Buffered(1)
    )
    return pl.pallas_call(
        ffn_kernel,
        grid=(steps,),
        out_shape=(
            jax.ShapeDtypeStruct((1024, D), BF),
            jax.ShapeDtypeStruct((1024, D), F32),
            jax.ShapeDtypeStruct((1024, D), BF),
            jax.ShapeDtypeStruct((2, D), F32),
            jax.ShapeDtypeStruct((144, 32, TILE, LANES), BF),
        ),
        in_specs=[
            once(1024, D),
            whole(4, D),
            once(1024, D),
            once(1024, D),
            pl.BlockSpec((64, chunks, TILE, LANES), lambda j: (1, j, 0, 0)),
            pl.BlockSpec((width // TILE, 8, TILE, LANES), lambda j: (512 * TILE // width + j, 0, 0, 0)),
        ],
        out_specs=(
            once(1024, D),
            once(1024, D),
            once(1024, D),
            whole(2, D),
            pl.BlockSpec(memory_space=pl.ANY),
        ),
        scratch_shapes=[
            pltpu.VMEM((1024, D), F32),
            pltpu.VMEM((1024, D), F32),
            pltpu.VMEM((D, 1024), BF),
            pltpu.VMEM((1024, width), BF),
            pltpu.VMEM((1024, width), BF),
            pltpu.VMEM((2, 64, 4, TILE, LANES), BF),
            pltpu.VMEM((2, 8, 32, TILE, LANES), BF),
            pltpu.SemaphoreType.DMA((2, 2)),
        ],
        compiler_params=params_of("arbitrary"),
        cost_estimate=cost(52e9, 60e6, 4e6),
        name="ffn_both",
    )(
        middle, mod, low_two, dy,
        tiles.reshape(-1, 32, TILE, LANES), tiles.reshape(-1, 8, TILE, LANES),
    )


def out_back_kernel(mix_ref, dmid_ref, w_ref, grads_ref, dmix_ref, dw_ref):
    weights = from_tiles(w_ref, 0, w_ref.shape[1])
    dmix_ref[...] = dot_nt(dmid_ref[...], weights).astype(BF)
    to_tiles(dw_ref, 0, dot_tn(mix_ref[...], dmid_ref[...]))


def out_back(mixture, low_dmid, tiles, grads):
    width = 256
    return pl.pallas_call(
        out_back_kernel,
        grid=(D // width,),
        out_shape=(
            jax.ShapeDtypeStruct((1024, D), BF),
            jax.ShapeDtypeStruct((576, 8, TILE, LANES), BF),
        ),
        in_specs=[
            pl.BlockSpec((1024, width), lambda j: (0, j)),
            pl.BlockSpec((1024, D), lambda j: (0, 0)),
            pl.BlockSpec((width // TILE, 8, TILE, LANES), lambda j: (192 * TILE // width + j, 0, 0, 0)),
            pl.BlockSpec(memory_space=pl.ANY),
        ],
        input_output_aliases={3: 1},
        out_specs=(
            pl.BlockSpec((1024, width), lambda j: (0, j)),
            pl.BlockSpec((width // TILE, 8, TILE, LANES), lambda j: (j, 0, 0, 0)),
        ),
        compiler_params=params_of("arbitrary"),
        cost_estimate=cost(4.3e9, 10e6),
        name="out_back",
    )(mixture, low_dmid, tiles.reshape(-1, 8, TILE, LANES), grads.reshape(-1, 8, TILE, LANES))


def qkv_weight_kernel(low_ref, dq_ref, dk_ref, dv_ref, dw_ref):
    for third, grad_ref in enumerate((dq_ref, dk_ref, dv_ref)):
        to_tiles(dw_ref, third * 8, dot_tn(low_ref[...], grad_ref[...]))


def qkv_weight_grad(low_one, dq, dk, dv, waits=()):
    width = 256
    whole = pl.BlockSpec((1024, D), lambda j: (0, 0))
    return pl.pallas_call(
        without(qkv_weight_kernel, 4, len(waits)),
        grid=(D // width,),
        out_shape=jax.ShapeDtypeStruct((64, 24, TILE, LANES), BF),
        in_specs=[pl.BlockSpec((1024, width), lambda j: (0, j)), whole, whole, whole]
        + [ANYWHERE] * len(waits),
        out_specs=pl.BlockSpec((width // TILE, 24, TILE, LANES), lambda j: (j, 0, 0, 0)),
        compiler_params=params_of("arbitrary"),
        cost_estimate=cost(6.4e9, 15e6),
        name="qkv_weight_grad",
    )(low_one, dq, dk, dv, *waits)


def input_kernel(x_ref, mod_ref, dmid_ref, dq_ref, dk_ref, dv_ref, w_ref, grad_ref, dmod_ref):
    grad = None
    for third, part_ref in enumerate((dq_ref, dk_ref, dv_ref)):
        part = dot_nt(part_ref[...], from_tiles(w_ref, third * 8, 8))
        grad = part if grad is None else grad + part
    zhat, inverse = centre(x_ref[...].astype(F32))

    @pl.when(pl.program_id(0) == 0)
    def _():
        dmod_ref[...] = jnp.zeros_like(dmod_ref)

    dmod_ref[0:1, :] += jnp.sum(grad * zhat, 0, keepdims=True)
    dmod_ref[1:2, :] += jnp.sum(grad, 0, keepdims=True)
    grad_ref[...] = (dmid_ref[...] + norm_back(zhat, inverse, grad, mod_ref[0:1, :])).astype(BF)


def input_back(x, mod, dmid, dq, dk, dv, tiles, waits=()):
    rows = 256
    block = pl.BlockSpec((rows, D), lambda i: (i, 0))
    return pl.pallas_call(
        without(input_kernel, 7, len(waits)),
        grid=(1024 // rows,),
        out_shape=(jax.ShapeDtypeStruct((1024, D), BF), jax.ShapeDtypeStruct((2, D), F32)),
        in_specs=[
            block,
            pl.BlockSpec((4, D), lambda i: (0, 0)),
            block,
            block,
            block,
            block,
            pl.BlockSpec((64, 24, TILE, LANES), lambda i: (0, 0, 0, 0)),
        ]
        + [ANYWHERE] * len(waits),
        out_specs=(block, pl.BlockSpec((2, D), lambda i: (0, 0))),
        compiler_params=params_of("arbitrary"),
        cost_estimate=cost(6.4e9, 22e6),
        name="input_back",
    )(x, mod, dmid, dq, dk, dv, tiles.reshape(-1, 24, TILE, LANES), *waits)


def tile_spec(*lead, index):
    return pl.BlockSpec((*lead, TILE, LANES), lambda i, at: (*index(i, at), 0, 0))


def staged(kernel, name, outs, out_lead, ins, in_specs, sel, steps, moved, waits):
    spec = tile_spec(*out_lead, index=lambda i, at: (i,) + (0,) * (len(out_lead) - 1))
    shape = (steps,) + tuple(out_lead[1:]) + (TILE, LANES)
    return pl.pallas_call(
        without(kernel, 1 + len(ins), len(waits)),
        out_shape=(jax.ShapeDtypeStruct(shape, BF),) * outs,
        grid_spec=pltpu.PrefetchScalarGridSpec(
            num_scalar_prefetch=1,
            grid=(steps,),
            in_specs=in_specs + [ANYWHERE] * len(waits),
            out_specs=(spec,) * outs,
        ),
        compiler_params=params_of("arbitrary"),
        cost_estimate=cost(0, moved),
        name=name,
    )(sel, *ins, *waits)


def take_kernel(sel, value_ref, out_ref):
    out_ref[...] = value_ref[:, :, :, 0]


def take_other(sel, value, waits=()):
    layers = value.shape[0]
    spec = tile_spec(1, 2, 2, 1, 192, index=lambda i, at: (i, 0, 0, 1 - at[2], 0))
    return staged(
        take_kernel, "take_other", 1, (1, 2, 2, 192), [value], [spec], sel, layers, 6e6 * layers, waits
    )[0]


def both(left, right):
    return (left.astype(F32) + right.astype(F32)).astype(BF)


def core_kernel(sel, value_ref, moved_ref, one_send, one_keep, two_send, two_keep):
    y, x = sel[0], sel[1]
    one, two = slice(0, 96), slice(96, 192)
    for k in range(2):
        one_send[0, k] = both(value_ref[0, k, 1 - x, 0, one], moved_ref[0, k, 1 - x, one])
        one_keep[0, k] = both(value_ref[0, k, x, 0, one], moved_ref[0, k, x, one])
        two_send[0, k] = both(value_ref[0, 1 - y, k, 0, two], moved_ref[0, 1 - y, k, two])
        two_keep[0, k] = both(value_ref[0, y, k, 0, two], moved_ref[0, y, k, two])


def core_sum(sel, value, moved, waits=()):
    layers = value.shape[0]
    specs = [
        tile_spec(1, 2, 2, 1, 192, index=lambda i, at: (i, 0, 0, at[2], 0)),
        tile_spec(1, 2, 2, 192, index=lambda i, at: (i, 0, 0, 0)),
    ]
    return staged(
        core_kernel, "core_sum", 4, (1, 2, 96), [value, moved], specs, sel, layers, 9e6 * layers, waits
    )


def plane_kernel(sel, one_keep, one_moved, two_keep, two_moved, one_send, one_own, two_send, two_own):
    y, x = sel[0], sel[1]
    one_send[0] = both(one_keep[0, 1 - y], one_moved[0, 1 - y])
    one_own[0] = both(one_keep[0, y], one_moved[0, y])
    two_send[0] = both(two_keep[0, 1 - x], two_moved[0, 1 - x])
    two_own[0] = both(two_keep[0, x], two_moved[0, x])


def plane_sum(sel, *values, waits=()):
    layers = values[0].shape[0]
    spec = tile_spec(1, 2, 96, index=lambda i, at: (i, 0, 0))
    return staged(
        plane_kernel, "plane_sum", 4, (1, 96), values, [spec] * 4, sel, layers, 5e6 * layers, waits
    )


def line_kernel(sel, one_own, one_moved, two_own, two_moved, out_ref):
    out_ref[0, 0:96] = both(one_own[0], one_moved[0])
    out_ref[0, 96:192] = both(two_own[0], two_moved[0])


def line_sum(sel, *values, waits=()):
    layers = values[0].shape[0]
    spec = tile_spec(1, 96, index=lambda i, at: (i, 0))
    return staged(
        line_kernel, "line_sum", 1, (1, 192), values, [spec] * 4, sel, layers, 2.4e6 * layers, waits
    )[0]


def flat_index():
    return lax.axis_index(("dp", "fsdp"))


def exchange(value, mask, count):
    return lax.ppermute(value, ("dp", "fsdp"), [(i, i ^ mask) for i in range(count)])


def sum_everywhere(value, count):
    mask = 1
    while mask < count:
        value = value + exchange(value, mask, count)
        mask *= 2
    return value


def fast_device(tokens, key_len, section, params, first_moment, second_moment, cotangent):
    count = lax.axis_size(("dp", "fsdp"))
    index = flat_index()
    shard = params.shape[0]
    table_size = SECTIONS * 4 * D
    aligned = (count * shard - table_size) // count
    slip = table_size // count
    kinds = shard_kinds(index)
    x = tokens[0]
    dy = cotangent[0]

    before = lax.ppermute(
        params[shard - table_size :], ("dp", "fsdp"), [(i, i + 1) for i in range(count - 1)]
    )
    own = lax.dynamic_slice(
        jnp.concatenate([before, params]), (table_size - index * slip,), (aligned,)
    )
    packed = pack_shard(kinds, own.reshape(aligned // LANES, LANES))
    sel = jnp.stack([index // 4 % 2, index // 2 % 2, index % 2]).astype(jnp.int32)

    last = index == count - 1
    table = jnp.where(last, params[shard - table_size :], 0.0).astype(BF)
    table = sum_everywhere(table.reshape(SECTIONS, 4 * D), count)
    tiles = lax.all_gather(packed, ("dp", "fsdp"), axis=0, tiled=True)
    picker = (section[0] - 1 == jnp.arange(SECTIONS)).astype(F32)[:, None]
    mod = jnp.sum(picker * table.astype(F32), 0).reshape(4, D)

    low_one, qkv = project_qkv(x, mod, tiles)
    mixture = attend(key_len, qkv)
    middle, low_two = middle_rows(x, mod, mixture, tiles)
    block_out, dmid, low_dmid, dmod_two, grads = ffn_both(middle, mod, low_two, dy, tiles)
    grad_mix, grads = out_back(mixture, low_dmid, tiles, grads)

    grads = grads.reshape(3, 2, 2, 2, 192, TILE, LANES)
    sent = take_other(sel, grads)
    moved = exchange(sent, 1, count)
    back = attend_back(key_len, qkv, grad_mix, 0, 2, None, (sent,))
    one_send, one_keep, two_send, two_keep = core_sum(sel, grads, moved, back[:1])
    one_moved, two_moved = exchange(one_send, 2, count), exchange(two_send, 4, count)
    back = attend_back(key_len, qkv, grad_mix, 2, 2, back, (one_send,))
    back = attend_back(key_len, qkv, grad_mix, 4, 2, back)
    dq, dk, dv = attend_back(key_len, qkv, grad_mix, 6, 2, back)
    one_send, one_keep, two_send, two_keep = plane_sum(
        sel, one_keep, one_moved, two_keep, two_moved, waits=(dq,)
    )
    one_moved, two_moved = exchange(one_send, 4, count), exchange(two_send, 2, count)
    grad_qkv = qkv_weight_grad(low_one, dq, dk, dv, (one_send,))
    held = (one_keep, one_moved, two_keep, two_moved)

    grad_qkv = grad_qkv.reshape(1, 2, 2, 2, 192, TILE, LANES)
    sent = take_other(sel, grad_qkv)
    moved = exchange(sent, 1, count)
    one_send, one_keep, two_send, two_keep = core_sum(sel, grad_qkv, moved)
    one_moved, two_moved = exchange(one_send, 2, count), exchange(two_send, 4, count)
    rest = line_sum(sel, *held, waits=(one_send,))
    input_grad, dmod_one = input_back(x, mod, dmid, dq, dk, dv, tiles, (rest,))
    one_send, one_keep, two_send, two_keep = plane_sum(
        sel, one_keep, one_moved, two_keep, two_moved, waits=(input_grad,)
    )
    one_moved, two_moved = exchange(one_send, 4, count), exchange(two_send, 2, count)
    first = line_sum(sel, one_keep, one_moved, two_keep, two_moved)

    per_item = jnp.concatenate([dmod_one, dmod_two], 0).reshape(1, 4 * D)
    section_grad = sum_everywhere(picker * per_item, count)

    reduced = jnp.where(
        index // 8 == 0, reduce_first(first[0], count), reduce_rest(rest, index, count)
    ).reshape(192, TILE, LANES)
    summed = unpack_shard(kinds, reduced).reshape(aligned)
    following = lax.ppermute(
        summed[:table_size], ("dp", "fsdp"), [(i, i - 1) for i in range(1, count)]
    )
    following = jnp.where(last, section_grad.reshape(table_size), following)
    param_grad = lax.dynamic_slice(jnp.concatenate([summed, following]), (index * slip,), (shard,))
    new_first = beta_one * first_moment + (1.0 - beta_one) * param_grad
    new_second = beta_two * second_moment + (1.0 - beta_two) * param_grad * param_grad
    new_params = params - learn_rate * (new_first / bias_one) / (
        jnp.sqrt(new_second / bias_two) + adam_eps
    )
    return (
        block_out[None],
        input_grad[None],
        param_grad,
        new_params,
        new_first,
        new_second,
        section_grad,
    )


def add_low(*terms):
    return add_wide(*terms).astype(BF)


def add_wide(*terms):
    total = terms[0].astype(F32)
    for term in terms[1:]:
        total = total + term.astype(F32)
    return total


def layer_move(value, moves):
    pairs = [(8 * a + i, 8 * b + i) for a, b in moves for i in range(8)]
    return lax.ppermute(value, ("dp", "fsdp"), pairs)


def pick(value, index, axis):
    return lax.dynamic_index_in_dim(value, index, axis, keepdims=False)


def reduce_first(value, count):
    value = add_low(value, layer_move(value, [(3, 2), (1, 0)]))
    return add_wide(value, layer_move(value, [(2, 0)]))


def reduce_rest(value, index, count):
    layer = index // 8
    choose = lambda at: pick(value, jnp.clip(at, 0, 2), 0)
    up = layer_move(value[2], [(0, 1)])
    down = layer_move(value[0], [(3, 2)])
    up = layer_move(add_low(choose(1 + layer), up), [(0, 1), (1, 2)])
    down = layer_move(add_low(choose(layer - 2), down), [(3, 2), (2, 1)])
    up = layer_move(add_low(choose(layer), up), [(0, 1), (1, 2), (2, 3)])
    return add_wide(choose(layer - 1), up, down)


def solution(mesh):
    in_specs = (
        P(("dp", "fsdp"), None, None),
        P(("dp", "fsdp")),
        P(("dp", "fsdp")),
        P(("dp", "fsdp")),
        P(("dp", "fsdp")),
        P(("dp", "fsdp")),
        P(("dp", "fsdp"), None, None),
    )
    out_specs = (
        P(("dp", "fsdp"), None, None),
        P(("dp", "fsdp"), None, None),
        P(("dp", "fsdp")),
        P(("dp", "fsdp")),
        P(("dp", "fsdp")),
        P(("dp", "fsdp")),
        P(),
    )
    fast = dict(mesh.shape) == {"dp": 8, "fsdp": 4}
    return jax.shard_map(
        fast_device if fast else per_device, mesh=mesh, in_specs=in_specs, out_specs=out_specs, check_vma=False
    )
```

```python
import jax
import jax.numpy as jnp
from jax import lax
from jax.experimental import pallas as pl
from jax.experimental.pallas import tpu as pltpu
from jax.sharding import PartitionSpec as P

D = 1024
HEADS = 16
FF = 4096
SECTIONS = 7


beta_one = 0.9
beta_two = 0.95
adam_eps = 1e-08
learn_rate = 0.05
bias_one = 1.0 - 0.9**10
bias_two = 1.0 - 0.95**10


def adanorm(field, gain_rows, shift_rows):
    average = jnp.mean(field, -1, keepdims=True)
    centred = field - average
    spread = jnp.mean(centred * centred, -1, keepdims=True)
    return centred * lax.rsqrt(spread + 1e-05) * gain_rows + shift_rows


def unpack(flat):
    first = 3 * D * D
    second = first + D * D
    third = second + D * FF
    fourth = third + FF * D
    return (
        flat[:first].reshape(D, 3 * D),
        flat[first:second].reshape(D, D),
        flat[second:third].reshape(D, FF),
        flat[third:fourth].reshape(FF, D),
        flat[fourth:].reshape(SECTIONS, 4 * D),
    )


def dot_trans(left, right):
    return lax.dot_general(
        left, right, (((1,), (1,)), ((), ())), preferred_element_type=jnp.float32
    )


def dot_inner(left, right):
    return lax.dot_general(
        left, right, (((0,), (0,)), ((), ())), preferred_element_type=jnp.float32
    )


def masked_scores(query_block, keys_all, key_valid, score_scale):
    scores = (
        jnp.einsum("qhd,khd->hqk", query_block, keys_all, preferred_element_type=jnp.float32)
        * score_scale
    )
    return jnp.where(key_valid, scores, -1e30)


def attend_forward(operands):
    queries, keys_all, values, valid_count = operands
    frames = queries.shape[0]
    block_rows = min(512, frames)
    score_scale = queries.shape[2] ** (-0.5)
    key_valid = (jnp.arange(frames) < valid_count)[None, None, :]
    outputs = []
    totals = []
    for offset in range(0, frames, block_rows):
        scores = masked_scores(
            queries[offset : offset + block_rows], keys_all, key_valid, score_scale
        )
        row_max = jnp.max(scores, -1, keepdims=True)
        log_total = row_max + jnp.log(jnp.sum(jnp.exp(scores - row_max), -1, keepdims=True))
        softmax_w = jnp.exp(scores - log_total).astype(jnp.bfloat16)
        outputs.append(
            jnp.einsum(
                "hqk,khd->qhd", softmax_w, values, preferred_element_type=jnp.float32
            ).astype(jnp.bfloat16)
        )
        totals.append(log_total[..., 0])
    return (jnp.concatenate(outputs, 0), jnp.concatenate(totals, 1))


def attend_backward(operands):
    queries, keys_all, values, valid_count, log_totals, grad_mix = operands
    frames = queries.shape[0]
    block_rows = min(512, frames)
    score_scale = queries.shape[2] ** (-0.5)
    key_valid = (jnp.arange(frames) < valid_count)[None, None, :]
    grad_keys = jnp.zeros(keys_all.shape, jnp.float32)
    grad_values = jnp.zeros(values.shape, jnp.float32)
    grad_queries = []
    for offset in range(0, frames, block_rows):
        query_block = queries[offset : offset + block_rows]
        grad_block = grad_mix[offset : offset + block_rows]
        scores = masked_scores(query_block, keys_all, key_valid, score_scale)
        softmax_w = jnp.exp(scores - log_totals[:, offset : offset + block_rows, None])
        grad_probs = jnp.einsum(
            "qhd,khd->hqk", grad_block, values, preferred_element_type=jnp.float32
        )
        grad_values = grad_values + jnp.einsum(
            "hqk,qhd->khd",
            softmax_w.astype(jnp.bfloat16),
            grad_block,
            preferred_element_type=jnp.float32,
        )
        grad_scores = (
            softmax_w * (grad_probs - jnp.sum(softmax_w * grad_probs, -1, keepdims=True))
        ).astype(jnp.bfloat16)
        grad_queries.append(
            jnp.einsum("hqk,khd->qhd", grad_scores, keys_all, preferred_element_type=jnp.float32)
            * score_scale
        )
        grad_keys = (
            grad_keys
            + jnp.einsum(
                "hqk,qhd->khd", grad_scores, query_block, preferred_element_type=jnp.float32
            )
            * score_scale
        )
    return jnp.stack([jnp.concatenate(grad_queries, 0), grad_keys, grad_values], 1).astype(
        jnp.bfloat16
    )


def per_device(tokens, key_len, section, params, first_moment, second_moment, cotangent):
    item_count, frames, features = tokens.shape
    row_count = item_count * frames
    head_size = features // HEADS
    low_params = params.astype(jnp.bfloat16)
    gathered = lax.all_gather(low_params, ("dp", "fsdp"), axis=0, tiled=True)
    w_qkv, w_out, w_up, w_down, table = unpack(gathered)
    picker = (section[:, None] - 1 == jnp.arange(SECTIONS)[None, :]).astype(jnp.float32)
    modulation = jnp.dot(picker, table.astype(jnp.float32), precision=lax.Precision.HIGHEST)
    gain_one = modulation[:, None, 0:features]
    shift_one = modulation[:, None, features : 2 * features]
    gain_two = modulation[:, None, 2 * features : 3 * features]
    shift_two = modulation[:, None, 3 * features : 4 * features]
    inputs = tokens.astype(jnp.float32)
    normed_one, norm_one_back = jax.vjp(adanorm, inputs, gain_one, shift_one)
    low_one = normed_one.astype(jnp.bfloat16).reshape(row_count, features)
    qkv = jnp.dot(low_one, w_qkv, preferred_element_type=jnp.float32).astype(jnp.bfloat16)
    qkv = qkv.reshape(item_count, frames, 3, HEADS, head_size)
    queries = qkv[:, :, 0]
    keys_all = qkv[:, :, 1]
    values = qkv[:, :, 2]
    mixture, log_totals = lax.map(attend_forward, (queries, keys_all, values, key_len))
    mixture = mixture.reshape(row_count, features)
    attended = jnp.dot(mixture, w_out, preferred_element_type=jnp.float32)
    middle = inputs + attended.reshape(item_count, frames, features)
    normed_two, norm_two_back = jax.vjp(adanorm, middle, gain_two, shift_two)
    low_two = normed_two.astype(jnp.bfloat16).reshape(row_count, features)
    projected = jnp.dot(low_two, w_up, preferred_element_type=jnp.float32)
    activated, gelu_back = jax.vjp(jax.nn.gelu, projected)
    low_act = activated.astype(jnp.bfloat16)
    branch = jnp.dot(low_act, w_down, preferred_element_type=jnp.float32)
    block_out = (middle + branch.reshape(item_count, frames, features)).astype(jnp.bfloat16)
    regathered = lax.all_gather(low_params, ("dp", "fsdp"), axis=0, tiled=True)
    w_qkv, w_out, w_up, w_down, table = unpack(regathered)
    grad_y = cotangent.astype(jnp.float32)
    low_gy = cotangent.reshape(row_count, features)
    grad_down = dot_inner(low_act, low_gy)
    grad_act = dot_trans(low_gy, w_down)
    (grad_proj,) = gelu_back(grad_act)
    low_gp = grad_proj.astype(jnp.bfloat16)
    grad_up = dot_inner(low_two, low_gp)
    grad_norm_two = dot_trans(low_gp, w_up).reshape(item_count, frames, features)
    grad_mid_part, grad_gain_two, grad_shift_two = norm_two_back(grad_norm_two)
    grad_mid = grad_y + grad_mid_part
    low_gm = grad_mid.astype(jnp.bfloat16).reshape(row_count, features)
    grad_out_w = dot_inner(mixture, low_gm)
    grad_mix = (
        dot_trans(low_gm, w_out).astype(jnp.bfloat16).reshape(item_count, frames, HEADS, head_size)
    )
    grad_qkv = lax.map(attend_backward, (queries, keys_all, values, key_len, log_totals, grad_mix))
    grad_qkv = grad_qkv.reshape(row_count, 3 * features)
    grad_qkv_w = dot_inner(low_one, grad_qkv)
    grad_norm_one = dot_trans(grad_qkv, w_qkv).reshape(item_count, frames, features)
    grad_in_part, grad_gain_one, grad_shift_one = norm_one_back(grad_norm_one)
    input_grad = (grad_mid + grad_in_part).astype(jnp.bfloat16)
    per_item = jnp.concatenate(
        [grad_gain_one[:, 0], grad_shift_one[:, 0], grad_gain_two[:, 0], grad_shift_two[:, 0]], 1
    )
    grad_table = jnp.einsum("is,ic->sc", picker, per_item, precision=lax.Precision.HIGHEST)
    table_flat = grad_table.ravel()
    table_size = table_flat.shape[0]
    flat_grads = jnp.concatenate(
        [
            grad_qkv_w.ravel(),
            grad_out_w.ravel(),
            grad_up.ravel(),
            grad_down.ravel(),
            jnp.zeros((table_size,), jnp.float32),
        ]
    )
    table_start = flat_grads.shape[0] - table_size
    shard_size = params.shape[0]
    weight_part = lax.psum_scatter(
        lax.slice_in_dim(flat_grads, 0, lax.axis_size(("dp", "fsdp")) * shard_size, axis=0),
        ("dp", "fsdp"),
        scatter_dimension=0,
        tiled=True,
    )
    section_total = lax.psum(table_flat, ("dp", "fsdp"))
    padded = jnp.concatenate(
        [
            jnp.zeros((shard_size,), jnp.float32),
            section_total,
            jnp.zeros((shard_size,), jnp.float32),
        ]
    )
    slice_start = jnp.clip(
        lax.axis_index(("dp", "fsdp")) * shard_size - table_start + shard_size,
        0,
        table_size + shard_size,
    ).astype(jnp.int32)
    param_grad = weight_part + lax.dynamic_slice_in_dim(padded, slice_start, shard_size)
    section_grad = section_total.reshape(SECTIONS, 4 * features)
    new_first = beta_one * first_moment + (1.0 - beta_one) * param_grad
    new_second = beta_two * second_moment + (1.0 - beta_two) * param_grad * param_grad
    new_params = params - learn_rate * (new_first / bias_one) / (
        jnp.sqrt(new_second / bias_two) + adam_eps
    )
    return (block_out, input_grad, param_grad, new_params, new_first, new_second, section_grad)


LANES = 128
TILE = 16
EPS = 1e-05
VMEM_LIMIT = 62 * 1024 * 1024
GELU_C = 0.7978845608028654
GELU_A = 0.044715
BF = jnp.bfloat16
F32 = jnp.float32


def params_of(*semantics):
    return pltpu.CompilerParams(
        dimension_semantics=semantics or None, vmem_limit_bytes=VMEM_LIMIT
    )


def cost(flops, moved, transcendentals=0):
    return pl.CostEstimate(
        flops=int(flops), bytes_accessed=int(moved), transcendentals=int(transcendentals)
    )


ANYWHERE = pl.BlockSpec(memory_space=pl.ANY)


def without(kernel, first, count):
    def called(*refs):
        kernel(*refs[:first], *refs[first + count :])

    return called


def dot_nn(left, right):
    return lax.dot_general(left, right, (((1,), (0,)), ((), ())), preferred_element_type=F32)


def dot_nt(left, right):
    return lax.dot_general(left, right, (((1,), (1,)), ((), ())), preferred_element_type=F32)


def dot_tn(left, right):
    return lax.dot_general(left, right, (((0,), (0,)), ((), ())), preferred_element_type=F32)


def from_tiles(ref, first, count):
    rows = ref.shape[0] * TILE
    parts = [ref[:, first + c].reshape(rows, LANES) for c in range(count)]
    return parts[0] if count == 1 else jnp.concatenate(parts, 1)


def to_tiles(ref, first, value):
    rows, columns = value.shape
    for c in range(columns // LANES):
        part = value[:, c * LANES : (c + 1) * LANES].astype(BF)
        ref[:, first + c] = part.reshape(rows // TILE, TILE, LANES)


def row_chunks(kind):
    return {0: 3 * D // LANES, 1: D // LANES, 2: FF // LANES}[kind]


def each_tile(kinds, body):
    def span(kind, start, rows):
        step = row_chunks(kind)
        block = TILE * step

        def one(index, carry):
            base = start + index * block
            for c in range(step):
                body(base // TILE + c, base + c, step)
            return carry

        lax.fori_loop(0, rows // block, one, 0)

    @pl.when(kinds[0] == 0)
    def _():
        span(0, 0, 3072)

    for part in range(3):
        for kind in (1, 2):

            @pl.when(kinds[part] == kind)
            def _():
                span(kind, part * 1024, 1024)


def pack_kernel(kinds, flat_ref, tiles_ref):
    def body(tile, row, step):
        tiles_ref[tile] = flat_ref[pl.ds(row, TILE, stride=step), :].astype(BF)

    each_tile(kinds, body)


def unpack_kernel(kinds, tiles_ref, flat_ref):
    def body(tile, row, step):
        flat_ref[pl.ds(row, TILE, stride=step), :] = tiles_ref[tile].astype(F32)

    each_tile(kinds, body)


def shard_kinds(index):
    start = index * 3072 + jnp.arange(3, dtype=jnp.int32) * 1024
    qkv_end = 3 * D * D // LANES
    out_end = qkv_end + D * D // LANES
    up_end = out_end + D * FF // LANES
    return jnp.where(
        start < qkv_end, 0, jnp.where((start < out_end) | (start >= up_end), 1, 2)
    ).astype(jnp.int32)


def pack_shard(kinds, flat):
    return pl.pallas_call(
        pack_kernel,
        out_shape=jax.ShapeDtypeStruct((192, TILE, LANES), BF),
        in_specs=[pl.BlockSpec(memory_space=pltpu.SMEM), pl.BlockSpec(memory_space=pltpu.VMEM)],
        out_specs=pl.BlockSpec(memory_space=pltpu.VMEM),
        compiler_params=params_of(),
        cost_estimate=cost(0, 3 << 20),
        name="pack_shard",
    )(kinds, flat)


def unpack_shard(kinds, tiles):
    return pl.pallas_call(
        unpack_kernel,
        out_shape=jax.ShapeDtypeStruct((3072, LANES), F32),
        in_specs=[pl.BlockSpec(memory_space=pltpu.SMEM), pl.BlockSpec(memory_space=pltpu.VMEM)],
        out_specs=pl.BlockSpec(memory_space=pltpu.VMEM),
        compiler_params=params_of(),
        cost_estimate=cost(0, 3 << 20),
        name="unpack_shard",
    )(kinds, tiles)


def centre(field):
    average = jnp.mean(field, -1, keepdims=True)
    centred = field - average
    spread = jnp.mean(centred * centred, -1, keepdims=True)
    inverse = lax.rsqrt(spread + EPS)
    return centred * inverse, inverse


def norm_back(zhat, inverse, grad, gain):
    scaled = grad * gain
    mean_one = jnp.mean(scaled, -1, keepdims=True)
    mean_two = jnp.mean(scaled * zhat, -1, keepdims=True)
    return inverse * (scaled - mean_one - zhat * mean_two)


def qkv_kernel(x_ref, mod_ref, w_ref, low_ref, qkv_ref):
    @pl.when(pl.program_id(0) == 0)
    def _():
        zhat, _ = centre(x_ref[...].astype(F32))
        low_ref[...] = (zhat * mod_ref[0:1, :] + mod_ref[1:2, :]).astype(BF)

    weights = from_tiles(w_ref, 0, w_ref.shape[1])
    qkv_ref[...] = dot_nn(low_ref[...], weights).astype(BF)


def project_qkv(x, mod, tiles):
    chunks = 4
    width = chunks * LANES
    return pl.pallas_call(
        qkv_kernel,
        grid=(3 * D // width,),
        out_shape=(
            jax.ShapeDtypeStruct((1024, D), BF),
            jax.ShapeDtypeStruct((1024, 3 * D), BF),
        ),
        in_specs=[
            pl.BlockSpec((1024, D), lambda j: (0, 0)),
            pl.BlockSpec((4, D), lambda j: (0, 0)),
            pl.BlockSpec((64, chunks, TILE, LANES), lambda j: (0, j, 0, 0)),
        ],
        out_specs=(
            pl.BlockSpec((1024, D), lambda j: (0, 0)),
            pl.BlockSpec((1024, width), lambda j: (0, j)),
        ),
        compiler_params=params_of("arbitrary"),
        cost_estimate=cost(6.4e9, 18e6),
        name="project_qkv",
    )(x, mod, tiles.reshape(-1, 24, TILE, LANES))


def head_lanes(head):
    lane = lax.broadcasted_iota(jnp.int32, (1, LANES), 1)
    return (lane >= 64) if head else (lane < 64)


def with_bias(keys, head, bias):
    lane = lax.broadcasted_iota(jnp.int32, (1, LANES), 1)
    rest = jnp.where(lane == 64 * (1 - head), bias, jnp.zeros((), BF))
    return jnp.where(head_lanes(head), keys, rest)


def with_one(queries, head):
    lane = lax.broadcasted_iota(jnp.int32, (1, LANES), 1)
    rest = jnp.where(lane == 64 * (1 - head), 1.0, 0.0).astype(BF)
    return jnp.where(head_lanes(head), queries * jnp.asarray(0.125, BF), rest)


def key_bias(len_ref, frames):
    row = lax.broadcasted_iota(jnp.int32, (frames, 1), 0)
    return jnp.where(row < len_ref[0], 0.0, -1e30).astype(BF)


def paired_blocks(body, frames, rows):
    def pair(index, carry):
        body(index * 2 * rows)
        body(index * 2 * rows + rows)
        return carry

    lax.fori_loop(0, frames // (2 * rows), pair, 0)


def attend_kernel(len_ref, q_ref, k_ref, v_ref, out_ref, total_ref):
    rows = 256
    frames = k_ref.shape[0]
    bias = key_bias(len_ref, frames)
    zero = jnp.zeros((), BF)
    keys = [with_bias(k_ref[...], h, bias) for h in range(2)]

    def one_block(offset):
        here = pl.ds(pl.multiple_of(offset, rows), rows)
        mixed = []
        for h in range(2):
            scores = dot_nt(with_one(q_ref[here, :], h), keys[h])
            largest = jnp.max(scores, -1, keepdims=True)
            weights = jnp.exp(scores - largest)
            total = jnp.sum(weights, -1, keepdims=True)
            mixed.append(dot_nn(weights.astype(BF), v_ref[...]) * (1.0 / total))
            wide = jnp.broadcast_to(largest + jnp.log(total), (rows, LANES))
            total_ref[0, h : h + 1, here] = wide.T[0:1, :]
        out_ref[here, :] = jnp.where(head_lanes(0), mixed[0], mixed[1]).astype(BF)

    paired_blocks(one_block, frames, rows)


def attend(key_len, qkv):
    pairs = HEADS // 2
    return pl.pallas_call(
        attend_kernel,
        grid=(pairs,),
        out_shape=(
            jax.ShapeDtypeStruct((1024, D), BF),
            jax.ShapeDtypeStruct((pairs, 2, 1024), F32),
        ),
        in_specs=[
            pl.BlockSpec(memory_space=pltpu.SMEM),
            pl.BlockSpec((1024, LANES), lambda j: (0, j)),
            pl.BlockSpec((1024, LANES), lambda j: (0, pairs + j)),
            pl.BlockSpec((1024, LANES), lambda j: (0, 2 * pairs + j)),
        ],
        out_specs=(
            pl.BlockSpec((1024, LANES), lambda j: (0, j)),
            pl.BlockSpec((1, 2, 1024), lambda j: (j, 0, 0)),
        ),
        compiler_params=params_of("arbitrary"),
        cost_estimate=cost(17e9, 8e6, 16e6),
        name="attend",
    )(key_len, qkv, qkv, qkv)


def attend_back_kernel(
    len_ref, q_ref, k_ref, v_ref, do_ref, mix_ref, total_ref,
    dq_ref, dk_ref, dv_ref, dk_acc, dv_acc,
):
    rows = 256
    frames = k_ref.shape[0]
    bias = key_bias(len_ref, frames)
    values = v_ref[...]
    zero = jnp.zeros((), BF)
    keys = [with_bias(k_ref[...], h, bias) for h in range(2)]
    masked_keys = [jnp.where(head_lanes(h), k_ref[...], zero) for h in range(2)]
    dk_acc[...] = jnp.zeros_like(dk_acc)
    dv_acc[...] = jnp.zeros_like(dv_acc)

    def one_block(offset):
        here = pl.ds(pl.multiple_of(offset, rows), rows)
        queries = q_ref[here, :]
        grads = do_ref[here, :]
        products = (grads.astype(F32) * mix_ref[here, :].astype(F32)).T
        total = None
        for h in range(2):
            masked_q = jnp.where(head_lanes(h), queries * jnp.asarray(0.125, BF), zero)
            masked_g = jnp.where(head_lanes(h), grads, zero)
            inner = jnp.sum(products[64 * h : 64 * h + 64, :], 0, keepdims=True)
            scores = dot_nt(keys[h], with_one(queries, h))
            weights = jnp.exp(scores - total_ref[0, h : h + 1, here])
            grad_w = dot_nt(values, masked_g)
            back = (weights * (grad_w - inner)).astype(BF)
            dv_acc[...] += dot_nn(weights.astype(BF), masked_g)
            dk_acc[...] += dot_nn(back, masked_q)
            part_q = dot_tn(back, masked_keys[h])
            total = part_q if total is None else total + part_q
        dq_ref[here, :] = (total * 0.125).astype(BF)

    paired_blocks(one_block, frames, rows)
    dk_ref[...] = dk_acc[...].astype(BF)
    dv_ref[...] = dv_acc[...].astype(BF)


def attend_back(key_len, qkv, grad_mix, mixture, totals, first, count, earlier, waits=()):
    pairs = HEADS // 2
    block = lambda shift: pl.BlockSpec((1024, LANES), lambda j: (0, shift + first + j))
    kept = () if earlier is None else tuple(earlier)
    return pl.pallas_call(
        without(attend_back_kernel, 7, len(kept) + len(waits)),
        grid=(count,),
        out_shape=(jax.ShapeDtypeStruct((1024, D), BF),) * 3,
        in_specs=[
            pl.BlockSpec(memory_space=pltpu.SMEM),
            block(0),
            block(pairs),
            block(2 * pairs),
            block(0),
            block(0),
            pl.BlockSpec((1, 2, 1024), lambda j: (first + j, 0, 0)),
        ]
        + [ANYWHERE] * (len(kept) + len(waits)),
        out_specs=(block(0),) * 3,
        input_output_aliases={7 + i: i for i in range(len(kept))},
        scratch_shapes=[pltpu.VMEM((1024, LANES), F32)] * 2,
        compiler_params=params_of("arbitrary"),
        cost_estimate=cost(11e9 * count, 2e6 * count, 4e6 * count),
        name="attend_back",
    )(key_len, qkv, qkv, qkv, grad_mix, mixture, totals, *kept, *waits)


def middle_kernel(x_ref, mod_ref, mix_ref, w_ref, mid_ref, low_ref):
    weights = from_tiles(w_ref, 0, w_ref.shape[1])
    middle = x_ref[...].astype(F32) + dot_nn(mix_ref[...], weights)
    mid_ref[...] = middle
    zhat, _ = centre(middle)
    low_ref[...] = (zhat * mod_ref[2:3, :] + mod_ref[3:4, :]).astype(BF)


def middle_rows(x, mod, mixture, tiles):
    rows = 256
    return pl.pallas_call(
        middle_kernel,
        grid=(1024 // rows,),
        out_shape=(jax.ShapeDtypeStruct((1024, D), F32), jax.ShapeDtypeStruct((1024, D), BF)),
        in_specs=[
            pl.BlockSpec((rows, D), lambda i: (i, 0)),
            pl.BlockSpec((4, D), lambda i: (0, 0)),
            pl.BlockSpec((rows, D), lambda i: (i, 0)),
            pl.BlockSpec((64, 8, TILE, LANES), lambda i: (3, 0, 0, 0)),
        ],
        out_specs=(
            pl.BlockSpec((rows, D), lambda i: (i, 0)),
            pl.BlockSpec((rows, D), lambda i: (i, 0)),
        ),
        compiler_params=params_of("arbitrary"),
        cost_estimate=cost(2.2e9, 12e6),
        name="middle_rows",
    )(x, mod, mixture, tiles.reshape(-1, 8, TILE, LANES))


def ffn_kernel(
    mid_ref, mod_ref, low_ref, dy_ref, up_ref, down_ref,
    out_ref, dmid_ref, low_dmid_ref, dmod_ref, grads_ref,
    y_acc, dh_acc, low_t, act_s, du_s, dup_s, ddown_s, sems,
):
    step = pl.program_id(0)
    frames = mid_ref.shape[0]
    rows = 256

    @pl.when(step == 0)
    def _():
        y_acc[...] = jnp.zeros_like(y_acc)
        dh_acc[...] = jnp.zeros_like(dh_acc)
        low_t[...] = low_ref[...].T

    up = from_tiles(up_ref, 0, up_ref.shape[1])
    down = from_tiles(down_ref, 0, down_ref.shape[1])
    for offset in range(0, frames, rows):
        here = slice(offset, offset + rows)
        hidden = dot_nn(low_ref[here, :], up)
        grad_act = dot_nt(dy_ref[here, :], down)
        square = hidden * hidden
        inner = GELU_C * (hidden + GELU_A * (square * hidden))
        bend = jnp.tanh(inner)
        half = 0.5 * (1.0 + bend)
        act = (hidden * half).astype(BF)
        slope = half + 0.5 * hidden * (1.0 - bend * bend) * (
            GELU_C * (1.0 + 3.0 * GELU_A * square)
        )
        grad_hidden = (grad_act * slope).astype(BF)
        act_s[here, :] = act
        du_s[here, :] = grad_hidden
        y_acc[here, :] += dot_nn(act, down)
        dh_acc[here, :] += dot_nt(grad_hidden, up)
    slot = step % 2

    def copies(which, index):
        return (
            pltpu.make_async_copy(
                ddown_s.at[which], grads_ref.at[pl.ds(80 + index * 8, 8)], sems.at[which, 0]
            ),
            pltpu.make_async_copy(
                dup_s.at[which],
                grads_ref.at[pl.ds(16, 64), pl.ds(index * 4, 4)],
                sems.at[which, 1],
            ),
        )

    @pl.when(step >= 2)
    def _():
        for copy in copies(slot, step - 2):
            copy.wait()

    grad_down = dot_tn(act_s[...], dy_ref[...])
    for c in range(D // LANES):
        part = grad_down[:, c * LANES : (c + 1) * LANES].astype(BF).reshape(8, 4, TILE, LANES)
        for r in range(4):
            ddown_s[slot, :, r * 8 + c] = part[:, r]
    grad_up = dot_nn(low_t[...], du_s[...])
    for c in range(4):
        part = grad_up[:, c * LANES : (c + 1) * LANES].astype(BF)
        dup_s[slot, :, c] = part.reshape(64, TILE, LANES)
    for copy in copies(slot, step):
        copy.start()

    @pl.when(step == pl.num_programs(0) - 1)
    def _():
        for index in (step - 1, step):
            for copy in copies(index % 2, index):
                copy.wait()

    @pl.when(step == pl.num_programs(0) - 1)
    def _():
        dmod_ref[...] = jnp.zeros_like(dmod_ref)

        def finish(index, carry):
            here = pl.ds(pl.multiple_of(index * rows, rows), rows)
            middle = mid_ref[here, :]
            out_ref[here, :] = (middle + y_acc[here, :]).astype(BF)
            zhat, inverse = centre(middle)
            grad = dh_acc[here, :]
            dmod_ref[0:1, :] += jnp.sum(grad * zhat, 0, keepdims=True)
            dmod_ref[1:2, :] += jnp.sum(grad, 0, keepdims=True)
            grad_mid = dy_ref[here, :].astype(F32) + norm_back(zhat, inverse, grad, mod_ref[2:3, :])
            dmid_ref[here, :] = grad_mid
            low_dmid_ref[here, :] = grad_mid.astype(BF)
            return carry

        lax.fori_loop(0, frames // rows, finish, 0)


def ffn_both(middle, mod, low_two, dy, tiles):
    chunks = 4
    width = chunks * LANES
    steps = FF // width
    whole = lambda *shape: pl.BlockSpec(shape, lambda j: (0,) * len(shape))
    once = lambda *shape: pl.BlockSpec(
        shape, lambda j: (0,) * len(shape), pipeline_mode=pl.Buffered(1)
    )
    return pl.pallas_call(
        ffn_kernel,
        grid=(steps,),
        out_shape=(
            jax.ShapeDtypeStruct((1024, D), BF),
            jax.ShapeDtypeStruct((1024, D), F32),
            jax.ShapeDtypeStruct((1024, D), BF),
            jax.ShapeDtypeStruct((2, D), F32),
            jax.ShapeDtypeStruct((144, 32, TILE, LANES), BF),
        ),
        in_specs=[
            once(1024, D),
            whole(4, D),
            once(1024, D),
            once(1024, D),
            pl.BlockSpec((64, chunks, TILE, LANES), lambda j: (1, j, 0, 0)),
            pl.BlockSpec((width // TILE, 8, TILE, LANES), lambda j: (512 * TILE // width + j, 0, 0, 0)),
        ],
        out_specs=(
            once(1024, D),
            once(1024, D),
            once(1024, D),
            whole(2, D),
            pl.BlockSpec(memory_space=pl.ANY),
        ),
        scratch_shapes=[
            pltpu.VMEM((1024, D), F32),
            pltpu.VMEM((1024, D), F32),
            pltpu.VMEM((D, 1024), BF),
            pltpu.VMEM((1024, width), BF),
            pltpu.VMEM((1024, width), BF),
            pltpu.VMEM((2, 64, 4, TILE, LANES), BF),
            pltpu.VMEM((2, 8, 32, TILE, LANES), BF),
            pltpu.SemaphoreType.DMA((2, 2)),
        ],
        compiler_params=params_of("arbitrary"),
        cost_estimate=cost(52e9, 60e6, 4e6),
        name="ffn_both",
    )(
        middle, mod, low_two, dy,
        tiles.reshape(-1, 32, TILE, LANES), tiles.reshape(-1, 8, TILE, LANES),
    )


def out_back_kernel(mix_ref, dmid_ref, w_ref, grads_ref, dmix_ref, dw_ref):
    weights = from_tiles(w_ref, 0, w_ref.shape[1])
    dmix_ref[...] = dot_nt(dmid_ref[...], weights).astype(BF)
    to_tiles(dw_ref, 0, dot_tn(mix_ref[...], dmid_ref[...]))


def out_back(mixture, low_dmid, tiles, grads):
    width = 256
    return pl.pallas_call(
        out_back_kernel,
        grid=(D // width,),
        out_shape=(
            jax.ShapeDtypeStruct((1024, D), BF),
            jax.ShapeDtypeStruct((576, 8, TILE, LANES), BF),
        ),
        in_specs=[
            pl.BlockSpec((1024, width), lambda j: (0, j)),
            pl.BlockSpec((1024, D), lambda j: (0, 0)),
            pl.BlockSpec((width // TILE, 8, TILE, LANES), lambda j: (192 * TILE // width + j, 0, 0, 0)),
            pl.BlockSpec(memory_space=pl.ANY),
        ],
        input_output_aliases={3: 1},
        out_specs=(
            pl.BlockSpec((1024, width), lambda j: (0, j)),
            pl.BlockSpec((width // TILE, 8, TILE, LANES), lambda j: (j, 0, 0, 0)),
        ),
        compiler_params=params_of("arbitrary"),
        cost_estimate=cost(4.3e9, 10e6),
        name="out_back",
    )(mixture, low_dmid, tiles.reshape(-1, 8, TILE, LANES), grads.reshape(-1, 8, TILE, LANES))


def qkv_weight_kernel(low_ref, dq_ref, dk_ref, dv_ref, dw_ref):
    for third, grad_ref in enumerate((dq_ref, dk_ref, dv_ref)):
        to_tiles(dw_ref, third * 8, dot_tn(low_ref[...], grad_ref[...]))


def qkv_weight_grad(low_one, dq, dk, dv, waits=()):
    width = 256
    whole = pl.BlockSpec((1024, D), lambda j: (0, 0))
    return pl.pallas_call(
        without(qkv_weight_kernel, 4, len(waits)),
        grid=(D // width,),
        out_shape=jax.ShapeDtypeStruct((64, 24, TILE, LANES), BF),
        in_specs=[pl.BlockSpec((1024, width), lambda j: (0, j)), whole, whole, whole]
        + [ANYWHERE] * len(waits),
        out_specs=pl.BlockSpec((width // TILE, 24, TILE, LANES), lambda j: (j, 0, 0, 0)),
        compiler_params=params_of("arbitrary"),
        cost_estimate=cost(6.4e9, 15e6),
        name="qkv_weight_grad",
    )(low_one, dq, dk, dv, *waits)


def input_kernel(x_ref, mod_ref, dmid_ref, dq_ref, dk_ref, dv_ref, w_ref, grad_ref, dmod_ref):
    grad = None
    for third, part_ref in enumerate((dq_ref, dk_ref, dv_ref)):
        part = dot_nt(part_ref[...], from_tiles(w_ref, third * 8, 8))
        grad = part if grad is None else grad + part
    zhat, inverse = centre(x_ref[...].astype(F32))

    @pl.when(pl.program_id(0) == 0)
    def _():
        dmod_ref[...] = jnp.zeros_like(dmod_ref)

    dmod_ref[0:1, :] += jnp.sum(grad * zhat, 0, keepdims=True)
    dmod_ref[1:2, :] += jnp.sum(grad, 0, keepdims=True)
    grad_ref[...] = (dmid_ref[...] + norm_back(zhat, inverse, grad, mod_ref[0:1, :])).astype(BF)


def input_back(x, mod, dmid, dq, dk, dv, tiles, waits=()):
    rows = 256
    block = pl.BlockSpec((rows, D), lambda i: (i, 0))
    return pl.pallas_call(
        without(input_kernel, 7, len(waits)),
        grid=(1024 // rows,),
        out_shape=(jax.ShapeDtypeStruct((1024, D), BF), jax.ShapeDtypeStruct((2, D), F32)),
        in_specs=[
            block,
            pl.BlockSpec((4, D), lambda i: (0, 0)),
            block,
            block,
            block,
            block,
            pl.BlockSpec((64, 24, TILE, LANES), lambda i: (0, 0, 0, 0)),
        ]
        + [ANYWHERE] * len(waits),
        out_specs=(block, pl.BlockSpec((2, D), lambda i: (0, 0))),
        compiler_params=params_of("arbitrary"),
        cost_estimate=cost(6.4e9, 22e6),
        name="input_back",
    )(x, mod, dmid, dq, dk, dv, tiles.reshape(-1, 24, TILE, LANES), *waits)


def tile_spec(*lead, index):
    return pl.BlockSpec((*lead, TILE, LANES), lambda i, at: (*index(i, at), 0, 0))


def staged(kernel, name, outs, out_lead, ins, in_specs, sel, steps, moved, waits):
    spec = tile_spec(*out_lead, index=lambda i, at: (i,) + (0,) * (len(out_lead) - 1))
    shape = (steps,) + tuple(out_lead[1:]) + (TILE, LANES)
    return pl.pallas_call(
        without(kernel, 1 + len(ins), len(waits)),
        out_shape=(jax.ShapeDtypeStruct(shape, BF),) * outs,
        grid_spec=pltpu.PrefetchScalarGridSpec(
            num_scalar_prefetch=1,
            grid=(steps,),
            in_specs=in_specs + [ANYWHERE] * len(waits),
            out_specs=(spec,) * outs,
        ),
        compiler_params=params_of("arbitrary"),
        cost_estimate=cost(0, moved),
        name=name,
    )(sel, *ins, *waits)


def take_kernel(sel, value_ref, out_ref):
    out_ref[...] = value_ref[:, :, :, 0]


def take_other(sel, value, waits=()):
    layers = value.shape[0]
    spec = tile_spec(1, 2, 2, 1, 192, index=lambda i, at: (i, 0, 0, 1 - at[2], 0))
    return staged(
        take_kernel, "take_other", 1, (1, 2, 2, 192), [value], [spec], sel, layers, 6e6 * layers, waits
    )[0]


def both(left, right):
    return (left.astype(F32) + right.astype(F32)).astype(BF)


def core_kernel(sel, value_ref, moved_ref, one_send, one_keep, two_send, two_keep):
    y, x = sel[0], sel[1]
    one, two = slice(0, 96), slice(96, 192)
    for k in range(2):
        one_send[0, k] = both(value_ref[0, k, 1 - x, 0, one], moved_ref[0, k, 1 - x, one])
        one_keep[0, k] = both(value_ref[0, k, x, 0, one], moved_ref[0, k, x, one])
        two_send[0, k] = both(value_ref[0, 1 - y, k, 0, two], moved_ref[0, 1 - y, k, two])
        two_keep[0, k] = both(value_ref[0, y, k, 0, two], moved_ref[0, y, k, two])


def core_sum(sel, value, moved, waits=()):
    layers = value.shape[0]
    specs = [
        tile_spec(1, 2, 2, 1, 192, index=lambda i, at: (i, 0, 0, at[2], 0)),
        tile_spec(1, 2, 2, 192, index=lambda i, at: (i, 0, 0, 0)),
    ]
    return staged(
        core_kernel, "core_sum", 4, (1, 2, 96), [value, moved], specs, sel, layers, 9e6 * layers, waits
    )


def plane_kernel(sel, one_keep, one_moved, two_keep, two_moved, one_send, one_own, two_send, two_own):
    y, x = sel[0], sel[1]
    one_send[0] = both(one_keep[0, 1 - y], one_moved[0, 1 - y])
    one_own[0] = both(one_keep[0, y], one_moved[0, y])
    two_send[0] = both(two_keep[0, 1 - x], two_moved[0, 1 - x])
    two_own[0] = both(two_keep[0, x], two_moved[0, x])


def plane_sum(sel, *values, waits=()):
    layers = values[0].shape[0]
    spec = tile_spec(1, 2, 96, index=lambda i, at: (i, 0, 0))
    return staged(
        plane_kernel, "plane_sum", 4, (1, 96), values, [spec] * 4, sel, layers, 5e6 * layers, waits
    )


def line_kernel(sel, one_own, one_moved, two_own, two_moved, out_ref):
    out_ref[0, 0:96] = both(one_own[0], one_moved[0])
    out_ref[0, 96:192] = both(two_own[0], two_moved[0])


def line_sum(sel, *values, waits=()):
    layers = values[0].shape[0]
    spec = tile_spec(1, 96, index=lambda i, at: (i, 0))
    return staged(
        line_kernel, "line_sum", 1, (1, 192), values, [spec] * 4, sel, layers, 2.4e6 * layers, waits
    )[0]


def flat_index():
    return lax.axis_index(("dp", "fsdp"))


def exchange(value, mask, count):
    return lax.ppermute(value, ("dp", "fsdp"), [(i, i ^ mask) for i in range(count)])


def sum_everywhere(value, count):
    mask = 1
    while mask < count:
        value = value + exchange(value, mask, count)
        mask *= 2
    return value


def fast_device(tokens, key_len, section, params, first_moment, second_moment, cotangent):
    count = lax.axis_size(("dp", "fsdp"))
    index = flat_index()
    shard = params.shape[0]
    table_size = SECTIONS * 4 * D
    aligned = (count * shard - table_size) // count
    slip = table_size // count
    kinds = shard_kinds(index)
    x = tokens[0]
    dy = cotangent[0]

    before = lax.ppermute(
        params[shard - table_size :], ("dp", "fsdp"), [(i, i + 1) for i in range(count - 1)]
    )
    own = lax.dynamic_slice(
        jnp.concatenate([before, params]), (table_size - index * slip,), (aligned,)
    )
    packed = pack_shard(kinds, own.reshape(aligned // LANES, LANES))
    sel = jnp.stack([index // 4 % 2, index // 2 % 2, index % 2]).astype(jnp.int32)

    last = index == count - 1
    table = jnp.where(last, params[shard - table_size :], 0.0).astype(BF)
    table = sum_everywhere(table.reshape(SECTIONS, 4 * D), count)
    tiles = lax.all_gather(packed, ("dp", "fsdp"), axis=0, tiled=True)
    picker = (section[0] - 1 == jnp.arange(SECTIONS)).astype(F32)[:, None]
    mod = jnp.sum(picker * table.astype(F32), 0).reshape(4, D)

    low_one, qkv = project_qkv(x, mod, tiles)
    mixture, totals = attend(key_len, qkv)
    middle, low_two = middle_rows(x, mod, mixture, tiles)
    block_out, dmid, low_dmid, dmod_two, grads = ffn_both(middle, mod, low_two, dy, tiles)
    grad_mix, grads = out_back(mixture, low_dmid, tiles, grads)

    grads = grads.reshape(3, 2, 2, 2, 192, TILE, LANES)
    sent = take_other(sel, grads)
    moved = exchange(sent, 1, count)
    back = attend_back(key_len, qkv, grad_mix, mixture, totals, 0, 2, None, (sent,))
    one_send, one_keep, two_send, two_keep = core_sum(sel, grads, moved, back[:1])
    one_moved, two_moved = exchange(one_send, 2, count), exchange(two_send, 4, count)
    dq, dk, dv = attend_back(key_len, qkv, grad_mix, mixture, totals, 2, 6, back, (one_send,))
    grad_qkv = qkv_weight_grad(low_one, dq, dk, dv)
    grad_qkv = grad_qkv.reshape(1, 2, 2, 2, 192, TILE, LANES)
    one_send, one_keep, two_send, two_keep = plane_sum(
        sel, one_keep, one_moved, two_keep, two_moved, waits=(grad_qkv,)
    )
    one_moved, two_moved = exchange(one_send, 4, count), exchange(two_send, 2, count)
    held = (one_keep, one_moved, two_keep, two_moved)
    sent = take_other(sel, grad_qkv, (one_send,))
    moved = exchange(sent, 1, count)
    one_send, one_keep, two_send, two_keep = core_sum(sel, grad_qkv, moved)
    one_moved, two_moved = exchange(one_send, 2, count), exchange(two_send, 4, count)
    input_grad, dmod_one = input_back(x, mod, dmid, dq, dk, dv, tiles, (one_send,))
    rest = line_sum(sel, *held, waits=(input_grad,))
    one_send, one_keep, two_send, two_keep = plane_sum(
        sel, one_keep, one_moved, two_keep, two_moved, waits=(rest,)
    )
    one_moved, two_moved = exchange(one_send, 4, count), exchange(two_send, 2, count)
    first = line_sum(sel, one_keep, one_moved, two_keep, two_moved)

    per_item = jnp.concatenate([dmod_one, dmod_two], 0).reshape(1, 4 * D)
    section_grad = sum_everywhere(picker * per_item, count)

    reduced = jnp.where(
        index // 8 == 0, reduce_first(first[0], count), reduce_rest(rest, index, count)
    ).reshape(192, TILE, LANES)
    summed = unpack_shard(kinds, reduced).reshape(aligned)
    following = lax.ppermute(
        summed[:table_size], ("dp", "fsdp"), [(i, i - 1) for i in range(1, count)]
    )
    following = jnp.where(last, section_grad.reshape(table_size), following)
    param_grad = lax.dynamic_slice(jnp.concatenate([summed, following]), (index * slip,), (shard,))
    new_first = beta_one * first_moment + (1.0 - beta_one) * param_grad
    new_second = beta_two * second_moment + (1.0 - beta_two) * param_grad * param_grad
    new_params = params - learn_rate * (new_first / bias_one) / (
        jnp.sqrt(new_second / bias_two) + adam_eps
    )
    return (
        block_out[None],
        input_grad[None],
        param_grad,
        new_params,
        new_first,
        new_second,
        section_grad,
    )


def add_low(*terms):
    return add_wide(*terms).astype(BF)


def add_wide(*terms):
    total = terms[0].astype(F32)
    for term in terms[1:]:
        total = total + term.astype(F32)
    return total


def layer_move(value, moves):
    pairs = [(8 * a + i, 8 * b + i) for a, b in moves for i in range(8)]
    return lax.ppermute(value, ("dp", "fsdp"), pairs)


def pick(value, index, axis):
    return lax.dynamic_index_in_dim(value, index, axis, keepdims=False)


def reduce_first(value, count):
    value = add_low(value, layer_move(value, [(3, 2), (1, 0)]))
    return add_wide(value, layer_move(value, [(2, 0)]))


def reduce_rest(value, index, count):
    layer = index // 8
    choose = lambda at: pick(value, jnp.clip(at, 0, 2), 0)
    up = layer_move(value[2], [(0, 1)])
    down = layer_move(value[0], [(3, 2)])
    up = layer_move(add_low(choose(1 + layer), up), [(0, 1), (1, 2)])
    down = layer_move(add_low(choose(layer - 2), down), [(3, 2), (2, 1)])
    up = layer_move(add_low(choose(layer), up), [(0, 1), (1, 2), (2, 3)])
    return add_wide(choose(layer - 1), up, down)


def solution(mesh):
    in_specs = (
        P(("dp", "fsdp"), None, None),
        P(("dp", "fsdp")),
        P(("dp", "fsdp")),
        P(("dp", "fsdp")),
        P(("dp", "fsdp")),
        P(("dp", "fsdp")),
        P(("dp", "fsdp"), None, None),
    )
    out_specs = (
        P(("dp", "fsdp"), None, None),
        P(("dp", "fsdp"), None, None),
        P(("dp", "fsdp")),
        P(("dp", "fsdp")),
        P(("dp", "fsdp")),
        P(("dp", "fsdp")),
        P(),
    )
    fast = dict(mesh.shape) == {"dp": 8, "fsdp": 4}
    return jax.shard_map(
        fast_device if fast else per_device, mesh=mesh, in_specs=in_specs, out_specs=out_specs, check_vma=False
    )
```

```python
import jax
import jax.numpy as jnp
from jax import lax
from jax.experimental import pallas as pl
from jax.experimental.pallas import tpu as pltpu
from jax.sharding import PartitionSpec as P

D = 1024
HEADS = 16
FF = 4096
SECTIONS = 7


beta_one = 0.9
beta_two = 0.95
adam_eps = 1e-08
learn_rate = 0.05
bias_one = 1.0 - 0.9**10
bias_two = 1.0 - 0.95**10


def adanorm(field, gain_rows, shift_rows):
    average = jnp.mean(field, -1, keepdims=True)
    centred = field - average
    spread = jnp.mean(centred * centred, -1, keepdims=True)
    return centred * lax.rsqrt(spread + 1e-05) * gain_rows + shift_rows


def unpack(flat):
    first = 3 * D * D
    second = first + D * D
    third = second + D * FF
    fourth = third + FF * D
    return (
        flat[:first].reshape(D, 3 * D),
        flat[first:second].reshape(D, D),
        flat[second:third].reshape(D, FF),
        flat[third:fourth].reshape(FF, D),
        flat[fourth:].reshape(SECTIONS, 4 * D),
    )


def dot_trans(left, right):
    return lax.dot_general(
        left, right, (((1,), (1,)), ((), ())), preferred_element_type=jnp.float32
    )


def dot_inner(left, right):
    return lax.dot_general(
        left, right, (((0,), (0,)), ((), ())), preferred_element_type=jnp.float32
    )


def masked_scores(query_block, keys_all, key_valid, score_scale):
    scores = (
        jnp.einsum("qhd,khd->hqk", query_block, keys_all, preferred_element_type=jnp.float32)
        * score_scale
    )
    return jnp.where(key_valid, scores, -1e30)


def attend_forward(operands):
    queries, keys_all, values, valid_count = operands
    frames = queries.shape[0]
    block_rows = min(512, frames)
    score_scale = queries.shape[2] ** (-0.5)
    key_valid = (jnp.arange(frames) < valid_count)[None, None, :]
    outputs = []
    totals = []
    for offset in range(0, frames, block_rows):
        scores = masked_scores(
            queries[offset : offset + block_rows], keys_all, key_valid, score_scale
        )
        row_max = jnp.max(scores, -1, keepdims=True)
        log_total = row_max + jnp.log(jnp.sum(jnp.exp(scores - row_max), -1, keepdims=True))
        softmax_w = jnp.exp(scores - log_total).astype(jnp.bfloat16)
        outputs.append(
            jnp.einsum(
                "hqk,khd->qhd", softmax_w, values, preferred_element_type=jnp.float32
            ).astype(jnp.bfloat16)
        )
        totals.append(log_total[..., 0])
    return (jnp.concatenate(outputs, 0), jnp.concatenate(totals, 1))


def attend_backward(operands):
    queries, keys_all, values, valid_count, log_totals, grad_mix = operands
    frames = queries.shape[0]
    block_rows = min(512, frames)
    score_scale = queries.shape[2] ** (-0.5)
    key_valid = (jnp.arange(frames) < valid_count)[None, None, :]
    grad_keys = jnp.zeros(keys_all.shape, jnp.float32)
    grad_values = jnp.zeros(values.shape, jnp.float32)
    grad_queries = []
    for offset in range(0, frames, block_rows):
        query_block = queries[offset : offset + block_rows]
        grad_block = grad_mix[offset : offset + block_rows]
        scores = masked_scores(query_block, keys_all, key_valid, score_scale)
        softmax_w = jnp.exp(scores - log_totals[:, offset : offset + block_rows, None])
        grad_probs = jnp.einsum(
            "qhd,khd->hqk", grad_block, values, preferred_element_type=jnp.float32
        )
        grad_values = grad_values + jnp.einsum(
            "hqk,qhd->khd",
            softmax_w.astype(jnp.bfloat16),
            grad_block,
            preferred_element_type=jnp.float32,
        )
        grad_scores = (
            softmax_w * (grad_probs - jnp.sum(softmax_w * grad_probs, -1, keepdims=True))
        ).astype(jnp.bfloat16)
        grad_queries.append(
            jnp.einsum("hqk,khd->qhd", grad_scores, keys_all, preferred_element_type=jnp.float32)
            * score_scale
        )
        grad_keys = (
            grad_keys
            + jnp.einsum(
                "hqk,qhd->khd", grad_scores, query_block, preferred_element_type=jnp.float32
            )
            * score_scale
        )
    return jnp.stack([jnp.concatenate(grad_queries, 0), grad_keys, grad_values], 1).astype(
        jnp.bfloat16
    )


def per_device(tokens, key_len, section, params, first_moment, second_moment, cotangent):
    item_count, frames, features = tokens.shape
    row_count = item_count * frames
    head_size = features // HEADS
    low_params = params.astype(jnp.bfloat16)
    gathered = lax.all_gather(low_params, ("dp", "fsdp"), axis=0, tiled=True)
    w_qkv, w_out, w_up, w_down, table = unpack(gathered)
    picker = (section[:, None] - 1 == jnp.arange(SECTIONS)[None, :]).astype(jnp.float32)
    modulation = jnp.dot(picker, table.astype(jnp.float32), precision=lax.Precision.HIGHEST)
    gain_one = modulation[:, None, 0:features]
    shift_one = modulation[:, None, features : 2 * features]
    gain_two = modulation[:, None, 2 * features : 3 * features]
    shift_two = modulation[:, None, 3 * features : 4 * features]
    inputs = tokens.astype(jnp.float32)
    normed_one, norm_one_back = jax.vjp(adanorm, inputs, gain_one, shift_one)
    low_one = normed_one.astype(jnp.bfloat16).reshape(row_count, features)
    qkv = jnp.dot(low_one, w_qkv, preferred_element_type=jnp.float32).astype(jnp.bfloat16)
    qkv = qkv.reshape(item_count, frames, 3, HEADS, head_size)
    queries = qkv[:, :, 0]
    keys_all = qkv[:, :, 1]
    values = qkv[:, :, 2]
    mixture, log_totals = lax.map(attend_forward, (queries, keys_all, values, key_len))
    mixture = mixture.reshape(row_count, features)
    attended = jnp.dot(mixture, w_out, preferred_element_type=jnp.float32)
    middle = inputs + attended.reshape(item_count, frames, features)
    normed_two, norm_two_back = jax.vjp(adanorm, middle, gain_two, shift_two)
    low_two = normed_two.astype(jnp.bfloat16).reshape(row_count, features)
    projected = jnp.dot(low_two, w_up, preferred_element_type=jnp.float32)
    activated, gelu_back = jax.vjp(jax.nn.gelu, projected)
    low_act = activated.astype(jnp.bfloat16)
    branch = jnp.dot(low_act, w_down, preferred_element_type=jnp.float32)
    block_out = (middle + branch.reshape(item_count, frames, features)).astype(jnp.bfloat16)
    regathered = lax.all_gather(low_params, ("dp", "fsdp"), axis=0, tiled=True)
    w_qkv, w_out, w_up, w_down, table = unpack(regathered)
    grad_y = cotangent.astype(jnp.float32)
    low_gy = cotangent.reshape(row_count, features)
    grad_down = dot_inner(low_act, low_gy)
    grad_act = dot_trans(low_gy, w_down)
    (grad_proj,) = gelu_back(grad_act)
    low_gp = grad_proj.astype(jnp.bfloat16)
    grad_up = dot_inner(low_two, low_gp)
    grad_norm_two = dot_trans(low_gp, w_up).reshape(item_count, frames, features)
    grad_mid_part, grad_gain_two, grad_shift_two = norm_two_back(grad_norm_two)
    grad_mid = grad_y + grad_mid_part
    low_gm = grad_mid.astype(jnp.bfloat16).reshape(row_count, features)
    grad_out_w = dot_inner(mixture, low_gm)
    grad_mix = (
        dot_trans(low_gm, w_out).astype(jnp.bfloat16).reshape(item_count, frames, HEADS, head_size)
    )
    grad_qkv = lax.map(attend_backward, (queries, keys_all, values, key_len, log_totals, grad_mix))
    grad_qkv = grad_qkv.reshape(row_count, 3 * features)
    grad_qkv_w = dot_inner(low_one, grad_qkv)
    grad_norm_one = dot_trans(grad_qkv, w_qkv).reshape(item_count, frames, features)
    grad_in_part, grad_gain_one, grad_shift_one = norm_one_back(grad_norm_one)
    input_grad = (grad_mid + grad_in_part).astype(jnp.bfloat16)
    per_item = jnp.concatenate(
        [grad_gain_one[:, 0], grad_shift_one[:, 0], grad_gain_two[:, 0], grad_shift_two[:, 0]], 1
    )
    grad_table = jnp.einsum("is,ic->sc", picker, per_item, precision=lax.Precision.HIGHEST)
    table_flat = grad_table.ravel()
    table_size = table_flat.shape[0]
    flat_grads = jnp.concatenate(
        [
            grad_qkv_w.ravel(),
            grad_out_w.ravel(),
            grad_up.ravel(),
            grad_down.ravel(),
            jnp.zeros((table_size,), jnp.float32),
        ]
    )
    table_start = flat_grads.shape[0] - table_size
    shard_size = params.shape[0]
    weight_part = lax.psum_scatter(
        lax.slice_in_dim(flat_grads, 0, lax.axis_size(("dp", "fsdp")) * shard_size, axis=0),
        ("dp", "fsdp"),
        scatter_dimension=0,
        tiled=True,
    )
    section_total = lax.psum(table_flat, ("dp", "fsdp"))
    padded = jnp.concatenate(
        [
            jnp.zeros((shard_size,), jnp.float32),
            section_total,
            jnp.zeros((shard_size,), jnp.float32),
        ]
    )
    slice_start = jnp.clip(
        lax.axis_index(("dp", "fsdp")) * shard_size - table_start + shard_size,
        0,
        table_size + shard_size,
    ).astype(jnp.int32)
    param_grad = weight_part + lax.dynamic_slice_in_dim(padded, slice_start, shard_size)
    section_grad = section_total.reshape(SECTIONS, 4 * features)
    new_first = beta_one * first_moment + (1.0 - beta_one) * param_grad
    new_second = beta_two * second_moment + (1.0 - beta_two) * param_grad * param_grad
    new_params = params - learn_rate * (new_first / bias_one) / (
        jnp.sqrt(new_second / bias_two) + adam_eps
    )
    return (block_out, input_grad, param_grad, new_params, new_first, new_second, section_grad)


LANES = 128
TILE = 16
EPS = 1e-05
VMEM_LIMIT = 62 * 1024 * 1024
GELU_C = 0.7978845608028654
GELU_A = 0.044715
BF = jnp.bfloat16
F32 = jnp.float32


def params_of(*semantics):
    return pltpu.CompilerParams(
        dimension_semantics=semantics or None, vmem_limit_bytes=VMEM_LIMIT
    )


def cost(flops, moved, transcendentals=0):
    return pl.CostEstimate(
        flops=int(flops), bytes_accessed=int(moved), transcendentals=int(transcendentals)
    )


ANYWHERE = pl.BlockSpec(memory_space=pl.ANY)


def without(kernel, first, count):
    def called(*refs):
        kernel(*refs[:first], *refs[first + count :])

    return called


def dot_nn(left, right):
    return lax.dot_general(left, right, (((1,), (0,)), ((), ())), preferred_element_type=F32)


def dot_nt(left, right):
    return lax.dot_general(left, right, (((1,), (1,)), ((), ())), preferred_element_type=F32)


def dot_tn(left, right):
    return lax.dot_general(left, right, (((0,), (0,)), ((), ())), preferred_element_type=F32)


def from_tiles(ref, first, count):
    rows = ref.shape[0] * TILE
    parts = [ref[:, first + c].reshape(rows, LANES) for c in range(count)]
    return parts[0] if count == 1 else jnp.concatenate(parts, 1)


def to_tiles(ref, first, value):
    rows, columns = value.shape
    for c in range(columns // LANES):
        part = value[:, c * LANES : (c + 1) * LANES].astype(BF)
        ref[:, first + c] = part.reshape(rows // TILE, TILE, LANES)


def row_chunks(kind):
    return {0: 3 * D // LANES, 1: D // LANES, 2: FF // LANES}[kind]


def each_tile(kinds, body):
    def span(kind, start, rows):
        step = row_chunks(kind)
        block = TILE * step

        def one(index, carry):
            base = start + index * block
            for c in range(step):
                body(base // TILE + c, base + c, step)
            return carry

        lax.fori_loop(0, rows // block, one, 0)

    @pl.when(kinds[0] == 0)
    def _():
        span(0, 0, 3072)

    def one_part(part, carry):
        for kind in (1, 2):

            @pl.when(kinds[part] == kind)
            def _():
                span(kind, part * 1024, 1024)

        return carry

    lax.fori_loop(0, 3, one_part, 0)


def pack_kernel(kinds, flat_ref, tiles_ref):
    def body(tile, row, step):
        tiles_ref[tile] = flat_ref[pl.ds(row, TILE, stride=step), :].astype(BF)

    each_tile(kinds, body)


def unpack_kernel(kinds, tiles_ref, flat_ref):
    def body(tile, row, step):
        flat_ref[pl.ds(row, TILE, stride=step), :] = tiles_ref[tile].astype(F32)

    each_tile(kinds, body)


def shard_kinds(index):
    start = index * 3072 + jnp.arange(3, dtype=jnp.int32) * 1024
    qkv_end = 3 * D * D // LANES
    out_end = qkv_end + D * D // LANES
    up_end = out_end + D * FF // LANES
    return jnp.where(
        start < qkv_end, 0, jnp.where((start < out_end) | (start >= up_end), 1, 2)
    ).astype(jnp.int32)


def pack_shard(kinds, flat):
    return pl.pallas_call(
        pack_kernel,
        out_shape=jax.ShapeDtypeStruct((192, TILE, LANES), BF),
        in_specs=[pl.BlockSpec(memory_space=pltpu.SMEM), pl.BlockSpec(memory_space=pltpu.VMEM)],
        out_specs=pl.BlockSpec(memory_space=pltpu.VMEM),
        compiler_params=params_of(),
        cost_estimate=cost(0, 3 << 20),
        name="pack_shard",
    )(kinds, flat)


def unpack_shard(kinds, tiles):
    return pl.pallas_call(
        unpack_kernel,
        out_shape=jax.ShapeDtypeStruct((3072, LANES), F32),
        in_specs=[pl.BlockSpec(memory_space=pltpu.SMEM), pl.BlockSpec(memory_space=pltpu.VMEM)],
        out_specs=pl.BlockSpec(memory_space=pltpu.VMEM),
        compiler_params=params_of(),
        cost_estimate=cost(0, 3 << 20),
        name="unpack_shard",
    )(kinds, tiles)


def centre(field):
    average = jnp.mean(field, -1, keepdims=True)
    centred = field - average
    spread = jnp.mean(centred * centred, -1, keepdims=True)
    inverse = lax.rsqrt(spread + EPS)
    return centred * inverse, inverse


def norm_back(zhat, inverse, grad, gain):
    scaled = grad * gain
    mean_one = jnp.mean(scaled, -1, keepdims=True)
    mean_two = jnp.mean(scaled * zhat, -1, keepdims=True)
    return inverse * (scaled - mean_one - zhat * mean_two)


def qkv_kernel(x_ref, mod_ref, w_ref, low_ref, qkv_ref):
    @pl.when(pl.program_id(0) == 0)
    def _():
        zhat, _ = centre(x_ref[...].astype(F32))
        low_ref[...] = (zhat * mod_ref[0:1, :] + mod_ref[1:2, :]).astype(BF)

    weights = from_tiles(w_ref, 0, w_ref.shape[1])
    qkv_ref[...] = dot_nn(low_ref[...], weights).astype(BF)


def project_qkv(x, mod, tiles):
    chunks = 4
    width = chunks * LANES
    return pl.pallas_call(
        qkv_kernel,
        grid=(3 * D // width,),
        out_shape=(
            jax.ShapeDtypeStruct((1024, D), BF),
            jax.ShapeDtypeStruct((1024, 3 * D), BF),
        ),
        in_specs=[
            pl.BlockSpec((1024, D), lambda j: (0, 0)),
            pl.BlockSpec((4, D), lambda j: (0, 0)),
            pl.BlockSpec((64, chunks, TILE, LANES), lambda j: (0, j, 0, 0)),
        ],
        out_specs=(
            pl.BlockSpec((1024, D), lambda j: (0, 0)),
            pl.BlockSpec((1024, width), lambda j: (0, j)),
        ),
        compiler_params=params_of("arbitrary"),
        cost_estimate=cost(6.4e9, 18e6),
        name="project_qkv",
    )(x, mod, tiles.reshape(-1, 24, TILE, LANES))


def head_lanes(head):
    lane = lax.broadcasted_iota(jnp.int32, (1, LANES), 1)
    return (lane >= 64) if head else (lane < 64)


def with_bias(keys, head, bias):
    lane = lax.broadcasted_iota(jnp.int32, (1, LANES), 1)
    rest = jnp.where(lane == 64 * (1 - head), bias, jnp.zeros((), BF))
    return jnp.where(head_lanes(head), keys, rest)


def with_one(queries, head):
    lane = lax.broadcasted_iota(jnp.int32, (1, LANES), 1)
    rest = jnp.where(lane == 64 * (1 - head), 1.0, 0.0).astype(BF)
    return jnp.where(head_lanes(head), queries * jnp.asarray(0.125, BF), rest)


def key_bias(len_ref, frames):
    row = lax.broadcasted_iota(jnp.int32, (frames, 1), 0)
    return jnp.where(row < len_ref[0], 0.0, -1e30).astype(BF)


def paired_blocks(body, frames, rows):
    def pair(index, carry):
        body(index * 2 * rows)
        body(index * 2 * rows + rows)
        return carry

    lax.fori_loop(0, frames // (2 * rows), pair, 0)


def attend_kernel(len_ref, q_ref, k_ref, v_ref, out_ref, total_ref):
    rows = 256
    frames = k_ref.shape[0]
    bias = key_bias(len_ref, frames)
    zero = jnp.zeros((), BF)
    keys = [with_bias(k_ref[...], h, bias) for h in range(2)]
    for offset in range(0, frames, rows):
        here = slice(offset, offset + rows)
        mixed = []
        for h in range(2):
            scores = dot_nt(with_one(q_ref[here, :], h), keys[h])
            largest = jnp.max(scores, -1, keepdims=True)
            weights = jnp.exp(scores - largest)
            total = jnp.sum(weights, -1, keepdims=True)
            mixed.append(dot_nn(weights.astype(BF), v_ref[...]) * (1.0 / total))
            wide = jnp.broadcast_to(largest + jnp.log(total), (rows, LANES))
            total_ref[0, h : h + 1, here] = wide.T[0:1, :]
        out_ref[here, :] = jnp.where(head_lanes(0), mixed[0], mixed[1]).astype(BF)


def attend(key_len, qkv):
    pairs = HEADS // 2
    return pl.pallas_call(
        attend_kernel,
        grid=(pairs,),
        out_shape=(
            jax.ShapeDtypeStruct((1024, D), BF),
            jax.ShapeDtypeStruct((pairs, 2, 1024), F32),
        ),
        in_specs=[
            pl.BlockSpec(memory_space=pltpu.SMEM),
            pl.BlockSpec((1024, LANES), lambda j: (0, j)),
            pl.BlockSpec((1024, LANES), lambda j: (0, pairs + j)),
            pl.BlockSpec((1024, LANES), lambda j: (0, 2 * pairs + j)),
        ],
        out_specs=(
            pl.BlockSpec((1024, LANES), lambda j: (0, j)),
            pl.BlockSpec((1, 2, 1024), lambda j: (j, 0, 0)),
        ),
        compiler_params=params_of("arbitrary"),
        cost_estimate=cost(17e9, 8e6, 16e6),
        name="attend",
    )(key_len, qkv, qkv, qkv)


def attend_back_kernel(
    len_ref, q_ref, k_ref, v_ref, do_ref, mix_ref, total_ref,
    dq_ref, dk_ref, dv_ref, dk_acc, dv_acc,
):
    rows = 256
    frames = k_ref.shape[0]
    bias = key_bias(len_ref, frames)
    values = v_ref[...]
    zero = jnp.zeros((), BF)
    keys = [with_bias(k_ref[...], h, bias) for h in range(2)]
    masked_keys = [jnp.where(head_lanes(h), k_ref[...], zero) for h in range(2)]
    dk_acc[...] = jnp.zeros_like(dk_acc)
    dv_acc[...] = jnp.zeros_like(dv_acc)

    def one_block(offset):
        here = pl.ds(pl.multiple_of(offset, rows), rows)
        queries = q_ref[here, :]
        grads = do_ref[here, :]
        products = (grads.astype(F32) * mix_ref[here, :].astype(F32)).T
        total = None
        for h in range(2):
            masked_q = jnp.where(head_lanes(h), queries * jnp.asarray(0.125, BF), zero)
            masked_g = jnp.where(head_lanes(h), grads, zero)
            inner = jnp.sum(products[64 * h : 64 * h + 64, :], 0, keepdims=True)
            scores = dot_nt(keys[h], with_one(queries, h))
            weights = jnp.exp(scores - total_ref[0, h : h + 1, here])
            grad_w = dot_nt(values, masked_g)
            back = (weights * (grad_w - inner)).astype(BF)
            dv_acc[...] += dot_nn(weights.astype(BF), masked_g)
            dk_acc[...] += dot_nn(back, masked_q)
            part_q = dot_tn(back, masked_keys[h])
            total = part_q if total is None else total + part_q
        dq_ref[here, :] = (total * 0.125).astype(BF)

    paired_blocks(one_block, frames, rows)
    dk_ref[...] = dk_acc[...].astype(BF)
    dv_ref[...] = dv_acc[...].astype(BF)


def attend_back(key_len, qkv, grad_mix, mixture, totals, first, count, earlier, waits=()):
    pairs = HEADS // 2
    block = lambda shift: pl.BlockSpec((1024, LANES), lambda j: (0, shift + first + j))
    kept = () if earlier is None else tuple(earlier)
    return pl.pallas_call(
        without(attend_back_kernel, 7, len(kept) + len(waits)),
        grid=(count,),
        out_shape=(jax.ShapeDtypeStruct((1024, D), BF),) * 3,
        in_specs=[
            pl.BlockSpec(memory_space=pltpu.SMEM),
            block(0),
            block(pairs),
            block(2 * pairs),
            block(0),
            block(0),
            pl.BlockSpec((1, 2, 1024), lambda j: (first + j, 0, 0)),
        ]
        + [ANYWHERE] * (len(kept) + len(waits)),
        out_specs=(block(0),) * 3,
        input_output_aliases={7 + i: i for i in range(len(kept))},
        scratch_shapes=[pltpu.VMEM((1024, LANES), F32)] * 2,
        compiler_params=params_of("arbitrary"),
        cost_estimate=cost(11e9 * count, 2e6 * count, 4e6 * count),
        name="attend_back",
    )(key_len, qkv, qkv, qkv, grad_mix, mixture, totals, *kept, *waits)


def middle_kernel(x_ref, mod_ref, mix_ref, w_ref, mid_ref, low_ref):
    weights = from_tiles(w_ref, 0, w_ref.shape[1])
    middle = x_ref[...].astype(F32) + dot_nn(mix_ref[...], weights)
    mid_ref[...] = middle
    zhat, _ = centre(middle)
    low_ref[...] = (zhat * mod_ref[2:3, :] + mod_ref[3:4, :]).astype(BF)


def middle_rows(x, mod, mixture, tiles):
    rows = 256
    return pl.pallas_call(
        middle_kernel,
        grid=(1024 // rows,),
        out_shape=(jax.ShapeDtypeStruct((1024, D), F32), jax.ShapeDtypeStruct((1024, D), BF)),
        in_specs=[
            pl.BlockSpec((rows, D), lambda i: (i, 0)),
            pl.BlockSpec((4, D), lambda i: (0, 0)),
            pl.BlockSpec((rows, D), lambda i: (i, 0)),
            pl.BlockSpec((64, 8, TILE, LANES), lambda i: (3, 0, 0, 0)),
        ],
        out_specs=(
            pl.BlockSpec((rows, D), lambda i: (i, 0)),
            pl.BlockSpec((rows, D), lambda i: (i, 0)),
        ),
        compiler_params=params_of("arbitrary"),
        cost_estimate=cost(2.2e9, 12e6),
        name="middle_rows",
    )(x, mod, mixture, tiles.reshape(-1, 8, TILE, LANES))


def ffn_kernel(
    mid_ref, mod_ref, low_ref, dy_ref, up_ref, down_ref,
    out_ref, dmid_ref, low_dmid_ref, dmod_ref, grads_ref,
    y_acc, dh_acc, low_t, act_s, du_s, dup_s, ddown_s, sems,
):
    step = pl.program_id(0)
    frames = mid_ref.shape[0]
    rows = 256

    @pl.when(step == 0)
    def _():
        y_acc[...] = jnp.zeros_like(y_acc)
        dh_acc[...] = jnp.zeros_like(dh_acc)
        low_t[...] = low_ref[...].T

    up = from_tiles(up_ref, 0, up_ref.shape[1])
    down = from_tiles(down_ref, 0, down_ref.shape[1])
    for offset in range(0, frames, rows):
        here = slice(offset, offset + rows)
        hidden = dot_nn(low_ref[here, :], up)
        grad_act = dot_nt(dy_ref[here, :], down)
        square = hidden * hidden
        inner = GELU_C * (hidden + GELU_A * (square * hidden))
        bend = jnp.tanh(inner)
        half = 0.5 * (1.0 + bend)
        act = (hidden * half).astype(BF)
        slope = half + 0.5 * hidden * (1.0 - bend * bend) * (
            GELU_C * (1.0 + 3.0 * GELU_A * square)
        )
        grad_hidden = (grad_act * slope).astype(BF)
        act_s[here, :] = act
        du_s[here, :] = grad_hidden
        y_acc[here, :] += dot_nn(act, down)
        dh_acc[here, :] += dot_nt(grad_hidden, up)
    slot = step % 2

    def copies(which, index):
        return (
            pltpu.make_async_copy(
                ddown_s.at[which], grads_ref.at[pl.ds(80 + index * 8, 8)], sems.at[which, 0]
            ),
            pltpu.make_async_copy(
                dup_s.at[which],
                grads_ref.at[pl.ds(16, 64), pl.ds(index * 4, 4)],
                sems.at[which, 1],
            ),
        )

    @pl.when(step >= 2)
    def _():
        for copy in copies(slot, step - 2):
            copy.wait()

    grad_down = dot_tn(act_s[...], dy_ref[...])
    for c in range(D // LANES):
        part = grad_down[:, c * LANES : (c + 1) * LANES].astype(BF).reshape(8, 4, TILE, LANES)
        for r in range(4):
            ddown_s[slot, :, r * 8 + c] = part[:, r]
    grad_up = dot_nn(low_t[...], du_s[...])
    for c in range(4):
        part = grad_up[:, c * LANES : (c + 1) * LANES].astype(BF)
        dup_s[slot, :, c] = part.reshape(64, TILE, LANES)
    for copy in copies(slot, step):
        copy.start()

    @pl.when(step == pl.num_programs(0) - 1)
    def _():
        for index in (step - 1, step):
            for copy in copies(index % 2, index):
                copy.wait()

    @pl.when(step == pl.num_programs(0) - 1)
    def _():
        dmod_ref[...] = jnp.zeros_like(dmod_ref)

        def finish(index, carry):
            here = pl.ds(pl.multiple_of(index * rows, rows), rows)
            middle = mid_ref[here, :]
            out_ref[here, :] = (middle + y_acc[here, :]).astype(BF)
            zhat, inverse = centre(middle)
            grad = dh_acc[here, :]
            dmod_ref[0:1, :] += jnp.sum(grad * zhat, 0, keepdims=True)
            dmod_ref[1:2, :] += jnp.sum(grad, 0, keepdims=True)
            grad_mid = dy_ref[here, :].astype(F32) + norm_back(zhat, inverse, grad, mod_ref[2:3, :])
            dmid_ref[here, :] = grad_mid
            low_dmid_ref[here, :] = grad_mid.astype(BF)
            return carry

        lax.fori_loop(0, frames // rows, finish, 0)


def ffn_both(middle, mod, low_two, dy, tiles):
    chunks = 4
    width = chunks * LANES
    steps = FF // width
    whole = lambda *shape: pl.BlockSpec(shape, lambda j: (0,) * len(shape))
    once = lambda *shape: pl.BlockSpec(
        shape, lambda j: (0,) * len(shape), pipeline_mode=pl.Buffered(1)
    )
    return pl.pallas_call(
        ffn_kernel,
        grid=(steps,),
        out_shape=(
            jax.ShapeDtypeStruct((1024, D), BF),
            jax.ShapeDtypeStruct((1024, D), F32),
            jax.ShapeDtypeStruct((1024, D), BF),
            jax.ShapeDtypeStruct((2, D), F32),
            jax.ShapeDtypeStruct((144, 32, TILE, LANES), BF),
        ),
        in_specs=[
            once(1024, D),
            whole(4, D),
            once(1024, D),
            once(1024, D),
            pl.BlockSpec((64, chunks, TILE, LANES), lambda j: (1, j, 0, 0)),
            pl.BlockSpec((width // TILE, 8, TILE, LANES), lambda j: (512 * TILE // width + j, 0, 0, 0)),
        ],
        out_specs=(
            once(1024, D),
            once(1024, D),
            once(1024, D),
            whole(2, D),
            pl.BlockSpec(memory_space=pl.ANY),
        ),
        scratch_shapes=[
            pltpu.VMEM((1024, D), F32),
            pltpu.VMEM((1024, D), F32),
            pltpu.VMEM((D, 1024), BF),
            pltpu.VMEM((1024, width), BF),
            pltpu.VMEM((1024, width), BF),
            pltpu.VMEM((2, 64, 4, TILE, LANES), BF),
            pltpu.VMEM((2, 8, 32, TILE, LANES), BF),
            pltpu.SemaphoreType.DMA((2, 2)),
        ],
        compiler_params=params_of("arbitrary"),
        cost_estimate=cost(52e9, 60e6, 4e6),
        name="ffn_both",
    )(
        middle, mod, low_two, dy,
        tiles.reshape(-1, 32, TILE, LANES), tiles.reshape(-1, 8, TILE, LANES),
    )


def out_back_kernel(mix_ref, dmid_ref, w_ref, grads_ref, dmix_ref, dw_ref):
    weights = from_tiles(w_ref, 0, w_ref.shape[1])
    dmix_ref[...] = dot_nt(dmid_ref[...], weights).astype(BF)
    to_tiles(dw_ref, 0, dot_tn(mix_ref[...], dmid_ref[...]))


def out_back(mixture, low_dmid, tiles, grads):
    width = 256
    return pl.pallas_call(
        out_back_kernel,
        grid=(D // width,),
        out_shape=(
            jax.ShapeDtypeStruct((1024, D), BF),
            jax.ShapeDtypeStruct((576, 8, TILE, LANES), BF),
        ),
        in_specs=[
            pl.BlockSpec((1024, width), lambda j: (0, j)),
            pl.BlockSpec((1024, D), lambda j: (0, 0)),
            pl.BlockSpec((width // TILE, 8, TILE, LANES), lambda j: (192 * TILE // width + j, 0, 0, 0)),
            pl.BlockSpec(memory_space=pl.ANY),
        ],
        input_output_aliases={3: 1},
        out_specs=(
            pl.BlockSpec((1024, width), lambda j: (0, j)),
            pl.BlockSpec((width // TILE, 8, TILE, LANES), lambda j: (j, 0, 0, 0)),
        ),
        compiler_params=params_of("arbitrary"),
        cost_estimate=cost(4.3e9, 10e6),
        name="out_back",
    )(mixture, low_dmid, tiles.reshape(-1, 8, TILE, LANES), grads.reshape(-1, 8, TILE, LANES))


def qkv_weight_kernel(low_ref, dq_ref, dk_ref, dv_ref, dw_ref):
    for third, grad_ref in enumerate((dq_ref, dk_ref, dv_ref)):
        to_tiles(dw_ref, third * 8, dot_tn(low_ref[...], grad_ref[...]))


def qkv_weight_grad(low_one, dq, dk, dv, waits=()):
    width = 256
    whole = pl.BlockSpec((1024, D), lambda j: (0, 0))
    return pl.pallas_call(
        without(qkv_weight_kernel, 4, len(waits)),
        grid=(D // width,),
        out_shape=jax.ShapeDtypeStruct((64, 24, TILE, LANES), BF),
        in_specs=[pl.BlockSpec((1024, width), lambda j: (0, j)), whole, whole, whole]
        + [ANYWHERE] * len(waits),
        out_specs=pl.BlockSpec((width // TILE, 24, TILE, LANES), lambda j: (j, 0, 0, 0)),
        compiler_params=params_of("arbitrary"),
        cost_estimate=cost(6.4e9, 15e6),
        name="qkv_weight_grad",
    )(low_one, dq, dk, dv, *waits)


def input_kernel(x_ref, mod_ref, dmid_ref, dq_ref, dk_ref, dv_ref, w_ref, grad_ref, dmod_ref):
    grad = None
    for third, part_ref in enumerate((dq_ref, dk_ref, dv_ref)):
        part = dot_nt(part_ref[...], from_tiles(w_ref, third * 8, 8))
        grad = part if grad is None else grad + part
    zhat, inverse = centre(x_ref[...].astype(F32))

    @pl.when(pl.program_id(0) == 0)
    def _():
        dmod_ref[...] = jnp.zeros_like(dmod_ref)

    dmod_ref[0:1, :] += jnp.sum(grad * zhat, 0, keepdims=True)
    dmod_ref[1:2, :] += jnp.sum(grad, 0, keepdims=True)
    grad_ref[...] = (dmid_ref[...] + norm_back(zhat, inverse, grad, mod_ref[0:1, :])).astype(BF)


def input_back(x, mod, dmid, dq, dk, dv, tiles, waits=()):
    rows = 256
    block = pl.BlockSpec((rows, D), lambda i: (i, 0))
    return pl.pallas_call(
        without(input_kernel, 7, len(waits)),
        grid=(1024 // rows,),
        out_shape=(jax.ShapeDtypeStruct((1024, D), BF), jax.ShapeDtypeStruct((2, D), F32)),
        in_specs=[
            block,
            pl.BlockSpec((4, D), lambda i: (0, 0)),
            block,
            block,
            block,
            block,
            pl.BlockSpec((64, 24, TILE, LANES), lambda i: (0, 0, 0, 0)),
        ]
        + [ANYWHERE] * len(waits),
        out_specs=(block, pl.BlockSpec((2, D), lambda i: (0, 0))),
        compiler_params=params_of("arbitrary"),
        cost_estimate=cost(6.4e9, 22e6),
        name="input_back",
    )(x, mod, dmid, dq, dk, dv, tiles.reshape(-1, 24, TILE, LANES), *waits)


def tile_spec(*lead, index):
    return pl.BlockSpec((*lead, TILE, LANES), lambda i, at: (*index(i, at), 0, 0))


def staged(kernel, name, outs, out_lead, ins, in_specs, sel, steps, moved, waits):
    spec = tile_spec(*out_lead, index=lambda i, at: (i,) + (0,) * (len(out_lead) - 1))
    shape = (steps,) + tuple(out_lead[1:]) + (TILE, LANES)
    return pl.pallas_call(
        without(kernel, 1 + len(ins), len(waits)),
        out_shape=(jax.ShapeDtypeStruct(shape, BF),) * outs,
        grid_spec=pltpu.PrefetchScalarGridSpec(
            num_scalar_prefetch=1,
            grid=(steps,),
            in_specs=in_specs + [ANYWHERE] * len(waits),
            out_specs=(spec,) * outs,
        ),
        compiler_params=params_of("arbitrary"),
        cost_estimate=cost(0, moved),
        name=name,
    )(sel, *ins, *waits)


def take_kernel(sel, value_ref, out_ref):
    out_ref[...] = value_ref[:, :, 0]


def take_other(sel, value, waits=()):
    layers = value.shape[0]
    value = value.reshape(2 * layers, 2, 2, 192, TILE, LANES)
    spec = tile_spec(1, 2, 1, 192, index=lambda i, at: (i, 0, 1 - at[2], 0))
    sent = staged(
        take_kernel, "take_other", 1, (1, 2, 192), [value], [spec], sel, 2 * layers, 6e6, waits
    )[0]
    return sent.reshape(layers, 2, 2, 192, TILE, LANES)


def both(left, right):
    return (left.astype(F32) + right.astype(F32)).astype(BF)


def core_kernel(sel, value_ref, moved_ref, one_send, one_keep, two_send, two_keep):
    y, x = sel[0], sel[1]
    one, two = slice(0, 96), slice(96, 192)
    for k in range(2):
        one_send[0, k] = both(value_ref[0, k, 1 - x, 0, one], moved_ref[0, k, 1 - x, one])
        one_keep[0, k] = both(value_ref[0, k, x, 0, one], moved_ref[0, k, x, one])
        two_send[0, k] = both(value_ref[0, 1 - y, k, 0, two], moved_ref[0, 1 - y, k, two])
        two_keep[0, k] = both(value_ref[0, y, k, 0, two], moved_ref[0, y, k, two])


def core_sum(sel, value, moved, waits=()):
    layers = value.shape[0]
    specs = [
        tile_spec(1, 2, 2, 1, 192, index=lambda i, at: (i, 0, 0, at[2], 0)),
        tile_spec(1, 2, 2, 192, index=lambda i, at: (i, 0, 0, 0)),
    ]
    return staged(
        core_kernel, "core_sum", 4, (1, 2, 96), [value, moved], specs, sel, layers, 9e6 * layers, waits
    )


def plane_kernel(sel, one_keep, one_moved, two_keep, two_moved, one_send, one_own, two_send, two_own):
    y, x = sel[0], sel[1]
    one_send[0] = both(one_keep[0, 1 - y], one_moved[0, 1 - y])
    one_own[0] = both(one_keep[0, y], one_moved[0, y])
    two_send[0] = both(two_keep[0, 1 - x], two_moved[0, 1 - x])
    two_own[0] = both(two_keep[0, x], two_moved[0, x])


def plane_sum(sel, *values, waits=()):
    layers = values[0].shape[0]
    spec = tile_spec(1, 2, 96, index=lambda i, at: (i, 0, 0))
    return staged(
        plane_kernel, "plane_sum", 4, (1, 96), values, [spec] * 4, sel, layers, 5e6 * layers, waits
    )


def line_kernel(sel, one_own, one_moved, two_own, two_moved, out_ref):
    out_ref[0, 0:96] = both(one_own[0], one_moved[0])
    out_ref[0, 96:192] = both(two_own[0], two_moved[0])


def line_sum(sel, *values, waits=()):
    layers = values[0].shape[0]
    spec = tile_spec(1, 96, index=lambda i, at: (i, 0))
    return staged(
        line_kernel, "line_sum", 1, (1, 192), values, [spec] * 4, sel, layers, 2.4e6 * layers, waits
    )[0]


def flat_index():
    return lax.axis_index(("dp", "fsdp"))


def exchange(value, mask, count):
    return lax.ppermute(value, ("dp", "fsdp"), [(i, i ^ mask) for i in range(count)])


def sum_everywhere(value, count):
    mask = 1
    while mask < count:
        value = value + exchange(value, mask, count)
        mask *= 2
    return value


def fast_device(tokens, key_len, section, params, first_moment, second_moment, cotangent):
    count = lax.axis_size(("dp", "fsdp"))
    index = flat_index()
    shard = params.shape[0]
    table_size = SECTIONS * 4 * D
    aligned = (count * shard - table_size) // count
    slip = table_size // count
    kinds = shard_kinds(index)
    x = tokens[0]
    dy = cotangent[0]

    before = lax.ppermute(
        params[shard - table_size :], ("dp", "fsdp"), [(i, i + 1) for i in range(count - 1)]
    )
    own = lax.dynamic_slice(
        jnp.concatenate([before, params]), (table_size - index * slip,), (aligned,)
    )
    packed = pack_shard(kinds, own.reshape(aligned // LANES, LANES))
    sel = jnp.stack([index // 4 % 2, index // 2 % 2, index % 2]).astype(jnp.int32)

    last = index == count - 1
    table = jnp.where(last, params[shard - table_size :], 0.0).astype(BF)
    table = sum_everywhere(table.reshape(SECTIONS, 4 * D), count)
    tiles = lax.all_gather(packed, ("dp", "fsdp"), axis=0, tiled=True)
    picker = (section[0] - 1 == jnp.arange(SECTIONS)).astype(F32)[:, None]
    mod = jnp.sum(picker * table.astype(F32), 0).reshape(4, D)

    low_one, qkv = project_qkv(x, mod, tiles)
    mixture, totals = attend(key_len, qkv)
    middle, low_two = middle_rows(x, mod, mixture, tiles)
    block_out, dmid, low_dmid, dmod_two, grads = ffn_both(middle, mod, low_two, dy, tiles)
    grad_mix, grads = out_back(mixture, low_dmid, tiles, grads)

    grads = grads.reshape(3, 2, 2, 2, 192, TILE, LANES)
    sent = take_other(sel, grads)
    moved = exchange(sent, 1, count)
    back = attend_back(key_len, qkv, grad_mix, mixture, totals, 0, 2, None, (sent,))
    one_send, one_keep, two_send, two_keep = core_sum(sel, grads, moved, back[:1])
    one_moved, two_moved = exchange(one_send, 2, count), exchange(two_send, 4, count)
    dq, dk, dv = attend_back(key_len, qkv, grad_mix, mixture, totals, 2, 6, back, (one_send,))
    grad_qkv = qkv_weight_grad(low_one, dq, dk, dv)
    grad_qkv = grad_qkv.reshape(1, 2, 2, 2, 192, TILE, LANES)
    one_send, one_keep, two_send, two_keep = plane_sum(
        sel, one_keep, one_moved, two_keep, two_moved, waits=(grad_qkv,)
    )
    one_moved, two_moved = exchange(one_send, 4, count), exchange(two_send, 2, count)
    held = (one_keep, one_moved, two_keep, two_moved)
    sent = take_other(sel, grad_qkv, (one_send,))
    moved = exchange(sent, 1, count)
    one_send, one_keep, two_send, two_keep = core_sum(sel, grad_qkv, moved)
    one_moved, two_moved = exchange(one_send, 2, count), exchange(two_send, 4, count)
    input_grad, dmod_one = input_back(x, mod, dmid, dq, dk, dv, tiles, (one_send,))
    rest = line_sum(sel, *held, waits=(input_grad,))
    one_send, one_keep, two_send, two_keep = plane_sum(
        sel, one_keep, one_moved, two_keep, two_moved, waits=(rest,)
    )
    one_moved, two_moved = exchange(one_send, 4, count), exchange(two_send, 2, count)
    first = line_sum(sel, one_keep, one_moved, two_keep, two_moved)

    per_item = jnp.concatenate([dmod_one, dmod_two], 0).reshape(1, 4 * D)
    section_grad = sum_everywhere(picker * per_item, count)

    reduced = jnp.where(
        index // 8 == 0, reduce_first(first[0], count), reduce_rest(rest, index, count)
    ).reshape(192, TILE, LANES)
    summed = unpack_shard(kinds, reduced).reshape(aligned)
    following = lax.ppermute(
        summed[:table_size], ("dp", "fsdp"), [(i, i - 1) for i in range(1, count)]
    )
    following = jnp.where(last, section_grad.reshape(table_size), following)
    param_grad = lax.dynamic_slice(jnp.concatenate([summed, following]), (index * slip,), (shard,))
    new_first = beta_one * first_moment + (1.0 - beta_one) * param_grad
    new_second = beta_two * second_moment + (1.0 - beta_two) * param_grad * param_grad
    new_params = params - learn_rate * (new_first / bias_one) / (
        jnp.sqrt(new_second / bias_two) + adam_eps
    )
    return (
        block_out[None],
        input_grad[None],
        param_grad,
        new_params,
        new_first,
        new_second,
        section_grad,
    )


def add_low(*terms):
    return add_wide(*terms).astype(BF)


def add_wide(*terms):
    total = terms[0].astype(F32)
    for term in terms[1:]:
        total = total + term.astype(F32)
    return total


def layer_move(value, moves):
    pairs = [(8 * a + i, 8 * b + i) for a, b in moves for i in range(8)]
    return lax.ppermute(value, ("dp", "fsdp"), pairs)


def pick(value, index, axis):
    return lax.dynamic_index_in_dim(value, index, axis, keepdims=False)


def reduce_first(value, count):
    value = add_low(value, layer_move(value, [(3, 2), (1, 0)]))
    return add_wide(value, layer_move(value, [(2, 0)]))


def reduce_rest(value, index, count):
    layer = index // 8
    choose = lambda at: pick(value, jnp.clip(at, 0, 2), 0)
    up = layer_move(value[2], [(0, 1)])
    down = layer_move(value[0], [(3, 2)])
    up = layer_move(add_low(choose(1 + layer), up), [(0, 1), (1, 2)])
    down = layer_move(add_low(choose(layer - 2), down), [(3, 2), (2, 1)])
    up = layer_move(add_low(choose(layer), up), [(0, 1), (1, 2), (2, 3)])
    return add_wide(choose(layer - 1), up, down)


def solution(mesh):
    in_specs = (
        P(("dp", "fsdp"), None, None),
        P(("dp", "fsdp")),
        P(("dp", "fsdp")),
        P(("dp", "fsdp")),
        P(("dp", "fsdp")),
        P(("dp", "fsdp")),
        P(("dp", "fsdp"), None, None),
    )
    out_specs = (
        P(("dp", "fsdp"), None, None),
        P(("dp", "fsdp"), None, None),
        P(("dp", "fsdp")),
        P(("dp", "fsdp")),
        P(("dp", "fsdp")),
        P(("dp", "fsdp")),
        P(),
    )
    fast = dict(mesh.shape) == {"dp": 8, "fsdp": 4}
    return jax.shard_map(
        fast_device if fast else per_device, mesh=mesh, in_specs=in_specs, out_specs=out_specs, check_vma=False
    )
```

```python
import jax
import jax.numpy as jnp
from jax import lax
from jax.experimental import pallas as pl
from jax.experimental.pallas import tpu as pltpu
from jax.sharding import PartitionSpec as P

D = 1024
HEADS = 16
FF = 4096
SECTIONS = 7


beta_one = 0.9
beta_two = 0.95
adam_eps = 1e-08
learn_rate = 0.05
bias_one = 1.0 - 0.9**10
bias_two = 1.0 - 0.95**10


def adanorm(field, gain_rows, shift_rows):
    average = jnp.mean(field, -1, keepdims=True)
    centred = field - average
    spread = jnp.mean(centred * centred, -1, keepdims=True)
    return centred * lax.rsqrt(spread + 1e-05) * gain_rows + shift_rows


def unpack(flat):
    first = 3 * D * D
    second = first + D * D
    third = second + D * FF
    fourth = third + FF * D
    return (
        flat[:first].reshape(D, 3 * D),
        flat[first:second].reshape(D, D),
        flat[second:third].reshape(D, FF),
        flat[third:fourth].reshape(FF, D),
        flat[fourth:].reshape(SECTIONS, 4 * D),
    )


def dot_trans(left, right):
    return lax.dot_general(
        left, right, (((1,), (1,)), ((), ())), preferred_element_type=jnp.float32
    )


def dot_inner(left, right):
    return lax.dot_general(
        left, right, (((0,), (0,)), ((), ())), preferred_element_type=jnp.float32
    )


def masked_scores(query_block, keys_all, key_valid, score_scale):
    scores = (
        jnp.einsum("qhd,khd->hqk", query_block, keys_all, preferred_element_type=jnp.float32)
        * score_scale
    )
    return jnp.where(key_valid, scores, -1e30)


def attend_forward(operands):
    queries, keys_all, values, valid_count = operands
    frames = queries.shape[0]
    block_rows = min(512, frames)
    score_scale = queries.shape[2] ** (-0.5)
    key_valid = (jnp.arange(frames) < valid_count)[None, None, :]
    outputs = []
    totals = []
    for offset in range(0, frames, block_rows):
        scores = masked_scores(
            queries[offset : offset + block_rows], keys_all, key_valid, score_scale
        )
        row_max = jnp.max(scores, -1, keepdims=True)
        log_total = row_max + jnp.log(jnp.sum(jnp.exp(scores - row_max), -1, keepdims=True))
        softmax_w = jnp.exp(scores - log_total).astype(jnp.bfloat16)
        outputs.append(
            jnp.einsum(
                "hqk,khd->qhd", softmax_w, values, preferred_element_type=jnp.float32
            ).astype(jnp.bfloat16)
        )
        totals.append(log_total[..., 0])
    return (jnp.concatenate(outputs, 0), jnp.concatenate(totals, 1))


def attend_backward(operands):
    queries, keys_all, values, valid_count, log_totals, grad_mix = operands
    frames = queries.shape[0]
    block_rows = min(512, frames)
    score_scale = queries.shape[2] ** (-0.5)
    key_valid = (jnp.arange(frames) < valid_count)[None, None, :]
    grad_keys = jnp.zeros(keys_all.shape, jnp.float32)
    grad_values = jnp.zeros(values.shape, jnp.float32)
    grad_queries = []
    for offset in range(0, frames, block_rows):
        query_block = queries[offset : offset + block_rows]
        grad_block = grad_mix[offset : offset + block_rows]
        scores = masked_scores(query_block, keys_all, key_valid, score_scale)
        softmax_w = jnp.exp(scores - log_totals[:, offset : offset + block_rows, None])
        grad_probs = jnp.einsum(
            "qhd,khd->hqk", grad_block, values, preferred_element_type=jnp.float32
        )
        grad_values = grad_values + jnp.einsum(
            "hqk,qhd->khd",
            softmax_w.astype(jnp.bfloat16),
            grad_block,
            preferred_element_type=jnp.float32,
        )
        grad_scores = (
            softmax_w * (grad_probs - jnp.sum(softmax_w * grad_probs, -1, keepdims=True))
        ).astype(jnp.bfloat16)
        grad_queries.append(
            jnp.einsum("hqk,khd->qhd", grad_scores, keys_all, preferred_element_type=jnp.float32)
            * score_scale
        )
        grad_keys = (
            grad_keys
            + jnp.einsum(
                "hqk,qhd->khd", grad_scores, query_block, preferred_element_type=jnp.float32
            )
            * score_scale
        )
    return jnp.stack([jnp.concatenate(grad_queries, 0), grad_keys, grad_values], 1).astype(
        jnp.bfloat16
    )


def per_device(tokens, key_len, section, params, first_moment, second_moment, cotangent):
    item_count, frames, features = tokens.shape
    row_count = item_count * frames
    head_size = features // HEADS
    low_params = params.astype(jnp.bfloat16)
    gathered = lax.all_gather(low_params, ("dp", "fsdp"), axis=0, tiled=True)
    w_qkv, w_out, w_up, w_down, table = unpack(gathered)
    picker = (section[:, None] - 1 == jnp.arange(SECTIONS)[None, :]).astype(jnp.float32)
    modulation = jnp.dot(picker, table.astype(jnp.float32), precision=lax.Precision.HIGHEST)
    gain_one = modulation[:, None, 0:features]
    shift_one = modulation[:, None, features : 2 * features]
    gain_two = modulation[:, None, 2 * features : 3 * features]
    shift_two = modulation[:, None, 3 * features : 4 * features]
    inputs = tokens.astype(jnp.float32)
    normed_one, norm_one_back = jax.vjp(adanorm, inputs, gain_one, shift_one)
    low_one = normed_one.astype(jnp.bfloat16).reshape(row_count, features)
    qkv = jnp.dot(low_one, w_qkv, preferred_element_type=jnp.float32).astype(jnp.bfloat16)
    qkv = qkv.reshape(item_count, frames, 3, HEADS, head_size)
    queries = qkv[:, :, 0]
    keys_all = qkv[:, :, 1]
    values = qkv[:, :, 2]
    mixture, log_totals = lax.map(attend_forward, (queries, keys_all, values, key_len))
    mixture = mixture.reshape(row_count, features)
    attended = jnp.dot(mixture, w_out, preferred_element_type=jnp.float32)
    middle = inputs + attended.reshape(item_count, frames, features)
    normed_two, norm_two_back = jax.vjp(adanorm, middle, gain_two, shift_two)
    low_two = normed_two.astype(jnp.bfloat16).reshape(row_count, features)
    projected = jnp.dot(low_two, w_up, preferred_element_type=jnp.float32)
    activated, gelu_back = jax.vjp(jax.nn.gelu, projected)
    low_act = activated.astype(jnp.bfloat16)
    branch = jnp.dot(low_act, w_down, preferred_element_type=jnp.float32)
    block_out = (middle + branch.reshape(item_count, frames, features)).astype(jnp.bfloat16)
    regathered = lax.all_gather(low_params, ("dp", "fsdp"), axis=0, tiled=True)
    w_qkv, w_out, w_up, w_down, table = unpack(regathered)
    grad_y = cotangent.astype(jnp.float32)
    low_gy = cotangent.reshape(row_count, features)
    grad_down = dot_inner(low_act, low_gy)
    grad_act = dot_trans(low_gy, w_down)
    (grad_proj,) = gelu_back(grad_act)
    low_gp = grad_proj.astype(jnp.bfloat16)
    grad_up = dot_inner(low_two, low_gp)
    grad_norm_two = dot_trans(low_gp, w_up).reshape(item_count, frames, features)
    grad_mid_part, grad_gain_two, grad_shift_two = norm_two_back(grad_norm_two)
    grad_mid = grad_y + grad_mid_part
    low_gm = grad_mid.astype(jnp.bfloat16).reshape(row_count, features)
    grad_out_w = dot_inner(mixture, low_gm)
    grad_mix = (
        dot_trans(low_gm, w_out).astype(jnp.bfloat16).reshape(item_count, frames, HEADS, head_size)
    )
    grad_qkv = lax.map(attend_backward, (queries, keys_all, values, key_len, log_totals, grad_mix))
    grad_qkv = grad_qkv.reshape(row_count, 3 * features)
    grad_qkv_w = dot_inner(low_one, grad_qkv)
    grad_norm_one = dot_trans(grad_qkv, w_qkv).reshape(item_count, frames, features)
    grad_in_part, grad_gain_one, grad_shift_one = norm_one_back(grad_norm_one)
    input_grad = (grad_mid + grad_in_part).astype(jnp.bfloat16)
    per_item = jnp.concatenate(
        [grad_gain_one[:, 0], grad_shift_one[:, 0], grad_gain_two[:, 0], grad_shift_two[:, 0]], 1
    )
    grad_table = jnp.einsum("is,ic->sc", picker, per_item, precision=lax.Precision.HIGHEST)
    table_flat = grad_table.ravel()
    table_size = table_flat.shape[0]
    flat_grads = jnp.concatenate(
        [
            grad_qkv_w.ravel(),
            grad_out_w.ravel(),
            grad_up.ravel(),
            grad_down.ravel(),
            jnp.zeros((table_size,), jnp.float32),
        ]
    )
    table_start = flat_grads.shape[0] - table_size
    shard_size = params.shape[0]
    weight_part = lax.psum_scatter(
        lax.slice_in_dim(flat_grads, 0, lax.axis_size(("dp", "fsdp")) * shard_size, axis=0),
        ("dp", "fsdp"),
        scatter_dimension=0,
        tiled=True,
    )
    section_total = lax.psum(table_flat, ("dp", "fsdp"))
    padded = jnp.concatenate(
        [
            jnp.zeros((shard_size,), jnp.float32),
            section_total,
            jnp.zeros((shard_size,), jnp.float32),
        ]
    )
    slice_start = jnp.clip(
        lax.axis_index(("dp", "fsdp")) * shard_size - table_start + shard_size,
        0,
        table_size + shard_size,
    ).astype(jnp.int32)
    param_grad = weight_part + lax.dynamic_slice_in_dim(padded, slice_start, shard_size)
    section_grad = section_total.reshape(SECTIONS, 4 * features)
    new_first = beta_one * first_moment + (1.0 - beta_one) * param_grad
    new_second = beta_two * second_moment + (1.0 - beta_two) * param_grad * param_grad
    new_params = params - learn_rate * (new_first / bias_one) / (
        jnp.sqrt(new_second / bias_two) + adam_eps
    )
    return (block_out, input_grad, param_grad, new_params, new_first, new_second, section_grad)


LANES = 128
TILE = 16
EPS = 1e-05
VMEM_LIMIT = 62 * 1024 * 1024
GELU_C = 0.7978845608028654
GELU_A = 0.044715
BF = jnp.bfloat16
F32 = jnp.float32


def params_of(*semantics):
    return pltpu.CompilerParams(
        dimension_semantics=semantics or None, vmem_limit_bytes=VMEM_LIMIT
    )


def cost(flops, moved, transcendentals=0):
    return pl.CostEstimate(
        flops=int(flops), bytes_accessed=int(moved), transcendentals=int(transcendentals)
    )


ANYWHERE = pl.BlockSpec(memory_space=pl.ANY)


def without(kernel, first, count):
    def called(*refs):
        kernel(*refs[:first], *refs[first + count :])

    return called


def dot_nn(left, right):
    return lax.dot_general(left, right, (((1,), (0,)), ((), ())), preferred_element_type=F32)


def dot_nt(left, right):
    return lax.dot_general(left, right, (((1,), (1,)), ((), ())), preferred_element_type=F32)


def dot_tn(left, right):
    return lax.dot_general(left, right, (((0,), (0,)), ((), ())), preferred_element_type=F32)


def from_tiles(ref, first, count):
    rows = ref.shape[0] * TILE
    parts = [ref[:, first + c].reshape(rows, LANES) for c in range(count)]
    return parts[0] if count == 1 else jnp.concatenate(parts, 1)


def to_tiles(ref, first, value):
    rows, columns = value.shape
    for c in range(columns // LANES):
        part = value[:, c * LANES : (c + 1) * LANES].astype(BF)
        ref[:, first + c] = part.reshape(rows // TILE, TILE, LANES)


def row_chunks(kind):
    return {0: 3 * D // LANES, 1: D // LANES, 2: FF // LANES}[kind]


def each_tile(kinds, body):
    def span(kind, start, rows):
        step = row_chunks(kind)
        block = TILE * step

        def one(index, carry):
            base = start + index * block
            for c in range(step):
                body(base // TILE + c, base + c, step)
            return carry

        lax.fori_loop(0, rows // block, one, 0)

    @pl.when(kinds[0] == 0)
    def _():
        span(0, 0, 3072)

    def one_part(part, carry):
        for kind in (1, 2):

            @pl.when(kinds[part] == kind)
            def _():
                span(kind, part * 1024, 1024)

        return carry

    lax.fori_loop(0, 3, one_part, 0)


def pack_kernel(kinds, flat_ref, tiles_ref):
    def body(tile, row, step):
        tiles_ref[tile] = flat_ref[pl.ds(row, TILE, stride=step), :].astype(BF)

    each_tile(kinds, body)


def unpack_kernel(kinds, tiles_ref, flat_ref):
    def body(tile, row, step):
        flat_ref[pl.ds(row, TILE, stride=step), :] = tiles_ref[tile].astype(F32)

    each_tile(kinds, body)


def shard_kinds(index):
    start = index * 3072 + jnp.arange(3, dtype=jnp.int32) * 1024
    qkv_end = 3 * D * D // LANES
    out_end = qkv_end + D * D // LANES
    up_end = out_end + D * FF // LANES
    return jnp.where(
        start < qkv_end, 0, jnp.where((start < out_end) | (start >= up_end), 1, 2)
    ).astype(jnp.int32)


def pack_shard(kinds, flat):
    return pl.pallas_call(
        pack_kernel,
        out_shape=jax.ShapeDtypeStruct((192, TILE, LANES), BF),
        in_specs=[pl.BlockSpec(memory_space=pltpu.SMEM), pl.BlockSpec(memory_space=pltpu.VMEM)],
        out_specs=pl.BlockSpec(memory_space=pltpu.VMEM),
        compiler_params=params_of(),
        cost_estimate=cost(0, 3 << 20),
        name="pack_shard",
    )(kinds, flat)


def unpack_shard(kinds, tiles):
    return pl.pallas_call(
        unpack_kernel,
        out_shape=jax.ShapeDtypeStruct((3072, LANES), F32),
        in_specs=[pl.BlockSpec(memory_space=pltpu.SMEM), pl.BlockSpec(memory_space=pltpu.VMEM)],
        out_specs=pl.BlockSpec(memory_space=pltpu.VMEM),
        compiler_params=params_of(),
        cost_estimate=cost(0, 3 << 20),
        name="unpack_shard",
    )(kinds, tiles)


def centre(field):
    average = jnp.mean(field, -1, keepdims=True)
    centred = field - average
    spread = jnp.mean(centred * centred, -1, keepdims=True)
    inverse = lax.rsqrt(spread + EPS)
    return centred * inverse, inverse


def norm_back(zhat, inverse, grad, gain):
    scaled = grad * gain
    mean_one = jnp.mean(scaled, -1, keepdims=True)
    mean_two = jnp.mean(scaled * zhat, -1, keepdims=True)
    return inverse * (scaled - mean_one - zhat * mean_two)


def qkv_kernel(x_ref, mod_ref, w_ref, low_ref, qkv_ref):
    @pl.when(pl.program_id(0) == 0)
    def _():
        zhat, _ = centre(x_ref[...].astype(F32))
        low_ref[...] = (zhat * mod_ref[0:1, :] + mod_ref[1:2, :]).astype(BF)

    weights = from_tiles(w_ref, 0, w_ref.shape[1])
    qkv_ref[...] = dot_nn(low_ref[...], weights).astype(BF)


def project_qkv(x, mod, tiles):
    chunks = 4
    width = chunks * LANES
    return pl.pallas_call(
        qkv_kernel,
        grid=(3 * D // width,),
        out_shape=(
            jax.ShapeDtypeStruct((1024, D), BF),
            jax.ShapeDtypeStruct((1024, 3 * D), BF),
        ),
        in_specs=[
            pl.BlockSpec((1024, D), lambda j: (0, 0)),
            pl.BlockSpec((4, D), lambda j: (0, 0)),
            pl.BlockSpec((64, chunks, TILE, LANES), lambda j: (0, j, 0, 0)),
        ],
        out_specs=(
            pl.BlockSpec((1024, D), lambda j: (0, 0)),
            pl.BlockSpec((1024, width), lambda j: (0, j)),
        ),
        compiler_params=params_of("arbitrary"),
        cost_estimate=cost(6.4e9, 18e6),
        name="project_qkv",
    )(x, mod, tiles.reshape(-1, 24, TILE, LANES))


def head_lanes(head):
    lane = lax.broadcasted_iota(jnp.int32, (1, LANES), 1)
    return (lane >= 64) if head else (lane < 64)


def with_bias(keys, head, bias):
    lane = lax.broadcasted_iota(jnp.int32, (1, LANES), 1)
    rest = jnp.where(lane == 64 * (1 - head), bias, jnp.zeros((), BF))
    return jnp.where(head_lanes(head), keys, rest)


def with_one(queries, head):
    lane = lax.broadcasted_iota(jnp.int32, (1, LANES), 1)
    rest = jnp.where(lane == 64 * (1 - head), 1.0, 0.0).astype(BF)
    return jnp.where(head_lanes(head), queries * jnp.asarray(0.125, BF), rest)


def key_bias(len_ref, frames):
    row = lax.broadcasted_iota(jnp.int32, (frames, 1), 0)
    return jnp.where(row < len_ref[0], 0.0, -1e30).astype(BF)


def paired_blocks(body, frames, rows):
    def pair(index, carry):
        body(index * 2 * rows)
        body(index * 2 * rows + rows)
        return carry

    lax.fori_loop(0, frames // (2 * rows), pair, 0)


def attend_kernel(len_ref, q_ref, k_ref, v_ref, out_ref, total_ref):
    rows = 256
    frames = k_ref.shape[0]
    bias = key_bias(len_ref, frames)
    zero = jnp.zeros((), BF)
    keys = [with_bias(k_ref[...], h, bias) for h in range(2)]
    for offset in range(0, frames, rows):
        here = slice(offset, offset + rows)
        mixed = []
        for h in range(2):
            scores = dot_nt(with_one(q_ref[here, :], h), keys[h])
            largest = jnp.max(scores, -1, keepdims=True)
            weights = jnp.exp(scores - largest)
            total = jnp.sum(weights, -1, keepdims=True)
            mixed.append(dot_nn(weights.astype(BF), v_ref[...]) * (1.0 / total))
            wide = jnp.broadcast_to(largest + jnp.log(total), (rows, LANES))
            total_ref[0, h : h + 1, here] = wide.T[0:1, :]
        out_ref[here, :] = jnp.where(head_lanes(0), mixed[0], mixed[1]).astype(BF)


def attend(key_len, qkv):
    pairs = HEADS // 2
    return pl.pallas_call(
        attend_kernel,
        grid=(pairs,),
        out_shape=(
            jax.ShapeDtypeStruct((1024, D), BF),
            jax.ShapeDtypeStruct((pairs, 2, 1024), F32),
        ),
        in_specs=[
            pl.BlockSpec(memory_space=pltpu.SMEM),
            pl.BlockSpec((1024, LANES), lambda j: (0, j)),
            pl.BlockSpec((1024, LANES), lambda j: (0, pairs + j)),
            pl.BlockSpec((1024, LANES), lambda j: (0, 2 * pairs + j)),
        ],
        out_specs=(
            pl.BlockSpec((1024, LANES), lambda j: (0, j)),
            pl.BlockSpec((1, 2, 1024), lambda j: (j, 0, 0)),
        ),
        compiler_params=params_of("arbitrary"),
        cost_estimate=cost(17e9, 8e6, 16e6),
        name="attend",
    )(key_len, qkv, qkv, qkv)


def attend_back_kernel(
    len_ref, q_ref, k_ref, v_ref, do_ref, mix_ref, total_ref,
    dq_ref, dk_ref, dv_ref, dk_acc, dv_acc,
):
    rows = 256
    frames = k_ref.shape[0]
    bias = key_bias(len_ref, frames)
    values = v_ref[...]
    zero = jnp.zeros((), BF)
    keys = [with_bias(k_ref[...], h, bias) for h in range(2)]
    masked_keys = [jnp.where(head_lanes(h), k_ref[...], zero) for h in range(2)]
    dk_acc[...] = jnp.zeros_like(dk_acc)
    dv_acc[...] = jnp.zeros_like(dv_acc)

    def one_block(offset):
        here = pl.ds(pl.multiple_of(offset, rows), rows)
        queries = q_ref[here, :]
        grads = do_ref[here, :]
        products = (grads.astype(F32) * mix_ref[here, :].astype(F32)).T
        total = None
        for h in range(2):
            masked_q = jnp.where(head_lanes(h), queries * jnp.asarray(0.125, BF), zero)
            masked_g = jnp.where(head_lanes(h), grads, zero)
            inner = jnp.sum(products[64 * h : 64 * h + 64, :], 0, keepdims=True)
            scores = dot_nt(keys[h], with_one(queries, h))
            weights = jnp.exp(scores - total_ref[0, h : h + 1, here])
            grad_w = dot_nt(values, masked_g)
            back = (weights * (grad_w - inner)).astype(BF)
            dv_acc[...] += dot_nn(weights.astype(BF), masked_g)
            dk_acc[...] += dot_nn(back, masked_q)
            part_q = dot_tn(back, masked_keys[h])
            total = part_q if total is None else total + part_q
        dq_ref[here, :] = (total * 0.125).astype(BF)

    paired_blocks(one_block, frames, rows)
    dk_ref[...] = dk_acc[...].astype(BF)
    dv_ref[...] = dv_acc[...].astype(BF)


def attend_back(key_len, qkv, grad_mix, mixture, totals, first, count, earlier, waits=()):
    pairs = HEADS // 2
    block = lambda shift: pl.BlockSpec((1024, LANES), lambda j: (0, shift + first + j))
    kept = () if earlier is None else tuple(earlier)
    return pl.pallas_call(
        without(attend_back_kernel, 7, len(kept) + len(waits)),
        grid=(count,),
        out_shape=(jax.ShapeDtypeStruct((1024, D), BF),) * 3,
        in_specs=[
            pl.BlockSpec(memory_space=pltpu.SMEM),
            block(0),
            block(pairs),
            block(2 * pairs),
            block(0),
            block(0),
            pl.BlockSpec((1, 2, 1024), lambda j: (first + j, 0, 0)),
        ]
        + [ANYWHERE] * (len(kept) + len(waits)),
        out_specs=(block(0),) * 3,
        input_output_aliases={7 + i: i for i in range(len(kept))},
        scratch_shapes=[pltpu.VMEM((1024, LANES), F32)] * 2,
        compiler_params=params_of("arbitrary"),
        cost_estimate=cost(11e9 * count, 2e6 * count, 4e6 * count),
        name="attend_back",
    )(key_len, qkv, qkv, qkv, grad_mix, mixture, totals, *kept, *waits)


def middle_kernel(x_ref, mod_ref, mix_ref, w_ref, mid_ref, low_ref):
    weights = from_tiles(w_ref, 0, w_ref.shape[1])
    middle = x_ref[...].astype(F32) + dot_nn(mix_ref[...], weights)
    mid_ref[...] = middle
    zhat, _ = centre(middle)
    low_ref[...] = (zhat * mod_ref[2:3, :] + mod_ref[3:4, :]).astype(BF)


def middle_rows(x, mod, mixture, tiles):
    rows = 256
    return pl.pallas_call(
        middle_kernel,
        grid=(1024 // rows,),
        out_shape=(jax.ShapeDtypeStruct((1024, D), F32), jax.ShapeDtypeStruct((1024, D), BF)),
        in_specs=[
            pl.BlockSpec((rows, D), lambda i: (i, 0)),
            pl.BlockSpec((4, D), lambda i: (0, 0)),
            pl.BlockSpec((rows, D), lambda i: (i, 0)),
            pl.BlockSpec((64, 8, TILE, LANES), lambda i: (3, 0, 0, 0)),
        ],
        out_specs=(
            pl.BlockSpec((rows, D), lambda i: (i, 0)),
            pl.BlockSpec((rows, D), lambda i: (i, 0)),
        ),
        compiler_params=params_of("arbitrary"),
        cost_estimate=cost(2.2e9, 12e6),
        name="middle_rows",
    )(x, mod, mixture, tiles.reshape(-1, 8, TILE, LANES))


def ffn_kernel(
    mid_ref, mod_ref, low_ref, dy_ref, up_ref, down_ref,
    out_ref, dmid_ref, low_dmid_ref, dmod_ref, grads_ref,
    y_acc, dh_acc, low_t, act_s, du_s, dup_s, ddown_s, sems,
):
    step = pl.program_id(0)
    frames = mid_ref.shape[0]
    rows = 256

    @pl.when(step == 0)
    def _():
        y_acc[...] = jnp.zeros_like(y_acc)
        dh_acc[...] = jnp.zeros_like(dh_acc)
        low_t[...] = low_ref[...].T

    up = from_tiles(up_ref, 0, up_ref.shape[1])
    down = from_tiles(down_ref, 0, down_ref.shape[1])
    for offset in range(0, frames, rows):
        here = slice(offset, offset + rows)
        hidden = dot_nn(low_ref[here, :], up)
        grad_act = dot_nt(dy_ref[here, :], down)
        square = hidden * hidden
        inner = GELU_C * (hidden + GELU_A * (square * hidden))
        bend = jnp.tanh(inner)
        half = 0.5 * (1.0 + bend)
        act = (hidden * half).astype(BF)
        slope = half + 0.5 * hidden * (1.0 - bend * bend) * (
            GELU_C * (1.0 + 3.0 * GELU_A * square)
        )
        grad_hidden = (grad_act * slope).astype(BF)
        act_s[here, :] = act
        du_s[here, :] = grad_hidden
        y_acc[here, :] += dot_nn(act, down)
        dh_acc[here, :] += dot_nt(grad_hidden, up)
    slot = step % 2

    def copies(which, index):
        return (
            pltpu.make_async_copy(
                ddown_s.at[which], grads_ref.at[pl.ds(80 + index * 8, 8)], sems.at[which, 0]
            ),
            pltpu.make_async_copy(
                dup_s.at[which],
                grads_ref.at[pl.ds(16, 64), pl.ds(index * 4, 4)],
                sems.at[which, 1],
            ),
        )

    @pl.when(step >= 2)
    def _():
        for copy in copies(slot, step - 2):
            copy.wait()

    grad_down = dot_tn(act_s[...], dy_ref[...])
    for c in range(D // LANES):
        part = grad_down[:, c * LANES : (c + 1) * LANES].astype(BF).reshape(8, 4, TILE, LANES)
        for r in range(4):
            ddown_s[slot, :, r * 8 + c] = part[:, r]
    grad_up = dot_nn(low_t[...], du_s[...])
    for c in range(4):
        part = grad_up[:, c * LANES : (c + 1) * LANES].astype(BF)
        dup_s[slot, :, c] = part.reshape(64, TILE, LANES)
    for copy in copies(slot, step):
        copy.start()

    @pl.when(step == pl.num_programs(0) - 1)
    def _():
        for index in (step - 1, step):
            for copy in copies(index % 2, index):
                copy.wait()

    @pl.when(step == pl.num_programs(0) - 1)
    def _():
        dmod_ref[...] = jnp.zeros_like(dmod_ref)

        def finish(index, carry):
            here = pl.ds(pl.multiple_of(index * rows, rows), rows)
            middle = mid_ref[here, :]
            out_ref[here, :] = (middle + y_acc[here, :]).astype(BF)
            zhat, inverse = centre(middle)
            grad = dh_acc[here, :]
            dmod_ref[0:1, :] += jnp.sum(grad * zhat, 0, keepdims=True)
            dmod_ref[1:2, :] += jnp.sum(grad, 0, keepdims=True)
            grad_mid = dy_ref[here, :].astype(F32) + norm_back(zhat, inverse, grad, mod_ref[2:3, :])
            dmid_ref[here, :] = grad_mid
            low_dmid_ref[here, :] = grad_mid.astype(BF)
            return carry

        lax.fori_loop(0, frames // rows, finish, 0)


def ffn_both(middle, mod, low_two, dy, tiles):
    chunks = 4
    width = chunks * LANES
    steps = FF // width
    whole = lambda *shape: pl.BlockSpec(shape, lambda j: (0,) * len(shape))
    once = lambda *shape: pl.BlockSpec(
        shape, lambda j: (0,) * len(shape), pipeline_mode=pl.Buffered(1)
    )
    return pl.pallas_call(
        ffn_kernel,
        grid=(steps,),
        out_shape=(
            jax.ShapeDtypeStruct((1024, D), BF),
            jax.ShapeDtypeStruct((1024, D), F32),
            jax.ShapeDtypeStruct((1024, D), BF),
            jax.ShapeDtypeStruct((2, D), F32),
            jax.ShapeDtypeStruct((144, 32, TILE, LANES), BF),
        ),
        in_specs=[
            once(1024, D),
            whole(4, D),
            once(1024, D),
            once(1024, D),
            pl.BlockSpec((64, chunks, TILE, LANES), lambda j: (1, j, 0, 0)),
            pl.BlockSpec((width // TILE, 8, TILE, LANES), lambda j: (512 * TILE // width + j, 0, 0, 0)),
        ],
        out_specs=(
            once(1024, D),
            once(1024, D),
            once(1024, D),
            whole(2, D),
            pl.BlockSpec(memory_space=pl.ANY),
        ),
        scratch_shapes=[
            pltpu.VMEM((1024, D), F32),
            pltpu.VMEM((1024, D), F32),
            pltpu.VMEM((D, 1024), BF),
            pltpu.VMEM((1024, width), BF),
            pltpu.VMEM((1024, width), BF),
            pltpu.VMEM((2, 64, 4, TILE, LANES), BF),
            pltpu.VMEM((2, 8, 32, TILE, LANES), BF),
            pltpu.SemaphoreType.DMA((2, 2)),
        ],
        compiler_params=params_of("arbitrary"),
        cost_estimate=cost(52e9, 60e6, 4e6),
        name="ffn_both",
    )(
        middle, mod, low_two, dy,
        tiles.reshape(-1, 32, TILE, LANES), tiles.reshape(-1, 8, TILE, LANES),
    )


def out_back_kernel(mix_ref, dmid_ref, w_ref, grads_ref, dmix_ref, dw_ref):
    weights = from_tiles(w_ref, 0, w_ref.shape[1])
    dmix_ref[...] = dot_nt(dmid_ref[...], weights).astype(BF)
    to_tiles(dw_ref, 0, dot_tn(mix_ref[...], dmid_ref[...]))


def out_back(mixture, low_dmid, tiles, grads):
    width = 256
    return pl.pallas_call(
        out_back_kernel,
        grid=(D // width,),
        out_shape=(
            jax.ShapeDtypeStruct((1024, D), BF),
            jax.ShapeDtypeStruct((576, 8, TILE, LANES), BF),
        ),
        in_specs=[
            pl.BlockSpec((1024, width), lambda j: (0, j)),
            pl.BlockSpec((1024, D), lambda j: (0, 0)),
            pl.BlockSpec((width // TILE, 8, TILE, LANES), lambda j: (192 * TILE // width + j, 0, 0, 0)),
            pl.BlockSpec(memory_space=pl.ANY),
        ],
        input_output_aliases={3: 1},
        out_specs=(
            pl.BlockSpec((1024, width), lambda j: (0, j)),
            pl.BlockSpec((width // TILE, 8, TILE, LANES), lambda j: (j, 0, 0, 0)),
        ),
        compiler_params=params_of("arbitrary"),
        cost_estimate=cost(4.3e9, 10e6),
        name="out_back",
    )(mixture, low_dmid, tiles.reshape(-1, 8, TILE, LANES), grads.reshape(-1, 8, TILE, LANES))


def qkv_weight_kernel(low_ref, dq_ref, dk_ref, dv_ref, dw_ref):
    for third, grad_ref in enumerate((dq_ref, dk_ref, dv_ref)):
        to_tiles(dw_ref, third * 8, dot_tn(low_ref[...], grad_ref[...]))


def qkv_weight_grad(low_one, dq, dk, dv, waits=()):
    width = 256
    whole = pl.BlockSpec((1024, D), lambda j: (0, 0))
    return pl.pallas_call(
        without(qkv_weight_kernel, 4, len(waits)),
        grid=(D // width,),
        out_shape=jax.ShapeDtypeStruct((64, 24, TILE, LANES), BF),
        in_specs=[pl.BlockSpec((1024, width), lambda j: (0, j)), whole, whole, whole]
        + [ANYWHERE] * len(waits),
        out_specs=pl.BlockSpec((width // TILE, 24, TILE, LANES), lambda j: (j, 0, 0, 0)),
        compiler_params=params_of("arbitrary"),
        cost_estimate=cost(6.4e9, 15e6),
        name="qkv_weight_grad",
    )(low_one, dq, dk, dv, *waits)


def input_kernel(x_ref, mod_ref, dmid_ref, dq_ref, dk_ref, dv_ref, w_ref, grad_ref, dmod_ref):
    grad = None
    for third, part_ref in enumerate((dq_ref, dk_ref, dv_ref)):
        part = dot_nt(part_ref[...], from_tiles(w_ref, third * 8, 8))
        grad = part if grad is None else grad + part
    zhat, inverse = centre(x_ref[...].astype(F32))

    @pl.when(pl.program_id(0) == 0)
    def _():
        dmod_ref[...] = jnp.zeros_like(dmod_ref)

    dmod_ref[0:1, :] += jnp.sum(grad * zhat, 0, keepdims=True)
    dmod_ref[1:2, :] += jnp.sum(grad, 0, keepdims=True)
    grad_ref[...] = (dmid_ref[...] + norm_back(zhat, inverse, grad, mod_ref[0:1, :])).astype(BF)


def input_back(x, mod, dmid, dq, dk, dv, tiles, waits=()):
    rows = 256
    block = pl.BlockSpec((rows, D), lambda i: (i, 0))
    return pl.pallas_call(
        without(input_kernel, 7, len(waits)),
        grid=(1024 // rows,),
        out_shape=(jax.ShapeDtypeStruct((1024, D), BF), jax.ShapeDtypeStruct((2, D), F32)),
        in_specs=[
            block,
            pl.BlockSpec((4, D), lambda i: (0, 0)),
            block,
            block,
            block,
            block,
            pl.BlockSpec((64, 24, TILE, LANES), lambda i: (0, 0, 0, 0)),
        ]
        + [ANYWHERE] * len(waits),
        out_specs=(block, pl.BlockSpec((2, D), lambda i: (0, 0))),
        compiler_params=params_of("arbitrary"),
        cost_estimate=cost(6.4e9, 22e6),
        name="input_back",
    )(x, mod, dmid, dq, dk, dv, tiles.reshape(-1, 24, TILE, LANES), *waits)


def tile_spec(*lead, index):
    return pl.BlockSpec((*lead, TILE, LANES), lambda i, at: (*index(i, at), 0, 0))


def staged(kernel, name, outs, out_lead, ins, in_specs, sel, steps, moved, waits):
    spec = tile_spec(*out_lead, index=lambda i, at: (i,) + (0,) * (len(out_lead) - 1))
    shape = (steps,) + tuple(out_lead[1:]) + (TILE, LANES)
    return pl.pallas_call(
        without(kernel, 1 + len(ins), len(waits)),
        out_shape=(jax.ShapeDtypeStruct(shape, BF),) * outs,
        grid_spec=pltpu.PrefetchScalarGridSpec(
            num_scalar_prefetch=1,
            grid=(steps,),
            in_specs=in_specs + [ANYWHERE] * len(waits),
            out_specs=(spec,) * outs,
        ),
        compiler_params=params_of("arbitrary"),
        cost_estimate=cost(0, moved),
        name=name,
    )(sel, *ins, *waits)


def take_kernel(sel, value_ref, out_ref):
    out_ref[...] = value_ref[:, :, 0]


def take_other(sel, value, waits=()):
    layers = value.shape[0]
    value = value.reshape(2 * layers, 2, 2, 192, TILE, LANES)
    spec = tile_spec(1, 2, 1, 192, index=lambda i, at: (i, 0, 1 - at[2], 0))
    sent = staged(
        take_kernel, "take_other", 1, (1, 2, 192), [value], [spec], sel, 2 * layers, 6e6, waits
    )[0]
    return sent.reshape(layers, 2, 2, 192, TILE, LANES)


def both(left, right):
    return (left.astype(F32) + right.astype(F32)).astype(BF)


def core_kernel(sel, value_ref, moved_ref, one_send, one_keep, two_send, two_keep):
    y, x = sel[0], sel[1]
    one, two = slice(0, 96), slice(96, 192)
    for k in range(2):
        one_send[0, k] = both(value_ref[0, k, 1 - x, 0, one], moved_ref[0, k, 1 - x, one])
        one_keep[0, k] = both(value_ref[0, k, x, 0, one], moved_ref[0, k, x, one])
        two_send[0, k] = both(value_ref[0, 1 - y, k, 0, two], moved_ref[0, 1 - y, k, two])
        two_keep[0, k] = both(value_ref[0, y, k, 0, two], moved_ref[0, y, k, two])


def core_sum(sel, value, moved, waits=()):
    layers = value.shape[0]
    specs = [
        tile_spec(1, 2, 2, 1, 192, index=lambda i, at: (i, 0, 0, at[2], 0)),
        tile_spec(1, 2, 2, 192, index=lambda i, at: (i, 0, 0, 0)),
    ]
    return staged(
        core_kernel, "core_sum", 4, (1, 2, 96), [value, moved], specs, sel, layers, 9e6 * layers, waits
    )


def plane_kernel(sel, one_keep, one_moved, two_keep, two_moved, one_send, one_own, two_send, two_own):
    y, x = sel[0], sel[1]
    one_send[0] = both(one_keep[0, 1 - y], one_moved[0, 1 - y])
    one_own[0] = both(one_keep[0, y], one_moved[0, y])
    two_send[0] = both(two_keep[0, 1 - x], two_moved[0, 1 - x])
    two_own[0] = both(two_keep[0, x], two_moved[0, x])


def plane_sum(sel, *values, waits=()):
    layers = values[0].shape[0]
    spec = tile_spec(1, 2, 96, index=lambda i, at: (i, 0, 0))
    return staged(
        plane_kernel, "plane_sum", 4, (1, 96), values, [spec] * 4, sel, layers, 5e6 * layers, waits
    )


def line_kernel(sel, one_own, one_moved, two_own, two_moved, *outs):
    for layer, out_ref in enumerate(outs):

        @pl.when(pl.program_id(0) == layer)
        def _():
            out_ref[0:96] = both(one_own[0], one_moved[0])
            out_ref[96:192] = both(two_own[0], two_moved[0])


def line_sum(sel, *values, waits=()):
    layers = values[0].shape[0]
    spec = tile_spec(1, 96, index=lambda i, at: (i, 0))
    whole = tile_spec(192, index=lambda i, at: (0,))
    return pl.pallas_call(
        without(line_kernel, 1 + len(values), len(waits)),
        out_shape=(jax.ShapeDtypeStruct((192, TILE, LANES), BF),) * layers,
        grid_spec=pltpu.PrefetchScalarGridSpec(
            num_scalar_prefetch=1,
            grid=(layers,),
            in_specs=[spec] * 4 + [ANYWHERE] * len(waits),
            out_specs=(whole,) * layers,
        ),
        compiler_params=params_of("arbitrary"),
        cost_estimate=cost(0, 2.4e6 * layers),
        name="line_sum",
    )(sel, *values, *waits)


def flat_index():
    return lax.axis_index(("dp", "fsdp"))


def exchange(value, mask, count):
    return lax.ppermute(value, ("dp", "fsdp"), [(i, i ^ mask) for i in range(count)])


def sum_everywhere(value, count):
    mask = 1
    while mask < count:
        value = value + exchange(value, mask, count)
        mask *= 2
    return value


def fast_device(tokens, key_len, section, params, first_moment, second_moment, cotangent):
    count = lax.axis_size(("dp", "fsdp"))
    index = flat_index()
    shard = params.shape[0]
    table_size = SECTIONS * 4 * D
    aligned = (count * shard - table_size) // count
    slip = table_size // count
    kinds = shard_kinds(index)
    x = tokens[0]
    dy = cotangent[0]

    before = lax.ppermute(
        params[shard - table_size :], ("dp", "fsdp"), [(i, i + 1) for i in range(count - 1)]
    )
    own = lax.dynamic_slice(
        jnp.concatenate([before, params]), (table_size - index * slip,), (aligned,)
    )
    packed = pack_shard(kinds, own.reshape(aligned // LANES, LANES))
    sel = jnp.stack([index // 4 % 2, index // 2 % 2, index % 2]).astype(jnp.int32)

    last = index == count - 1
    table = jnp.where(last, params[shard - table_size :], 0.0).astype(BF)
    table = sum_everywhere(table.reshape(SECTIONS, 4 * D), count)
    tiles = lax.all_gather(packed, ("dp", "fsdp"), axis=0, tiled=True)
    picker = (section[0] - 1 == jnp.arange(SECTIONS)).astype(F32)[:, None]
    mod = jnp.sum(picker * table.astype(F32), 0).reshape(4, D)

    low_one, qkv = project_qkv(x, mod, tiles)
    mixture, totals = attend(key_len, qkv)
    middle, low_two = middle_rows(x, mod, mixture, tiles)
    block_out, dmid, low_dmid, dmod_two, grads = ffn_both(middle, mod, low_two, dy, tiles)
    grad_mix, grads = out_back(mixture, low_dmid, tiles, grads)

    grads = grads.reshape(3, 2, 2, 2, 192, TILE, LANES)
    sent = take_other(sel, grads)
    moved = exchange(sent, 1, count)
    back = attend_back(key_len, qkv, grad_mix, mixture, totals, 0, 2, None, (sent,))
    one_send, one_keep, two_send, two_keep = core_sum(sel, grads, moved, back[:1])
    one_moved, two_moved = exchange(one_send, 2, count), exchange(two_send, 4, count)
    dq, dk, dv = attend_back(key_len, qkv, grad_mix, mixture, totals, 2, 6, back, (one_send,))
    grad_qkv = qkv_weight_grad(low_one, dq, dk, dv)
    grad_qkv = grad_qkv.reshape(1, 2, 2, 2, 192, TILE, LANES)
    one_send, one_keep, two_send, two_keep = plane_sum(
        sel, one_keep, one_moved, two_keep, two_moved, waits=(grad_qkv,)
    )
    one_moved, two_moved = exchange(one_send, 4, count), exchange(two_send, 2, count)
    held = (one_keep, one_moved, two_keep, two_moved)
    sent = take_other(sel, grad_qkv, (one_send,))
    moved = exchange(sent, 1, count)
    one_send, one_keep, two_send, two_keep = core_sum(sel, grad_qkv, moved)
    one_moved, two_moved = exchange(one_send, 2, count), exchange(two_send, 4, count)
    input_grad, dmod_one = input_back(x, mod, dmid, dq, dk, dv, tiles, (one_send,))
    rest = line_sum(sel, *held, waits=(input_grad,))
    one_send, one_keep, two_send, two_keep = plane_sum(
        sel, one_keep, one_moved, two_keep, two_moved, waits=(rest[0],)
    )
    one_moved, two_moved = exchange(one_send, 4, count), exchange(two_send, 2, count)
    first = line_sum(sel, one_keep, one_moved, two_keep, two_moved)

    per_item = jnp.concatenate([dmod_one, dmod_two], 0).reshape(1, 4 * D)
    section_grad = sum_everywhere(picker * per_item, count)

    reduced = jnp.where(
        index // 8 == 0, reduce_first(first[0], count), reduce_rest(rest, index, count)
    ).reshape(192, TILE, LANES)
    summed = unpack_shard(kinds, reduced).reshape(aligned)
    following = lax.ppermute(
        summed[:table_size], ("dp", "fsdp"), [(i, i - 1) for i in range(1, count)]
    )
    following = jnp.where(last, section_grad.reshape(table_size), following)
    param_grad = lax.dynamic_slice(jnp.concatenate([summed, following]), (index * slip,), (shard,))
    new_first = beta_one * first_moment + (1.0 - beta_one) * param_grad
    new_second = beta_two * second_moment + (1.0 - beta_two) * param_grad * param_grad
    new_params = params - learn_rate * (new_first / bias_one) / (
        jnp.sqrt(new_second / bias_two) + adam_eps
    )
    return (
        block_out[None],
        input_grad[None],
        param_grad,
        new_params,
        new_first,
        new_second,
        section_grad,
    )


def add_low(*terms):
    return add_wide(*terms).astype(BF)


def add_wide(*terms):
    total = terms[0].astype(F32)
    for term in terms[1:]:
        total = total + term.astype(F32)
    return total


def layer_move(value, moves):
    pairs = [(8 * a + i, 8 * b + i) for a, b in moves for i in range(8)]
    return lax.ppermute(value, ("dp", "fsdp"), pairs)


def pick(value, index, axis):
    return lax.dynamic_index_in_dim(value, index, axis, keepdims=False)


def reduce_first(value, count):
    value = add_low(value, layer_move(value, [(3, 2), (1, 0)]))
    return add_wide(value, layer_move(value, [(2, 0)]))


def reduce_rest(value, index, count):
    layer = index // 8
    choose = lambda at: jnp.where(at <= 0, value[0], jnp.where(at == 1, value[1], value[2]))
    up = layer_move(value[2], [(0, 1)])
    down = layer_move(value[0], [(3, 2)])
    up = layer_move(add_low(choose(1 + layer), up), [(0, 1), (1, 2)])
    down = layer_move(add_low(choose(layer - 2), down), [(3, 2), (2, 1)])
    up = layer_move(add_low(choose(layer), up), [(0, 1), (1, 2), (2, 3)])
    return add_wide(choose(layer - 1), up, down)


def solution(mesh):
    in_specs = (
        P(("dp", "fsdp"), None, None),
        P(("dp", "fsdp")),
        P(("dp", "fsdp")),
        P(("dp", "fsdp")),
        P(("dp", "fsdp")),
        P(("dp", "fsdp")),
        P(("dp", "fsdp"), None, None),
    )
    out_specs = (
        P(("dp", "fsdp"), None, None),
        P(("dp", "fsdp"), None, None),
        P(("dp", "fsdp")),
        P(("dp", "fsdp")),
        P(("dp", "fsdp")),
        P(("dp", "fsdp")),
        P(),
    )
    fast = dict(mesh.shape) == {"dp": 8, "fsdp": 4}
    return jax.shard_map(
        fast_device if fast else per_device, mesh=mesh, in_specs=in_specs, out_specs=out_specs, check_vma=False
    )
```
